128 devices in a mesh: ctx: 32 (over z, x, core), head: 4 (over y).
Axes of the slice: x: 4, y: 4, z: 4, core: 2. Of those that a mesh axis runs over, the one named last changes fastest.
Arguments:
- inputs: bfloat16 [4096, 2048], P('ctx'), may hold values from -6 to 6
- grad_out: bfloat16 [4096, 2048], P('ctx'), may hold values from -6 to 6
- w_query: bfloat16 [2048, 4096], P(None, 'head'), may hold values from -0.125 to 0.125
- w_key: bfloat16 [2048, 4096], P(None, 'head'), may hold values from -0.125 to 0.125
- w_value: bfloat16 [2048, 4096], P(None, 'head'), may hold values from -0.125 to 0.125
- w_beta: bfloat16 [2048, 32], P(None, 'head'), may hold values from -0.125 to 0.125
- w_out: bfloat16 [4096, 2048], P('head'), may hold values from -0.09375 to 0.09375
- log_decay: float32 [4096, 32], P('ctx', 'head'), may hold values from -0.69 to 0
- lengths: int32 [16], replicated, may hold values from 1 to 1024, 4096 in all
Outputs:
- grad_x: bfloat16 [4096, 2048], P('ctx', 'head')
- grad_log_decay: float32 [4096, 32], P('ctx', 'head')
The draws below stay inside these ranges and needn't reach their ends.
Inputs may be any that keep to these rules, and one draw needn't show every extreme that they name: The lengths sum to 4096, and the longest document has exactly 1024 tokens.
All inputs are finite; a program needn't handle non-finite values.
Results may differ from the reference program's by a relative error of at most 0.005.
Values sent between devices are 32-bit elements; how exact they have to be, the bound alone decides.
No kernel may reach another device: no remote copies, remote signals or barrier semaphores. Data moves between devices by JAX's collectives and lax.ppermute only.
A program may use at most 192 MiB of HBM per device.

```python
import math
from functools import partial
import jax
import jax.numpy as jnp
import numpy as np
from jax import lax

D = 2048
HEAD_COUNT = 32
DK = 128
DV = 128
STRETCH = 64
NDOC = 16
TOK_DEV = 128
TOKEN_COUNT = 4096


def draw_log_decay(key, part):
    key_rows = jax.random.split(key, 7)
    slow_share = 0.5
    slow = jax.random.uniform(key_rows[0], (HEAD_COUNT,)) < slow_share
    slow_rate = 2.0 / TOKEN_COUNT * jnp.exp(jax.random.uniform(key_rows[1], (HEAD_COUNT,), minval=-0.7, maxval=0.0))
    fast_rate = jnp.exp(jax.random.uniform(key_rows[2], (HEAD_COUNT,), minval=math.log(1.0 / 50.0), maxval=math.log(1.0 / 30.0)))
    decay_speed = jnp.where(slow, slow_rate, fast_rate)
    block_multiplier = jnp.exp(jax.random.uniform(key_rows[3], (TOKEN_COUNT // TOK_DEV, HEAD_COUNT), minval=math.log(0.5), maxval=math.log(2.0)))
    block_multiplier = jnp.repeat(block_multiplier, TOK_DEV, axis=0)
    coarse_estimate = jax.random.uniform(key_rows[4], (TOKEN_COUNT, HEAD_COUNT), minval=0.5, maxval=2.0)
    segment_span_local = jax.random.uniform(key_rows[5], (TOKEN_COUNT, HEAD_COUNT)) < 4.0 / TOKEN_COUNT
    segment_span = -jax.random.uniform(key_rows[6], (TOKEN_COUNT, HEAD_COUNT), minval=0.22, maxval=0.69)
    return jnp.where(segment_span_local, segment_span, -decay_speed[None, :] * block_multiplier * coarse_estimate).astype(jnp.float32)


def level_of(stream_key, shape, cuts, least, largest):
    loudness = 1.0
    for axis_at, blocks in cuts:
        heights = jax.random.uniform(jax.random.fold_in(jax.random.fold_in(stream_key, 6), axis_at), (blocks,), jnp.float32, least / len(cuts), largest / len(cuts))
        loudness = loudness * jnp.repeat(jnp.exp(heights), shape[axis_at] // blocks).reshape((-1,) + (1,) * (len(shape) - 1 - axis_at))
    return loudness


def profile(number_of, total, bound, slope):
    loads = [(1 << 20) // math.isqrt(grade ** slope) + 1 for grade in range(2, number_of + 1)]
    spare, holding = total - bound - (number_of - 1), [1] * (number_of - 1)
    while spare > 0:
        movable = [i for i in range(number_of - 1) if holding[i] < bound]
        pool, remaining = sum([loads[i] for i in movable]), spare
        for i in movable:
            addition = min(bound - holding[i], max(1, remaining * loads[i] // pool), spare)
            holding[i] = holding[i] + addition
            spare = spare - addition
    return np.array([bound] + holding)


def ragged(stream_key, number_of, total, limit, lean):
    if number_of == 2:
        one = jax.random.randint(stream_key, (), max(1, total - limit), min(limit, total - 1) + 1)
        return jnp.stack([one, total - one])
    sizes = jnp.asarray(profile(number_of, total, limit, lean), jnp.int32)
    twos = (number_of - 1) // 2
    giver, receiver = sizes[1:1 + 2 * twos:2], sizes[2:2 + 2 * twos:2]
    room = jnp.minimum(giver - 1, limit - receiver)
    moved = jax.random.randint(jax.random.fold_in(stream_key, 1), (twos,), 0, 1 << 20) % (room + 1)
    sizes = sizes.at[1:1 + 2 * twos:2].set(giver - moved).at[2:2 + 2 * twos:2].set(receiver + moved)
    return sizes[jax.random.permutation(jax.random.fold_in(stream_key, 2), number_of)]


def centred(stream_key, extent, deviation, bound, cuts=(), kind=jnp.bfloat16):
    values = deviation * jax.random.normal(stream_key, extent, jnp.float32)
    if cuts:
        values = values * level_of(stream_key, extent, cuts, -0.22, 0.18)
    return jnp.clip(values, -bound, bound).astype(kind)


def setup_inputs(seed: int = 0) -> dict:
    streams_of = jax.random.split(jax.random.key(seed), 10)
    return {
        "inputs": centred(streams_of[0], (TOKEN_COUNT, D), 1.0, 6.0, ((0, 32),)),
        "grad_out": centred(streams_of[1], (TOKEN_COUNT, D), 1.0, 6.0, ((0, 32),)),
        "w_query": centred(streams_of[2], (D, HEAD_COUNT * DK), D ** -0.5, 0.125, ((1, 4),)),
        "w_key": centred(streams_of[3], (D, HEAD_COUNT * DK), D ** -0.5, 0.125, ((1, 4),)),
        "w_value": centred(streams_of[4], (D, HEAD_COUNT * DV), D ** -0.5, 0.125, ((1, 4),)),
        "w_beta": centred(streams_of[5], (D, HEAD_COUNT), D ** -0.5, 0.125, ((1, 4),)),
        "w_out": centred(streams_of[6], (HEAD_COUNT * DV, D), (HEAD_COUNT * DV) ** -0.5, 0.09375, ((0, 4),)),
        "log_decay": draw_log_decay(jax.random.fold_in(streams_of[9], 71), 0),
        "lengths": ragged(streams_of[8], NDOC, TOKEN_COUNT, TOKEN_COUNT // 4, 2).astype(jnp.int32),
    }


def normalize(raw, width):
    rows = raw.shape[0]
    shaped = raw.reshape(rows, -1, width)
    return shaped * lax.rsqrt(lax.optimization_barrier(jnp.sum(shaped * shaped, axis=-1, keepdims=True)) + 1e-06)

def stretch_step(state, pieces):
    query, key_rows, values, beta, decay, flags = pieces
    highest = lax.Precision.HIGHEST
    count = jnp.cumsum(flags)
    same = count[:, None] == count[None, :]
    length = flags.shape[0]
    index = jnp.arange(length)
    lower = index[:, None] >= index[None, :]
    strict = index[:, None] > index[None, :]
    running = jnp.cumsum(decay, axis=1)
    spread = running[:, :, None] - running[:, None, :]
    keep = jnp.logical_and(same, lower)[None]
    weight = jnp.where(keep, jnp.exp(jnp.where(keep, spread, 0.0)), 0.0)
    carried = jnp.exp(running) * (count == 0).astype(running.dtype)[None, :]
    key_key = jnp.einsum('htk,hsk->hts', key_rows, key_rows, precision=highest)
    query_key = jnp.einsum('htk,hsk->hts', query, key_rows, precision=highest)
    mixing = jnp.where(strict[None], weight, 0.0) * key_key * beta[:, :, None]
    identity = jnp.eye(length, dtype=mixing.dtype)
    known = jnp.einsum('htk,hvk->htv', key_rows, state, precision=highest)
    right = beta[:, :, None] * (values - carried[:, :, None] * known)
    fresh = jax.vmap(partial(jax.scipy.linalg.solve_triangular, lower=True, unit_diagonal=True))(identity[None] + mixing, right)
    seen = jnp.einsum('htk,hvk->htv', query, state, precision=highest)
    output = carried[:, :, None] * seen + jnp.einsum('hts,hsv->htv', weight * query_key, fresh, precision=highest)
    closing = weight[:, -1, :]
    state = carried[:, -1][:, None, None] * state + jnp.einsum('hs,hsv,hsk->hvk', closing, fresh, key_rows, precision=highest)
    return (state, output)

def layer_core(raw_q, raw_k, raw_v, logits, decay, flags, state):
    heads = logits.shape[1]
    width = state.shape[2]
    vwidth = state.shape[1]
    rows = raw_q.shape[0]
    blocks = rows // STRETCH
    query = normalize(raw_q, width) * width ** (-0.5)
    key_rows = normalize(raw_k, width)
    values = raw_v.reshape(rows, heads, vwidth)
    beta = jax.nn.sigmoid(logits)

    def split(array):
        array = array.reshape((blocks, STRETCH) + array.shape[1:])
        return jnp.moveaxis(array, 1, 2)
    pieces = (split(query), split(key_rows), split(values), split(beta), split(decay), flags.reshape(blocks, STRETCH))
    state, output = lax.scan(stretch_step, state, pieces)
    output = jnp.moveaxis(output, 1, 2).reshape(rows, heads * vwidth)
    return (output, state)

def project_back(grad, weight):
    return lax.dot_general(grad.astype(jnp.bfloat16).astype(jnp.float32), weight.astype(jnp.float32), (((1,), (1,)), ((), ())), preferred_element_type=jnp.float32)

def reference(inputs, grad_out, w_query, w_key, w_value, w_beta, w_out, log_decay, lengths):
    raw_q = jnp.dot(inputs.astype(jnp.float32), w_query.astype(jnp.float32), preferred_element_type=jnp.float32)
    raw_k = jnp.dot(inputs.astype(jnp.float32), w_key.astype(jnp.float32), preferred_element_type=jnp.float32)
    raw_v = jnp.dot(inputs.astype(jnp.float32), w_value.astype(jnp.float32), preferred_element_type=jnp.float32)
    logits = jnp.dot(inputs.astype(jnp.float32), w_beta.astype(jnp.float32), preferred_element_type=jnp.float32)
    finish = jnp.cumsum(lengths)
    begins = finish - lengths
    places = jnp.arange(TOKEN_COUNT, dtype=jnp.int32)
    flags = lax.optimization_barrier(jnp.sum((places[:, None] == begins[None, :]).astype(jnp.int32), axis=1))
    grad_heads = lax.dot_general(grad_out.astype(jnp.float32), w_out.astype(jnp.float32), (((1,), (1,)), ((), ())), preferred_element_type=jnp.float32)
    initial = jnp.zeros((HEAD_COUNT, DV, DK), jnp.float32)

    def forward(part_q, part_k, part_v, part_b, part_d):
        return layer_core(part_q, part_k, part_v, part_b, part_d, flags, initial)[0]
    _, pullback = jax.vjp(forward, raw_q, raw_k, raw_v, logits, log_decay)
    grad_q, grad_k, grad_v, grad_b, grad_d = pullback(grad_heads)
    total = project_back(grad_q, w_query) + project_back(grad_k, w_key)
    total = total + project_back(grad_v, w_value) + project_back(grad_b, w_beta)
    return (total.astype(jnp.bfloat16), grad_d)
```

```python
import jax
import jax.numpy as jnp
from jax import lax
from jax.experimental import pallas as pl
from jax.experimental.pallas import tpu as pltpu
from jax.sharding import PartitionSpec as P

F32 = jnp.float32
BF16 = jnp.bfloat16
W = 128
GROUP = 4
ROW = 8
NN = (((1,), (0,)), ((), ()))
NT = (((1,), (1,)), ((), ()))
TN = (((0,), (0,)), ((), ()))


def dot(a, b, dims=NN):
    return lax.dot_general(a, b, dims, preferred_element_type=F32)


def exact(a, b, dims=NN):
    return lax.dot_general(a, b, dims, precision=lax.Precision.HIGHEST, preferred_element_type=F32)


def halves(a):
    high = a.astype(BF16)
    return high, (a - high.astype(F32)).astype(BF16)


def mm3(a, b, dims=NN):
    ah, al = halves(a)
    bh, bl = halves(b)
    return dot(ah, bh, dims) + (dot(ah, bl, dims) + dot(al, bh, dims))


def iotas(shape):
    return lax.broadcasted_iota(jnp.int32, shape, 0), lax.broadcasted_iota(jnp.int32, shape, 1)


def column(array, index):
    lanes = lax.broadcasted_iota(jnp.int32, array.shape, 1)
    return jnp.sum(jnp.where(lanes == index, array, 0.0), axis=1, keepdims=True)


def inverse_all(mixes):
    ti, si = iotas((W, W))
    eye = jnp.where(ti == si, 1.0, 0.0)
    below = jnp.logical_and((ti >> 1) == (si >> 1), ti > si)
    done = [eye - jnp.where(below, a, 0.0) for a in mixes]
    for shift in range(1, 7):
        below = jnp.logical_and((ti >> (shift + 1)) == (si >> (shift + 1)), (ti >> shift) > (si >> shift))
        parts = [jnp.where(below, a, 0.0) for a in mixes]
        inner = [mm3(p, d) for p, d in zip(parts, done)]
        done = [d - mm3(d, i) for d, i in zip(done, inner)]
    return done


def first_kernel(
    len_ref, base_ref, x_ref, go_ref, wq_ref, wk_ref, wv_ref, wb_ref, wo_ref, dec_ref,
    send_ref, k_ref, q_ref, v_ref, do_ref, p_ref, l_ref, wkk_ref, w_ref, uv_ref, kw_ref, col_ref,
):
    step = pl.program_id(0)
    base = base_ref[0]
    ti, si = iotas((W, W))
    begin = jnp.int32(0)
    seg_t = jnp.zeros((W, W), jnp.int32)
    seg_s = jnp.zeros((W, W), jnp.int32)
    seg_in = jnp.int32(0)
    for j in range(len_ref.shape[0]):
        seg_t = seg_t + (ti + base >= begin).astype(jnp.int32)
        seg_s = seg_s + (si + base >= begin).astype(jnp.int32)
        seg_in = seg_in + (base - 1 >= begin).astype(jnp.int32)
        begin = begin + len_ref[j]
    keep = jnp.logical_and(seg_t == seg_s, ti >= si)
    strict = ti > si
    first = (seg_t == seg_in)[:, :1]
    x = x_ref[...]
    raw_q = dot(x, wq_ref[...])
    raw_k = dot(x, wk_ref[...])
    raw_v = dot(x, wv_ref[...])
    grad_o = dot(go_ref[...], wo_ref[...], NT)
    beta_all = 1.0 / (1.0 + jnp.exp(-dot(x, wb_ref[...])))
    tril = jnp.where(ti >= si, 1.0, 0.0)
    run_all = exact(tril, dec_ref[...])
    heads = range(GROUP)
    cut = lambda a, i: a[:, i * W:(i + 1) * W]
    ks, qs, betas, carries, weights, wkks, mixes, pmats = [], [], [], [], [], [], [], []
    for i in heads:
        head = step * GROUP + i
        rk = cut(raw_k, i)
        rq = cut(raw_q, i)
        inv_k = lax.rsqrt(jnp.sum(rk * rk, axis=1, keepdims=True) + 1e-06)
        inv_q = lax.rsqrt(jnp.sum(rq * rq, axis=1, keepdims=True) + 1e-06)
        k = rk * inv_k
        q = rq * inv_q * (W ** -0.5)
        beta = column(beta_all, head)
        run = column(run_all, head)
        run_b = jnp.broadcast_to(run, (W, W))
        spread = run_b - run_b.T
        weight = jnp.where(keep, jnp.exp(jnp.where(keep, spread, 0.0)), 0.0)
        carried = jnp.where(first, jnp.exp(run), 0.0)
        both = mm3(jnp.concatenate([k, q], axis=0), k, NT)
        wkk = jnp.where(strict, weight, 0.0) * both[:W]
        pmat = weight * both[W:]
        ks.append(k)
        qs.append(q)
        betas.append(beta)
        carries.append(carried)
        weights.append(weight)
        wkks.append(wkk)
        mixes.append(wkk * beta)
        pmats.append(pmat)
        lanes = si
        closing = jnp.sum(jnp.where(ti == si, jnp.broadcast_to(weight[W - 1:W, :], (W, W)), 0.0), axis=1, keepdims=True)
        col = jnp.where(lanes == 0, beta, jnp.where(lanes == 1, carried, jnp.where(lanes == 2, closing, jnp.where(lanes == 3, inv_k, inv_q))))
        col_ref[i] = col
        k_ref[i] = k
        q_ref[i] = q
        v_ref[i] = cut(raw_v, i)
        do_ref[i] = cut(grad_o, i)
        p_ref[i] = pmat
        wkk_ref[i] = wkk
        w_ref[i] = weight
    solved = inverse_all(mixes)
    for i in heads:
        k, q, beta, carried = ks[i], qs[i], betas[i], carries[i]
        l_ref[i] = solved[i]
        right = jnp.concatenate([beta * cut(raw_v, i), (beta * carried) * k], axis=1)
        both = mm3(solved[i], right)
        uv = both[:, :W]
        kw = both[:, W:]
        uv_ref[i] = uv
        kw_ref[i] = kw
        eff = carried * q - mm3(pmats[i], kw)
        closing = col_ref[i][:, 2:3]
        ends = mm3(jnp.concatenate([kw, uv], axis=1), closing * k, TN)
        last = carried[W - 1:W, :]
        send_ref[i, 0] = jnp.where(ti == si, last, 0.0) - ends[:W]
        send_ref[i, 1] = ends[W:]
        send_ref[i, 2] = mm3(cut(grad_o, i), eff, TN)


def row_kernel(r_ref, out_ref):
    state = r_ref[0, 1]
    grad = r_ref[ROW - 1, 2]
    for j in range(1, ROW):
        state = mm3(state, r_ref[j, 0]) + r_ref[j, 1]
        b = ROW - 1 - j
        grad = mm3(grad, r_ref[b, 0], NT) + r_ref[b, 2]
    out_ref[0] = state
    out_ref[1] = grad


def spread_kernel(r_ref, s_ref, g_ref, out_ref):
    state = s_ref[...]
    grad = g_ref[...]
    out_ref[0, 0] = state
    out_ref[ROW - 1, 1] = grad
    for j in range(1, ROW):
        state = mm3(state, r_ref[j - 1, 0]) + r_ref[j - 1, 1]
        out_ref[j, 0] = state
        b = ROW - j
        grad = mm3(grad, r_ref[b, 0], NT) + r_ref[b, 2]
        out_ref[b - 1, 1] = grad


def second_kernel(
    back_ref, k_ref, q_ref, v_ref, do_ref, p_ref, l_ref, wkk_ref, w_ref, uv_ref, kw_ref, col_ref,
    wq_ref, wk_ref, wv_ref, wb_ref, total_ref, gd_ref, cterm_ref, fterm_ref, eterm_ref, db_ref,
):
    step = pl.program_id(0)
    ti, si = iotas((W, W))
    strict = ti > si
    upper = jnp.where(si >= ti, 1.0, 0.0)
    t8, h8 = iotas((W, ROW))

    @pl.when(step == 0)
    def _():
        cterm_ref[...] = jnp.zeros((W, ROW), F32)
        fterm_ref[...] = jnp.zeros((W, ROW), F32)
        eterm_ref[...] = jnp.zeros((W, ROW), F32)
        db_ref[...] = jnp.zeros((W, ROW), F32)

    cterm, fterm, eterm, dball = cterm_ref[...], fterm_ref[...], eterm_ref[...], db_ref[...]
    gqs, gks, gvs = [], [], []
    for i in range(GROUP):
        head = step * GROUP + i
        s0, g1 = back_ref[i, 0], back_ref[i, 1]
        k, q, v, do = k_ref[i], q_ref[i], v_ref[i], do_ref[i]
        pmat, wkk, weight = p_ref[i], wkk_ref[i], w_ref[i]
        col = col_ref[i]
        beta, carried, closing, inv_k, inv_q = (col[:, j:j + 1] for j in range(5))
        u = uv_ref[i] - mm3(kw_ref[i], s0, NT)
        du = mm3(pmat, do, TN) + mm3(closing * k, g1, NT)
        dr = mm3(l_ref[i], du, TN)
        dpa = mm3(jnp.concatenate([do, dr], axis=0), u, NT)
        dp = dpa[:W]
        da = -dpa[W:]
        ds = mm3(jnp.concatenate([carried * do, dr], axis=0), s0)
        dq_state = ds[:W]
        dr_s = carried * ds[W:]
        ug = closing * mm3(u, g1)
        dqk = weight * dp
        dkk = jnp.where(strict, weight, 0.0) * da * beta
        front = mm3(jnp.concatenate([dqk, dkk], axis=0), k)
        dq = front[:W] + dq_state
        dk = front[W:] + mm3(jnp.concatenate([dkk, dqk], axis=0), jnp.concatenate([k, q], axis=0), TN)
        dk = dk - beta * dr_s + ug
        known = jnp.sum(dr_s * k, axis=1, keepdims=True)
        dbeta = jnp.sum(dr * v, axis=1, keepdims=True) - known + jnp.sum(da * wkk, axis=1, keepdims=True)
        dlogit = dbeta * beta * (1.0 - beta)
        pairs = dp * pmat + da * wkk * beta
        ph, plow = halves(pairs)
        ub = upper.astype(BF16)
        across = dot(ub, ph) + dot(ub, plow)
        evec = jnp.sum(jnp.where(strict, across, 0.0), axis=1, keepdims=True)
        fvec = jnp.sum(ug * k, axis=1, keepdims=True)
        cvec = jnp.sum(dq_state * q, axis=1, keepdims=True) - beta * known
        ends = carried[W - 1:W, :] * jnp.sum(jnp.sum(g1 * s0, axis=1, keepdims=True), axis=0, keepdims=True)
        cvec = cvec + jnp.where(t8[:, :1] == W - 1, ends, 0.0)
        here = h8 == head
        cterm = jnp.where(here, cvec, cterm)
        fterm = jnp.where(here, fvec, fterm)
        eterm = jnp.where(here, evec, eterm)
        dball = jnp.where(here, dlogit, dball)
        gk = inv_k * (dk - k * jnp.sum(k * dk, axis=1, keepdims=True))
        gq = (inv_q * (W ** -0.5)) * (dq - (q * float(W)) * jnp.sum(q * dq, axis=1, keepdims=True))
        gqs.append(gq.astype(BF16))
        gks.append(gk.astype(BF16))
        gvs.append((beta * dr).astype(BF16))
    cterm_ref[...], fterm_ref[...], eterm_ref[...], db_ref[...] = cterm, fterm, eterm, dball
    part = dot(jnp.concatenate(gqs, axis=1), wq_ref[...], NT)
    part = part + dot(jnp.concatenate(gks, axis=1), wk_ref[...], NT)
    part = part + dot(jnp.concatenate(gvs, axis=1), wv_ref[...], NT)

    @pl.when(step == 0)
    def _():
        total_ref[...] = part

    @pl.when(step > 0)
    def _():
        total_ref[...] += part

    @pl.when(step == pl.num_programs(0) - 1)
    def _():
        total_ref[...] += dot(dball.astype(BF16), wb_ref[...], NT)
        lower = jnp.where(strict, 1.0, 0.0)
        gd_ref[...] = exact(upper, cterm) + exact(lower, fterm) + eterm


def per_device(inputs, grad_out, w_query, w_key, w_value, w_beta, w_out, log_decay, lengths):
    rows, width = inputs.shape
    heads = w_beta.shape[1]
    steps = heads // GROUP
    span = GROUP * W
    base = (lax.axis_index("ctx") * rows).astype(jnp.int32).reshape(1)
    smem = pl.BlockSpec(memory_space=pltpu.SMEM)
    whole = lambda *shape: pl.BlockSpec(shape, lambda g: (0,) * len(shape))
    mats = pl.BlockSpec((GROUP, W, W), lambda g: (g, 0, 0))
    cols = pl.BlockSpec((width, span), lambda g: (0, g))
    mat_shape = jax.ShapeDtypeStruct((heads, W, W), F32)
    params = pltpu.CompilerParams(dimension_semantics=("arbitrary",), vmem_limit_bytes=56 << 20)
    send, *kept = pl.pallas_call(
        first_kernel,
        grid=(steps,),
        in_specs=[
            smem, smem, whole(rows, width), whole(rows, width), cols, cols, cols, whole(width, heads),
            pl.BlockSpec((span, width), lambda g: (g, 0)), whole(rows, heads),
        ],
        out_specs=[pl.BlockSpec((GROUP, 3, W, W), lambda g: (g, 0, 0, 0))] + [mats] * 11,
        out_shape=[jax.ShapeDtypeStruct((heads, 3, W, W), F32)] + [mat_shape] * 11,
        compiler_params=params,
        name="block_forward",
    )(lengths, base, inputs, grad_out, w_query, w_key, w_value, w_beta, w_out, log_decay)
    size = lax.axis_size("ctx")
    groups = [[z * ROW + j for j in range(ROW)] for z in range(size // ROW)]
    mine = lax.all_to_all(send, "ctx", 0, 0, axis_index_groups=groups, tiled=True)
    small = pltpu.CompilerParams(vmem_limit_bytes=32 << 20)
    ends = pl.pallas_call(
        row_kernel, out_shape=jax.ShapeDtypeStruct((2, W, W), F32), compiler_params=small, name="row_ends"
    )(mine)
    state = lax.ppermute(ends[0], "ctx", [(j, j + ROW) for j in range(size - ROW)])
    grad = lax.ppermute(ends[1], "ctx", [(j + ROW, j) for j in range(size - ROW)])
    spread = pl.pallas_call(
        spread_kernel, out_shape=jax.ShapeDtypeStruct((ROW, 2, W, W), F32), compiler_params=small, name="row_states"
    )(mine, state, grad)
    back = lax.all_to_all(spread, "ctx", 0, 0, axis_index_groups=groups, tiled=True)
    total, grad_d = pl.pallas_call(
        second_kernel,
        grid=(steps,),
        in_specs=[pl.BlockSpec((GROUP, 2, W, W), lambda g: (g, 0, 0, 0))] + [mats] * 11 + [cols, cols, cols, whole(width, heads)],
        out_specs=[whole(rows, width), whole(rows, heads)],
        out_shape=[jax.ShapeDtypeStruct((rows, width), F32), jax.ShapeDtypeStruct((rows, heads), F32)],
        scratch_shapes=[pltpu.VMEM((rows, heads), F32)] * 4,
        compiler_params=params,
        name="block_backward",
    )(back, *kept, w_query, w_key, w_value, w_beta)
    grad_x = lax.psum_scatter(total, "head", scatter_dimension=1, tiled=True).astype(BF16)
    return (grad_x, grad_d)


def solution(mesh):
    placed = (
        P("ctx", None),
        P("ctx", None),
        P(None, "head"),
        P(None, "head"),
        P(None, "head"),
        P(None, "head"),
        P("head", None),
        P("ctx", "head"),
        P(),
    )
    return jax.shard_map(
        per_device,
        mesh=mesh,
        in_specs=placed,
        out_specs=(P("ctx", "head"), P("ctx", "head")),
        check_vma=False,
    )
```

```python
import jax
import jax.numpy as jnp
from jax import lax
from jax.experimental import pallas as pl
from jax.experimental.pallas import tpu as pltpu
from jax.sharding import PartitionSpec as P

F32 = jnp.float32
BF16 = jnp.bfloat16
W = 128
GROUP = 4
ROW = 8
NN = (((1,), (0,)), ((), ()))
NT = (((1,), (1,)), ((), ()))
TN = (((0,), (0,)), ((), ()))


def dot(a, b, dims=NN):
    return lax.dot_general(a, b, dims, preferred_element_type=F32)


def exact(a, b, dims=NN):
    return lax.dot_general(a, b, dims, precision=lax.Precision.HIGHEST, preferred_element_type=F32)


def halves(a):
    high = a.astype(BF16)
    return high, (a - high.astype(F32)).astype(BF16)


def mm3(a, b, dims=NN):
    ah, al = halves(a)
    bh, bl = halves(b)
    return dot(ah, bh, dims) + (dot(ah, bl, dims) + dot(al, bh, dims))


def iotas(shape):
    return lax.broadcasted_iota(jnp.int32, shape, 0), lax.broadcasted_iota(jnp.int32, shape, 1)


def column(array, index):
    lanes = lax.broadcasted_iota(jnp.int32, array.shape, 1)
    return jnp.sum(jnp.where(lanes == index, array, 0.0), axis=1, keepdims=True)


def inverse_all(mixes):
    ti, si = iotas((W, W))
    eye = jnp.where(ti == si, 1.0, 0.0)
    below = jnp.logical_and((ti >> 1) == (si >> 1), ti > si)
    done = [eye - jnp.where(below, a, 0.0) for a in mixes]
    for shift in range(1, 7):
        below = jnp.logical_and((ti >> (shift + 1)) == (si >> (shift + 1)), (ti >> shift) > (si >> shift))
        parts = [jnp.where(below, a, 0.0) for a in mixes]
        inner = [mm3(p, d) for p, d in zip(parts, done)]
        done = [d - mm3(d, i) for d, i in zip(done, inner)]
    return done


def first_kernel(
    len_ref, base_ref, x_ref, go_ref, wq_ref, wk_ref, wv_ref, wb_ref, wo_ref, dec_ref,
    send_ref, k_ref, q_ref, v_ref, do_ref, p_ref, l_ref, wkk_ref, w_ref, uv_ref, kw_ref, col_ref,
):
    step = pl.program_id(0)
    base = base_ref[0]
    ti, si = iotas((W, W))
    begin = jnp.int32(0)
    seg_t = jnp.zeros((W, W), jnp.int32)
    seg_s = jnp.zeros((W, W), jnp.int32)
    seg_in = jnp.int32(0)
    for j in range(len_ref.shape[0]):
        seg_t = seg_t + (ti + base >= begin).astype(jnp.int32)
        seg_s = seg_s + (si + base >= begin).astype(jnp.int32)
        seg_in = seg_in + (base - 1 >= begin).astype(jnp.int32)
        begin = begin + len_ref[j]
    keep = jnp.logical_and(seg_t == seg_s, ti >= si)
    strict = ti > si
    first = (seg_t == seg_in)[:, :1]
    x = x_ref[...]
    raw_q = dot(x, wq_ref[...])
    raw_k = dot(x, wk_ref[...])
    raw_v = dot(x, wv_ref[...])
    grad_o = dot(go_ref[...], wo_ref[...], NT)
    beta_all = 1.0 / (1.0 + jnp.exp(-dot(x, wb_ref[...], NT)))
    tril = jnp.where(ti >= si, 1.0, 0.0)
    run_all = exact(tril, dec_ref[...], NT)
    run_rows = exact(dec_ref[...], tril, NT)
    heads = range(GROUP)
    cut = lambda a, i: a[:, i * W:(i + 1) * W]
    ks, qs, betas, carries, weights, wkks, mixes, pmats = [], [], [], [], [], [], [], []
    for i in heads:
        head = step * GROUP + i
        rk = cut(raw_k, i)
        rq = cut(raw_q, i)
        inv_k = lax.rsqrt(jnp.sum(rk * rk, axis=1, keepdims=True) + 1e-06)
        inv_q = lax.rsqrt(jnp.sum(rq * rq, axis=1, keepdims=True) + 1e-06)
        k = rk * inv_k
        q = rq * inv_q * (W ** -0.5)
        beta = column(beta_all, head)
        run = column(run_all, head)
        heads_at = lax.broadcasted_iota(jnp.int32, run_rows.shape, 0)
        spread = run - jnp.sum(jnp.where(heads_at == head, run_rows, 0.0), axis=0, keepdims=True)
        weight = jnp.where(keep, jnp.exp(jnp.where(keep, spread, 0.0)), 0.0)
        carried = jnp.where(first, jnp.exp(run), 0.0)
        both = mm3(jnp.concatenate([k, q], axis=0), k, NT)
        wkk = jnp.where(strict, weight, 0.0) * both[:W]
        pmat = weight * both[W:]
        ks.append(k)
        qs.append(q)
        betas.append(beta)
        carries.append(carried)
        weights.append(weight)
        wkks.append(wkk)
        mixes.append(wkk * beta)
        pmats.append(pmat)
        lanes = si
        closing = jnp.sum(jnp.where(ti == si, jnp.broadcast_to(weight[W - 1:W, :], (W, W)), 0.0), axis=1, keepdims=True)
        col = jnp.where(lanes == 0, beta, jnp.where(lanes == 1, carried, jnp.where(lanes == 2, closing, jnp.where(lanes == 3, inv_k, inv_q))))
        col_ref[i] = col
        k_ref[i] = k
        q_ref[i] = q
        v_ref[i] = cut(raw_v, i)
        do_ref[i] = cut(grad_o, i)
        p_ref[i] = pmat
        wkk_ref[i] = wkk
        w_ref[i] = weight
    solved = inverse_all(mixes)
    for i in heads:
        k, q, beta, carried = ks[i], qs[i], betas[i], carries[i]
        l_ref[i] = solved[i]
        right = jnp.concatenate([beta * cut(raw_v, i), (beta * carried) * k], axis=1)
        both = mm3(solved[i], right)
        uv = both[:, :W]
        kw = both[:, W:]
        uv_ref[i] = uv
        kw_ref[i] = kw
        eff = carried * q - mm3(pmats[i], kw)
        closing = col_ref[i][:, 2:3]
        ends = mm3(jnp.concatenate([kw, uv], axis=1), closing * k, TN)
        last = carried[W - 1:W, :]
        send_ref[i, 0] = jnp.where(ti == si, last, 0.0) - ends[:W]
        send_ref[i, 1] = ends[W:]
        send_ref[i, 2] = mm3(cut(grad_o, i), eff, TN)


def row_kernel(r_ref, out_ref):
    state = r_ref[0, 1]
    grad = r_ref[ROW - 1, 2]
    for j in range(1, ROW):
        state = mm3(state, r_ref[j, 0]) + r_ref[j, 1]
        b = ROW - 1 - j
        grad = mm3(grad, r_ref[b, 0], NT) + r_ref[b, 2]
    out_ref[0] = state
    out_ref[1] = grad


def spread_kernel(r_ref, s_ref, g_ref, out_ref):
    state = s_ref[...]
    grad = g_ref[...]
    out_ref[0, 0] = state
    out_ref[ROW - 1, 1] = grad
    for j in range(1, ROW):
        state = mm3(state, r_ref[j - 1, 0]) + r_ref[j - 1, 1]
        out_ref[j, 0] = state
        b = ROW - j
        grad = mm3(grad, r_ref[b, 0], NT) + r_ref[b, 2]
        out_ref[b - 1, 1] = grad


def second_kernel(
    back_ref, k_ref, q_ref, v_ref, do_ref, p_ref, l_ref, wkk_ref, w_ref, uv_ref, kw_ref, col_ref,
    wq_ref, wk_ref, wv_ref, wb_ref, total_ref, gd_ref, cterm_ref, fterm_ref, eterm_ref, db_ref,
):
    step = pl.program_id(0)
    ti, si = iotas((W, W))
    strict = ti > si
    upper = jnp.where(si >= ti, 1.0, 0.0)
    t8, h8 = iotas((W, ROW))

    @pl.when(step == 0)
    def _():
        cterm_ref[...] = jnp.zeros((W, ROW), F32)
        fterm_ref[...] = jnp.zeros((W, ROW), F32)
        eterm_ref[...] = jnp.zeros((W, ROW), F32)
        db_ref[...] = jnp.zeros((W, ROW), F32)

    cterm, fterm, eterm, dball = cterm_ref[...], fterm_ref[...], eterm_ref[...], db_ref[...]
    gqs, gks, gvs = [], [], []
    for i in range(GROUP):
        head = step * GROUP + i
        s0, g1 = back_ref[i, 0], back_ref[i, 1]
        k, q, v, do = k_ref[i], q_ref[i], v_ref[i], do_ref[i]
        pmat, wkk, weight = p_ref[i], wkk_ref[i], w_ref[i]
        col = col_ref[i]
        beta, carried, closing, inv_k, inv_q = (col[:, j:j + 1] for j in range(5))
        u = uv_ref[i] - mm3(kw_ref[i], s0, NT)
        du = mm3(pmat, do, TN) + mm3(closing * k, g1, NT)
        dr = mm3(l_ref[i], du, TN)
        dpa = mm3(jnp.concatenate([do, dr], axis=0), u, NT)
        dp = dpa[:W]
        da = -dpa[W:]
        ds = mm3(jnp.concatenate([carried * do, dr], axis=0), s0)
        dq_state = ds[:W]
        dr_s = carried * ds[W:]
        ug = closing * mm3(u, g1)
        dqk = weight * dp
        dkk = jnp.where(strict, weight, 0.0) * da * beta
        front = mm3(jnp.concatenate([dqk, dkk], axis=0), k)
        dq = front[:W] + dq_state
        dk = front[W:] + mm3(jnp.concatenate([dkk, dqk], axis=0), jnp.concatenate([k, q], axis=0), TN)
        dk = dk - beta * dr_s + ug
        known = jnp.sum(dr_s * k, axis=1, keepdims=True)
        dbeta = jnp.sum(dr * v, axis=1, keepdims=True) - known + jnp.sum(da * wkk, axis=1, keepdims=True)
        dlogit = dbeta * beta * (1.0 - beta)
        pairs = dp * pmat + da * wkk * beta
        ph, plow = halves(pairs)
        ub = upper.astype(BF16)
        across = dot(ub, ph) + dot(ub, plow)
        evec = jnp.sum(jnp.where(strict, across, 0.0), axis=1, keepdims=True)
        fvec = jnp.sum(ug * k, axis=1, keepdims=True)
        cvec = jnp.sum(dq_state * q, axis=1, keepdims=True) - beta * known
        ends = carried[W - 1:W, :] * jnp.sum(jnp.sum(g1 * s0, axis=1, keepdims=True), axis=0, keepdims=True)
        cvec = cvec + jnp.where(t8[:, :1] == W - 1, ends, 0.0)
        here = h8 == head
        cterm = jnp.where(here, cvec, cterm)
        fterm = jnp.where(here, fvec, fterm)
        eterm = jnp.where(here, evec, eterm)
        dball = jnp.where(here, dlogit, dball)
        gk = inv_k * (dk - k * jnp.sum(k * dk, axis=1, keepdims=True))
        gq = (inv_q * (W ** -0.5)) * (dq - (q * float(W)) * jnp.sum(q * dq, axis=1, keepdims=True))
        gqs.append(gq.astype(BF16))
        gks.append(gk.astype(BF16))
        gvs.append((beta * dr).astype(BF16))
    cterm_ref[...], fterm_ref[...], eterm_ref[...], db_ref[...] = cterm, fterm, eterm, dball
    part = dot(jnp.concatenate(gqs, axis=1), wq_ref[...], NT)
    part = part + dot(jnp.concatenate(gks, axis=1), wk_ref[...], NT)
    part = part + dot(jnp.concatenate(gvs, axis=1), wv_ref[...], NT)

    chunks, _, wide = total_ref.shape

    @pl.when(step == 0)
    def _():
        for c in range(chunks):
            total_ref[c] = part[:, c * wide:(c + 1) * wide]

    @pl.when(step > 0)
    def _():
        full = part + dot(dball.astype(BF16), wb_ref[...])
        for c in range(chunks):
            total_ref[c] += full[:, c * wide:(c + 1) * wide]
        lower = jnp.where(strict, 1.0, 0.0)
        eye = jnp.where(ti == si, 1.0, 0.0)
        turn = (((0,), (1,)), ((), ()))
        gd_ref[...] = exact(cterm, upper, turn) + exact(fterm, lower, turn) + exact(eterm, eye, turn)


def per_device(inputs, grad_out, w_query, w_key, w_value, w_beta, w_out, log_decay, lengths):
    rows, width = inputs.shape
    heads = w_beta.shape[1]
    steps = heads // GROUP
    span = GROUP * W
    base = (lax.axis_index("ctx") * rows).astype(jnp.int32).reshape(1)
    smem = pl.BlockSpec(memory_space=pltpu.SMEM)
    whole = lambda *shape: pl.BlockSpec(shape, lambda g: (0,) * len(shape))
    mats = pl.BlockSpec((GROUP, W, W), lambda g: (g, 0, 0))
    cols = pl.BlockSpec((width, span), lambda g: (0, g))
    mat_shape = jax.ShapeDtypeStruct((heads, W, W), F32)
    params = pltpu.CompilerParams(dimension_semantics=("arbitrary",), vmem_limit_bytes=56 << 20)
    send, *kept = pl.pallas_call(
        first_kernel,
        grid=(steps,),
        in_specs=[
            smem, smem, whole(rows, width), whole(rows, width), cols, cols, cols, whole(heads, width),
            pl.BlockSpec((span, width), lambda g: (g, 0)), whole(heads, rows),
        ],
        out_specs=[pl.BlockSpec((GROUP, 3, W, W), lambda g: (g, 0, 0, 0))] + [mats] * 11,
        out_shape=[jax.ShapeDtypeStruct((heads, 3, W, W), F32)] + [mat_shape] * 11,
        compiler_params=params,
        name="block_forward",
    )(lengths, base, inputs, grad_out, w_query, w_key, w_value, w_beta.T, w_out, log_decay.T)
    size = lax.axis_size("ctx")
    groups = [[z * ROW + j for j in range(ROW)] for z in range(size // ROW)]
    mine = lax.all_to_all(send, "ctx", 0, 0, axis_index_groups=groups, tiled=True)
    small = pltpu.CompilerParams(vmem_limit_bytes=32 << 20)
    ends = pl.pallas_call(
        row_kernel, out_shape=jax.ShapeDtypeStruct((2, W, W), F32), compiler_params=small, name="row_ends"
    )(mine)
    state = lax.ppermute(ends[0], "ctx", [(j, j + ROW) for j in range(size - ROW)])
    grad = lax.ppermute(ends[1], "ctx", [(j + ROW, j) for j in range(size - ROW)])
    spread = pl.pallas_call(
        spread_kernel, out_shape=jax.ShapeDtypeStruct((ROW, 2, W, W), F32), compiler_params=small, name="row_states"
    )(mine, state, grad)
    back = lax.all_to_all(spread, "ctx", 0, 0, axis_index_groups=groups, tiled=True)
    sides = lax.axis_size("head")
    total, grad_d = pl.pallas_call(
        second_kernel,
        grid=(steps,),
        in_specs=[pl.BlockSpec((GROUP, 2, W, W), lambda g: (g, 0, 0, 0))] + [mats] * 11 + [cols, cols, cols, whole(heads, width)],
        out_specs=[whole(sides, rows, width // sides), whole(heads, rows)],
        out_shape=[jax.ShapeDtypeStruct((sides, rows, width // sides), F32), jax.ShapeDtypeStruct((heads, rows), F32)],
        scratch_shapes=[pltpu.VMEM((rows, heads), F32)] * 4,
        compiler_params=params,
        name="block_backward",
    )(back, *kept, w_query, w_key, w_value, w_beta.T)
    grad_x = jnp.sum(lax.all_to_all(total, "head", 0, 0, tiled=True), axis=0).astype(BF16)
    return (grad_x, grad_d.T)


def solution(mesh):
    placed = (
        P("ctx", None),
        P("ctx", None),
        P(None, "head"),
        P(None, "head"),
        P(None, "head"),
        P(None, "head"),
        P("head", None),
        P("ctx", "head"),
        P(),
    )
    return jax.shard_map(
        per_device,
        mesh=mesh,
        in_specs=placed,
        out_specs=(P("ctx", "head"), P("ctx", "head")),
        check_vma=False,
    )
```

```python
from functools import partial

import jax
import jax.numpy as jnp
from jax import lax
from jax.experimental import pallas as pl
from jax.experimental.pallas import tpu as pltpu
from jax.sharding import PartitionSpec as P

F32 = jnp.float32
BF16 = jnp.bfloat16
W = 128
GROUP = 4
NN = (((1,), (0,)), ((), ()))
NT = (((1,), (1,)), ((), ()))
TN = (((0,), (0,)), ((), ()))


def dot(a, b, dims=NN):
    return lax.dot_general(a, b, dims, preferred_element_type=F32)


def exact(a, b, dims=NN):
    return lax.dot_general(a, b, dims, precision=lax.Precision.HIGHEST, preferred_element_type=F32)


def halves(a):
    high = a.astype(BF16)
    return high, (a - high.astype(F32)).astype(BF16)


def mm3(a, b, dims=NN):
    ah, al = halves(a)
    bh, bl = halves(b)
    return dot(ah, bh, dims) + (dot(ah, bl, dims) + dot(al, bh, dims))


def iotas(shape):
    return lax.broadcasted_iota(jnp.int32, shape, 0), lax.broadcasted_iota(jnp.int32, shape, 1)


def column(array, index):
    lanes = lax.broadcasted_iota(jnp.int32, array.shape, 1)
    return jnp.sum(jnp.where(lanes == index, array, 0.0), axis=1, keepdims=True)


def inverse_all(mixes):
    ti, si = iotas((W, W))
    eye = jnp.where(ti == si, 1.0, 0.0)
    below = jnp.logical_and((ti >> 1) == (si >> 1), ti > si)
    done = [eye - jnp.where(below, a, 0.0) for a in mixes]
    for shift in range(1, 7):
        below = jnp.logical_and((ti >> (shift + 1)) == (si >> (shift + 1)), (ti >> shift) > (si >> shift))
        parts = [jnp.where(below, a, 0.0) for a in mixes]
        inner = [mm3(p, d) for p, d in zip(parts, done)]
        done = [d - mm3(d, i) for d, i in zip(done, inner)]
    return done


def first_kernel(
    meta_ref, x_ref, go_ref, wb_ref, dec_ref, wk_hbm, wq_hbm, wo_hbm, wv_hbm,
    send_ref, k_ref, q_ref, v_ref, do_ref, p_ref, l_ref, wkk_ref, w_ref, uv_ref, kw_ref, col_ref,
    wk_ref, wq_ref, wo_ref, wv_ref, sems,
):
    head0 = meta_ref[0]
    base = meta_ref[1]
    at = pl.ds(pl.multiple_of(head0 * W, GROUP * W), GROUP * W)
    get_k = pltpu.make_async_copy(wk_hbm.at[:, at], wk_ref, sems.at[0])
    get_q = pltpu.make_async_copy(wq_hbm.at[:, at], wq_ref, sems.at[1])
    get_o = pltpu.make_async_copy(wo_hbm.at[at, :], wo_ref, sems.at[2])
    get_v = pltpu.make_async_copy(wv_hbm.at[:, at], wv_ref, sems.at[3])
    for get in (get_k, get_q, get_v, get_o):
        get.start()
    ti, si = iotas((W, W))
    begin = jnp.int32(0)
    seg_t = jnp.zeros((W, W), jnp.int32)
    seg_s = jnp.zeros((W, W), jnp.int32)
    seg_in = jnp.int32(0)
    for j in range(2, meta_ref.shape[0]):
        seg_t = seg_t + (ti + base >= begin).astype(jnp.int32)
        seg_s = seg_s + (si + base >= begin).astype(jnp.int32)
        seg_in = seg_in + (base - 1 >= begin).astype(jnp.int32)
        begin = begin + meta_ref[j]
    keep = jnp.logical_and(seg_t == seg_s, ti >= si)
    strict = ti > si
    first = (seg_t == seg_in)[:, :1]
    x = x_ref[...]
    beta_all = 1.0 / (1.0 + jnp.exp(-dot(x, wb_ref[...], NT)))
    tril = jnp.where(ti >= si, 1.0, 0.0)
    run_all = exact(tril, dec_ref[...], NT)
    run_rows = exact(dec_ref[...], tril, NT)
    heads = range(GROUP)
    cut = lambda a, i: a[:, i * W:(i + 1) * W]
    get_k.wait()
    raw_k = dot(x, wk_ref[...])
    get_q.wait()
    raw_q = dot(x, wq_ref[...])
    ks, qs, betas, carries, wkks, mixes, pmats = [], [], [], [], [], [], []
    for i in heads:
        head = head0 + i
        rk = cut(raw_k, i)
        rq = cut(raw_q, i)
        inv_k = lax.rsqrt(jnp.sum(rk * rk, axis=1, keepdims=True) + 1e-06)
        inv_q = lax.rsqrt(jnp.sum(rq * rq, axis=1, keepdims=True) + 1e-06)
        k = rk * inv_k
        q = rq * inv_q * (W ** -0.5)
        beta = column(beta_all, head)
        run = column(run_all, head)
        heads_at = lax.broadcasted_iota(jnp.int32, run_rows.shape, 0)
        spread = run - jnp.sum(jnp.where(heads_at == head, run_rows, 0.0), axis=0, keepdims=True)
        weight = jnp.where(keep, jnp.exp(jnp.where(keep, spread, 0.0)), 0.0)
        carried = jnp.where(first, jnp.exp(run), 0.0)
        both = mm3(jnp.concatenate([k, q], axis=0), k, NT)
        wkk = jnp.where(strict, weight, 0.0) * both[:W]
        pmat = weight * both[W:]
        ks.append(k)
        qs.append(q)
        betas.append(beta)
        carries.append(carried)
        wkks.append(wkk)
        mixes.append(wkk * beta)
        pmats.append(pmat)
        lanes = si
        closing = jnp.sum(jnp.where(ti == si, jnp.broadcast_to(weight[W - 1:W, :], (W, W)), 0.0), axis=1, keepdims=True)
        col = jnp.where(lanes == 0, beta, jnp.where(lanes == 1, carried, jnp.where(lanes == 2, closing, jnp.where(lanes == 3, inv_k, inv_q))))
        col_ref[i] = col
        k_ref[i] = k
        q_ref[i] = q
        p_ref[i] = pmat
        wkk_ref[i] = wkk
        w_ref[i] = weight
    get_v.wait()
    raw_v = dot(x, wv_ref[...])
    get_o.wait()
    grad_o = dot(go_ref[...], wo_ref[...], NT)
    solved = inverse_all(mixes)
    for i in heads:
        k, q, beta, carried = ks[i], qs[i], betas[i], carries[i]
        l_ref[i] = solved[i]
        v_ref[i] = cut(raw_v, i)
        do_ref[i] = cut(grad_o, i)
        right = jnp.concatenate([beta * cut(raw_v, i), (beta * carried) * k], axis=1)
        both = mm3(solved[i], right)
        uv = both[:, :W]
        kw = both[:, W:]
        uv_ref[i] = uv
        kw_ref[i] = kw
        eff = carried * q - mm3(pmats[i], kw)
        closing = col_ref[i][:, 2:3]
        ends = mm3(jnp.concatenate([kw, uv], axis=1), closing * k, TN)
        last = carried[W - 1:W, :]
        send_ref[i, 0] = jnp.where(ti == si, last, 0.0) - ends[:W]
        send_ref[i, 1] = ends[W:]
        send_ref[i, 2] = mm3(cut(grad_o, i), eff, TN)


def join_kernel(core_ref, own_ref, other_ref, out_ref):
    second = core_ref[0] == 1
    for i in range(GROUP):
        ta = jnp.where(second, other_ref[i, 0], own_ref[i, 0])
        tb = jnp.where(second, own_ref[i, 0], other_ref[i, 0])
        oa = jnp.where(second, other_ref[i, 1], own_ref[i, 1])
        ob = jnp.where(second, own_ref[i, 1], other_ref[i, 1])
        ga = jnp.where(second, other_ref[i, 2], own_ref[i, 2])
        gb = jnp.where(second, own_ref[i, 2], other_ref[i, 2])
        front = mm3(jnp.concatenate([ta, oa], axis=0), tb)
        out_ref[i, 0] = front[:W]
        out_ref[i, 1] = front[W:] + ob
        out_ref[i, 2] = mm3(gb, ta, NT) + ga


def row_kernel(r_ref, state_ref, grad_ref):
    size = r_ref.shape[0]
    state = r_ref[0, 1]
    grad = r_ref[size - 1, 2]
    for j in range(1, size):
        state = mm3(state, r_ref[j, 0]) + r_ref[j, 1]
        b = size - 1 - j
        grad = mm3(grad, r_ref[b, 0], NT) + r_ref[b, 2]
    state_ref[...] = state
    grad_ref[...] = grad


def spread_kernel(r_ref, s_ref, g_ref, out_ref):
    size = r_ref.shape[0]
    state = s_ref[...]
    grad = g_ref[...]
    out_ref[0, 0] = state
    out_ref[size - 1, 1] = grad
    for j in range(1, size):
        state = mm3(state, r_ref[j - 1, 0]) + r_ref[j - 1, 1]
        out_ref[j, 0] = state
        b = size - j
        grad = mm3(grad, r_ref[b, 0], NT) + r_ref[b, 2]
        out_ref[b - 1, 1] = grad


def part_kernel(core_ref, own_ref, other_ref, chip_ref, mine_ref, give_ref):
    second = core_ref[0] == 1
    for i in range(GROUP):
        ta = jnp.where(second, other_ref[i, 0], own_ref[i, 0])
        tb = jnp.where(second, own_ref[i, 0], other_ref[i, 0])
        oa = jnp.where(second, other_ref[i, 1], own_ref[i, 1])
        gb = jnp.where(second, own_ref[i, 2], other_ref[i, 2])
        s_in, g_end = chip_ref[i, 0], chip_ref[i, 1]
        s_mid = mm3(s_in, ta) + oa
        g_mid = mm3(g_end, tb, NT) + gb
        mine_ref[i, 0] = jnp.where(second, s_mid, s_in)
        mine_ref[i, 1] = jnp.where(second, g_end, g_mid)
        give_ref[i, 0] = jnp.where(second, s_in, s_mid)
        give_ref[i, 1] = jnp.where(second, g_mid, g_end)


def second_kernel(chained, *refs):
    (meta_ref, back_ref, k_ref, q_ref, v_ref, do_ref, p_ref, l_ref, wkk_ref, w_ref, uv_ref, kw_ref, col_ref,
     wb_ref, wq_hbm, wk_hbm, wv_hbm) = refs[:17]
    refs = refs[17:]
    if chained:
        before_ref, gd_before_ref = refs[:2]
        refs = refs[2:]
    total_ref, gd_ref, wq_ref, wk_ref, wv_ref, sems = refs
    head0 = meta_ref[0]
    at = pl.ds(pl.multiple_of(head0 * W, GROUP * W), GROUP * W)
    gets = [
        pltpu.make_async_copy(hbm.at[:, at], ref, sems.at[j])
        for j, (hbm, ref) in enumerate(((wq_hbm, wq_ref), (wk_hbm, wk_ref), (wv_hbm, wv_ref)))
    ]
    for get in gets:
        get.start()
    ti, si = iotas((W, W))
    strict = ti > si
    upper = jnp.where(si >= ti, 1.0, 0.0)
    t8, h8 = iotas((W, 8))
    none = jnp.zeros((W, 8), F32)
    cterm, fterm, eterm, dball = none, none, none, none
    gqs, gks, gvs = [], [], []
    for i in range(GROUP):
        head = head0 + i
        s0, g1 = back_ref[i, 0], back_ref[i, 1]
        k, q, v, do = k_ref[i], q_ref[i], v_ref[i], do_ref[i]
        pmat, wkk, weight = p_ref[i], wkk_ref[i], w_ref[i]
        col = col_ref[i]
        beta, carried, closing, inv_k, inv_q = (col[:, j:j + 1] for j in range(5))
        u = uv_ref[i] - mm3(kw_ref[i], s0, NT)
        du = mm3(pmat, do, TN) + mm3(closing * k, g1, NT)
        dr = mm3(l_ref[i], du, TN)
        dpa = mm3(jnp.concatenate([do, dr], axis=0), u, NT)
        dp = dpa[:W]
        da = -dpa[W:]
        ds = mm3(jnp.concatenate([carried * do, dr], axis=0), s0)
        dq_state = ds[:W]
        dr_s = carried * ds[W:]
        ug = closing * mm3(u, g1)
        dqk = weight * dp
        dkk = jnp.where(strict, weight, 0.0) * da * beta
        front = mm3(jnp.concatenate([dqk, dkk], axis=0), k)
        dq = front[:W] + dq_state
        dk = front[W:] + mm3(jnp.concatenate([dkk, dqk], axis=0), jnp.concatenate([k, q], axis=0), TN)
        dk = dk - beta * dr_s + ug
        known = jnp.sum(dr_s * k, axis=1, keepdims=True)
        dbeta = jnp.sum(dr * v, axis=1, keepdims=True) - known + jnp.sum(da * wkk, axis=1, keepdims=True)
        dlogit = dbeta * beta * (1.0 - beta)
        pairs = dp * pmat + da * wkk * beta
        ph, plow = halves(pairs)
        ub = upper.astype(BF16)
        across = dot(ub, ph) + dot(ub, plow)
        evec = jnp.sum(jnp.where(strict, across, 0.0), axis=1, keepdims=True)
        fvec = jnp.sum(ug * k, axis=1, keepdims=True)
        cvec = jnp.sum(dq_state * q, axis=1, keepdims=True) - beta * known
        ends = carried[W - 1:W, :] * jnp.sum(jnp.sum(g1 * s0, axis=1, keepdims=True), axis=0, keepdims=True)
        cvec = cvec + jnp.where(t8[:, :1] == W - 1, ends, 0.0)
        here = h8 == head
        cterm = jnp.where(here, cvec, cterm)
        fterm = jnp.where(here, fvec, fterm)
        eterm = jnp.where(here, evec, eterm)
        dball = jnp.where(here, dlogit, dball)
        gk = inv_k * (dk - k * jnp.sum(k * dk, axis=1, keepdims=True))
        gq = (inv_q * (W ** -0.5)) * (dq - (q * float(W)) * jnp.sum(q * dq, axis=1, keepdims=True))
        gqs.append(gq.astype(BF16))
        gks.append(gk.astype(BF16))
        gvs.append((beta * dr).astype(BF16))
    for get in gets:
        get.wait()
    part = dot(jnp.concatenate(gqs, axis=1), wq_ref[...], NT)
    part = part + dot(jnp.concatenate(gks, axis=1), wk_ref[...], NT)
    part = part + dot(jnp.concatenate(gvs, axis=1), wv_ref[...], NT)
    part = part + dot(dball.astype(BF16), wb_ref[...])
    chunks, _, wide = total_ref.shape
    for c in range(chunks):
        piece = part[:, c * wide:(c + 1) * wide]
        total_ref[c] = before_ref[c] + piece if chained else piece
    lower = jnp.where(strict, 1.0, 0.0)
    eye = jnp.where(ti == si, 1.0, 0.0)
    turn = (((0,), (1,)), ((), ()))
    decays = exact(cterm, upper, turn) + exact(fterm, lower, turn) + exact(eterm, eye, turn)
    gd_ref[...] = gd_before_ref[...] + decays if chained else decays


def per_device(inputs, grad_out, w_query, w_key, w_value, w_beta, w_out, log_decay, lengths):
    rows, width = inputs.shape
    heads = w_beta.shape[1]
    span = GROUP * W
    size = lax.axis_size("ctx")
    sides = lax.axis_size("head")
    place = lax.axis_index("ctx").astype(jnp.int32)
    core = (place & 1).reshape(1)
    keep0 = core * GROUP
    give0 = GROUP - keep0
    base = (place * rows).reshape(1)
    beta_t, decay_t = w_beta.T, log_decay.T
    smem = pl.BlockSpec(memory_space=pltpu.SMEM)
    vmem = pl.BlockSpec(memory_space=pltpu.VMEM)
    hbm = pl.BlockSpec(memory_space=pl.ANY)
    shape = lambda *dims: jax.ShapeDtypeStruct(dims, F32)
    params = pltpu.CompilerParams(vmem_limit_bytes=56 << 20)
    small = pltpu.CompilerParams(vmem_limit_bytes=32 << 20)
    tall, flat = pltpu.VMEM((width, span), BF16), pltpu.VMEM((span, width), BF16)

    def forward(head0):
        send, *kept = pl.pallas_call(
            first_kernel,
            in_specs=[smem] + [vmem] * 4 + [hbm] * 4,
            out_specs=[vmem] * 12,
            out_shape=[shape(GROUP, 3, W, W)] + [shape(GROUP, W, W)] * 11,
            scratch_shapes=[tall, tall, flat, tall, pltpu.SemaphoreType.DMA((4,))],
            compiler_params=params,
            name="block_forward",
        )(jnp.concatenate([head0, base, lengths]), inputs, grad_out, beta_t, decay_t, w_key, w_query, w_out, w_value)
        return send, kept

    def backward(head0, back, kept, before):
        return pl.pallas_call(
            partial(second_kernel, bool(before)),
            in_specs=[smem] + [vmem] * 13 + [hbm] * 3 + [vmem] * len(before),
            out_specs=[vmem] * 2,
            out_shape=[shape(sides, rows, width // sides), shape(heads, rows)],
            scratch_shapes=[tall, tall, tall, pltpu.SemaphoreType.DMA((3,))],
            compiler_params=params,
            name="block_backward",
        )(head0, back, *kept, beta_t, w_query, w_key, w_value, *before)

    pair = [(j, j ^ 1) for j in range(size)]
    groups = [[z + j * 2 + c for j in range(GROUP)] for z in range(0, size, 2 * GROUP) for c in range(2)]
    give, give_kept = forward(give0)
    other = lax.ppermute(give, "ctx", pair)
    own, own_kept = forward(keep0)
    whole = pl.pallas_call(
        join_kernel, in_specs=[smem, vmem, vmem], out_shape=shape(GROUP, 3, W, W), compiler_params=small, name="chip_join"
    )(core, own, other)
    mine = lax.all_to_all(whole, "ctx", 0, 0, axis_index_groups=groups, tiled=True)
    ends = pl.pallas_call(
        row_kernel, out_shape=[shape(W, W)] * 2, compiler_params=small, name="row_ends"
    )(mine)
    step = 2 * GROUP
    state = lax.ppermute(ends[0], "ctx", [(j, j + step) for j in range(size - step)])
    grad = lax.ppermute(ends[1], "ctx", [(j + step, j) for j in range(size - step)])
    spread = pl.pallas_call(
        spread_kernel, out_shape=shape(GROUP, 2, W, W), compiler_params=small, name="row_states"
    )(mine, state, grad)
    chips = lax.all_to_all(spread, "ctx", 0, 0, axis_index_groups=groups, tiled=True)
    own_back, give_back = pl.pallas_call(
        part_kernel, in_specs=[smem, vmem, vmem, vmem], out_shape=[shape(GROUP, 2, W, W)] * 2, compiler_params=small, name="chip_part"
    )(core, own, other, chips)
    other_back = lax.ppermute(give_back, "ctx", pair)
    before = backward(keep0, own_back, own_kept, ())
    total, grad_d = backward(give0, other_back, give_kept, before)
    grad_x = jnp.sum(lax.all_to_all(total, "head", 0, 0, tiled=True), axis=0).astype(BF16)
    return (grad_x, grad_d.T)


def solution(mesh):
    placed = (
        P("ctx", None),
        P("ctx", None),
        P(None, "head"),
        P(None, "head"),
        P(None, "head"),
        P(None, "head"),
        P("head", None),
        P("ctx", "head"),
        P(),
    )
    return jax.shard_map(
        per_device,
        mesh=mesh,
        in_specs=placed,
        out_specs=(P("ctx", "head"), P("ctx", "head")),
        check_vma=False,
    )
```

```python
from functools import partial

import jax
import jax.numpy as jnp
from jax import lax
from jax.experimental import pallas as pl
from jax.experimental.pallas import tpu as pltpu
from jax.sharding import PartitionSpec as P

F32 = jnp.float32
BF16 = jnp.bfloat16
W = 128
GROUP = 4
NN = (((1,), (0,)), ((), ()))
NT = (((1,), (1,)), ((), ()))
TN = (((0,), (0,)), ((), ()))


def dot(a, b, dims=NN):
    return lax.dot_general(a, b, dims, preferred_element_type=F32)


def exact(a, b, dims=NN):
    return lax.dot_general(a, b, dims, precision=lax.Precision.HIGHEST, preferred_element_type=F32)


def halves(a):
    high = a.astype(BF16)
    return high, (a - high.astype(F32)).astype(BF16)


def mm3(a, b, dims=NN):
    ah, al = halves(a)
    bh, bl = halves(b)
    (ca,), (cb,) = dims[0]
    return dot(jnp.concatenate([ah, al], axis=ca), jnp.concatenate([bh, bh], axis=cb), dims) + dot(ah, bl, dims)


def iotas(shape):
    return lax.broadcasted_iota(jnp.int32, shape, 0), lax.broadcasted_iota(jnp.int32, shape, 1)


def column(array, index):
    lanes = lax.broadcasted_iota(jnp.int32, array.shape, 1)
    return jnp.sum(jnp.where(lanes == index, array, 0.0), axis=1, keepdims=True)


def inverse_all(mixes):
    ti, si = iotas((W, W))
    eye = jnp.where(ti == si, 1.0, 0.0)
    below = jnp.logical_and((ti >> 1) == (si >> 1), ti > si)
    done = [eye - jnp.where(below, a, 0.0) for a in mixes]
    for shift in range(1, 7):
        below = jnp.logical_and((ti >> (shift + 1)) == (si >> (shift + 1)), (ti >> shift) > (si >> shift))
        parts = [jnp.where(below, a, 0.0) for a in mixes]
        inner = [mm3(p, d) for p, d in zip(parts, done)]
        done = [d - mm3(d, i) for d, i in zip(done, inner)]
    return done


def head_columns(head0):
    return pl.ds(pl.multiple_of(head0 * W, GROUP * W), GROUP * W)


def give_kernel(
    head_ref, keep_head_ref, base_ref, len_hbm, x_hbm, go_hbm, wb_hbm, dec_hbm, wk_hbm, wq_hbm, wo_hbm, wv_hbm, *refs
):
    outs, refs = refs[:12], refs[12:]
    x_ref, go_ref, beta_ref, run_ref, rows_ref, keep_ref, first_ref, wk_ref, wq_ref, wv_ref, wk2_ref, wq2_ref = refs[:12]
    len_ref, wb_ref, dec_ref, wo_ref, sems = refs[12:]
    head0 = head_ref[0]
    base = base_ref[0]
    at = head_columns(head0)
    at2 = head_columns(keep_head_ref[0])
    pairs = (
        (wk_hbm.at[:, at], wk_ref), (x_hbm, x_ref), (len_hbm, len_ref), (dec_hbm, dec_ref), (wb_hbm, wb_ref),
        (wq_hbm.at[:, at], wq_ref), (wv_hbm.at[:, at], wv_ref), (go_hbm, go_ref), (wo_hbm.at[at, :], wo_ref),
        (wk_hbm.at[:, at2], wk2_ref), (wq_hbm.at[:, at2], wq2_ref),
    )
    gets = [pltpu.make_async_copy(src, dst, sems.at[j]) for j, (src, dst) in enumerate(pairs)]
    for get in gets:
        get.start()
    gets[2].wait()
    ti, si = iotas((W, W))
    begin = jnp.int32(0)
    seg_t = jnp.zeros((W, 1), jnp.int32)
    seg_s = jnp.zeros((1, W), jnp.int32)
    seg_in = jnp.int32(0)
    for j in range(len_ref.shape[0]):
        seg_t = seg_t + (ti[:, :1] + base >= begin).astype(jnp.int32)
        seg_s = seg_s + (si[:1, :] + base >= begin).astype(jnp.int32)
        seg_in = seg_in + (base - 1 >= begin).astype(jnp.int32)
        begin = begin + len_ref[j]
    keep_ref[...] = jnp.where(jnp.logical_and(seg_t == seg_s, ti >= si), 1.0, 0.0)
    first_ref[...] = jnp.broadcast_to(jnp.where(seg_t == seg_in, 1.0, 0.0), first_ref.shape)
    gets[3].wait()
    tril = jnp.where(ti >= si, 1.0, 0.0)
    run_ref[...] = exact(tril, dec_ref[...], NT)
    rows_ref[...] = exact(dec_ref[...], tril, NT)
    gets[4].wait()
    gets[1].wait()
    beta_ref[...] = 1.0 / (1.0 + jnp.exp(-dot(x_ref[...], wb_ref[...], NT)))
    block_body(
        head0, x_ref, go_ref, beta_ref, run_ref, rows_ref, keep_ref, first_ref, wk_ref, wq_ref, wv_ref, wo_ref,
        (gets[0], gets[5], gets[6], gets[7], gets[8]), outs,
    )
    gets[9].wait()
    gets[10].wait()


def keep_kernel(
    head_ref, x_ref, go_ref, beta_ref, run_ref, rows_ref, keep_ref, first_ref, wk_ref, wq_ref, wo_hbm, wv_hbm, *refs
):
    outs = refs[:12]
    wv_ref, wo_ref, sems = refs[12:]
    head0 = head_ref[0]
    at = head_columns(head0)
    get_v = pltpu.make_async_copy(wv_hbm.at[:, at], wv_ref, sems.at[0])
    get_o = pltpu.make_async_copy(wo_hbm.at[at, :], wo_ref, sems.at[1])
    get_v.start()
    get_o.start()
    block_body(
        head0, x_ref, go_ref, beta_ref, run_ref, rows_ref, keep_ref, first_ref, wk_ref, wq_ref, wv_ref, wo_ref,
        (None, None, get_v, None, get_o), outs,
    )


def block_body(
    head0, x_ref, go_ref, beta_ref, run_ref, rows_ref, keep_ref, first_ref, wk_ref, wq_ref, wv_ref, wo_ref, gets, outs
):
    send_ref, k_ref, q_ref, v_ref, do_ref, p_ref, l_ref, wkk_ref, w_ref, uv_ref, kw_ref, col_ref = outs

    def ready(*which):
        for j in which:
            if gets[j] is not None:
                gets[j].wait()

    ti, si = iotas((W, W))
    strict = ti > si
    keep = keep_ref[...] > 0.0
    first = first_ref[...][:, :1] > 0.0
    beta_all, run_all, run_rows = beta_ref[...], run_ref[...], rows_ref[...]
    heads = range(GROUP)
    cut = lambda a, i: a[:, i * W:(i + 1) * W]
    ready(0)
    x = x_ref[...]
    raw_k = dot(x, wk_ref[...])
    ready(1)
    raw_q = dot(x, wq_ref[...])
    ks, qs, betas, carries, wkks, mixes, pmats = [], [], [], [], [], [], []
    for i in heads:
        head = head0 + i
        rk = cut(raw_k, i)
        rq = cut(raw_q, i)
        inv_k = lax.rsqrt(jnp.sum(rk * rk, axis=1, keepdims=True) + 1e-06)
        inv_q = lax.rsqrt(jnp.sum(rq * rq, axis=1, keepdims=True) + 1e-06)
        k = rk * inv_k
        q = rq * inv_q * (W ** -0.5)
        beta = column(beta_all, head)
        run = column(run_all, head)
        heads_at = lax.broadcasted_iota(jnp.int32, run_rows.shape, 0)
        spread = run - jnp.sum(jnp.where(heads_at == head, run_rows, 0.0), axis=0, keepdims=True)
        weight = jnp.where(keep, jnp.exp(jnp.where(keep, spread, 0.0)), 0.0)
        carried = jnp.where(first, jnp.exp(run), 0.0)
        both = mm3(jnp.concatenate([k, q], axis=0), k, NT)
        wkk = jnp.where(strict, weight, 0.0) * both[:W]
        pmat = weight * both[W:]
        ks.append(k)
        qs.append(q)
        betas.append(beta)
        carries.append(carried)
        wkks.append(wkk)
        mixes.append(wkk * beta)
        pmats.append(pmat)
        lanes = si
        closing = jnp.sum(jnp.where(ti == si, jnp.broadcast_to(weight[W - 1:W, :], (W, W)), 0.0), axis=1, keepdims=True)
        col = jnp.where(lanes == 0, beta, jnp.where(lanes == 1, carried, jnp.where(lanes == 2, closing, jnp.where(lanes == 3, inv_k, inv_q))))
        col_ref[i] = col
        k_ref[i] = k
        q_ref[i] = q
        p_ref[i] = pmat
        wkk_ref[i] = wkk
        w_ref[i] = weight
    ready(2)
    raw_v = dot(x, wv_ref[...])
    ready(3, 4)
    grad_o = dot(go_ref[...], wo_ref[...], NT)
    solved = inverse_all(mixes)
    for i in heads:
        k, q, beta, carried = ks[i], qs[i], betas[i], carries[i]
        l_ref[i] = solved[i]
        v_ref[i] = cut(raw_v, i)
        do_ref[i] = cut(grad_o, i)
        right = jnp.concatenate([beta * cut(raw_v, i), (beta * carried) * k], axis=1)
        both = mm3(solved[i], right)
        uv = both[:, :W]
        kw = both[:, W:]
        uv_ref[i] = uv
        kw_ref[i] = kw
        eff = carried * q - mm3(pmats[i], kw)
        closing = col_ref[i][:, 2:3]
        ends = mm3(jnp.concatenate([kw, uv], axis=1), closing * k, TN)
        last = carried[W - 1:W, :]
        send_ref[i, 0] = jnp.where(ti == si, last, 0.0) - ends[:W]
        send_ref[i, 1] = ends[W:]
        send_ref[i, 2] = mm3(cut(grad_o, i), eff, TN)


def join_kernel(core_ref, own_ref, other_ref, out_ref):
    second = core_ref[0] == 1
    for i in range(GROUP):
        ta = jnp.where(second, other_ref[i, 0], own_ref[i, 0])
        tb = jnp.where(second, own_ref[i, 0], other_ref[i, 0])
        oa = jnp.where(second, other_ref[i, 1], own_ref[i, 1])
        ob = jnp.where(second, own_ref[i, 1], other_ref[i, 1])
        ga = jnp.where(second, other_ref[i, 2], own_ref[i, 2])
        gb = jnp.where(second, own_ref[i, 2], other_ref[i, 2])
        front = mm3(jnp.concatenate([ta, oa], axis=0), tb)
        out_ref[i, 0] = front[:W]
        out_ref[i, 1] = front[W:] + ob
        out_ref[i, 2] = mm3(gb, ta, NT) + ga


def row_kernel(r_ref, state_ref, grad_ref):
    size = r_ref.shape[0]
    state = r_ref[0, 1]
    grad = r_ref[size - 1, 2]
    for j in range(1, size):
        state = mm3(state, r_ref[j, 0]) + r_ref[j, 1]
        b = size - 1 - j
        grad = mm3(grad, r_ref[b, 0], NT) + r_ref[b, 2]
    state_ref[...] = state
    grad_ref[...] = grad


def spread_kernel(r_ref, s_ref, g_ref, out_ref):
    size = r_ref.shape[0]
    state = s_ref[...]
    grad = g_ref[...]
    out_ref[0, 0] = state
    out_ref[size - 1, 1] = grad
    for j in range(1, size):
        state = mm3(state, r_ref[j - 1, 0]) + r_ref[j - 1, 1]
        out_ref[j, 0] = state
        b = size - j
        grad = mm3(grad, r_ref[b, 0], NT) + r_ref[b, 2]
        out_ref[b - 1, 1] = grad


def part_kernel(core_ref, own_ref, other_ref, chip_ref, mine_ref, give_ref):
    second = core_ref[0] == 1
    for i in range(GROUP):
        ta = jnp.where(second, other_ref[i, 0], own_ref[i, 0])
        tb = jnp.where(second, own_ref[i, 0], other_ref[i, 0])
        oa = jnp.where(second, other_ref[i, 1], own_ref[i, 1])
        gb = jnp.where(second, own_ref[i, 2], other_ref[i, 2])
        s_in, g_end = chip_ref[i, 0], chip_ref[i, 1]
        s_mid = mm3(s_in, ta) + oa
        g_mid = mm3(g_end, tb, NT) + gb
        mine_ref[i, 0] = jnp.where(second, s_mid, s_in)
        mine_ref[i, 1] = jnp.where(second, g_end, g_mid)
        give_ref[i, 0] = jnp.where(second, s_in, s_mid)
        give_ref[i, 1] = jnp.where(second, g_mid, g_end)


def second_kernel(chained, *refs):
    (meta_ref, back_ref, k_ref, q_ref, v_ref, do_ref, p_ref, l_ref, wkk_ref, w_ref, uv_ref, kw_ref, col_ref,
     wb_ref, wq_ref, wk_ref, wv_ref) = refs[:17]
    refs = refs[17:]
    if chained:
        before_ref, gd_before_ref = refs[:2]
        refs = refs[2:]
    total_ref, gd_ref = refs
    head0 = meta_ref[0]
    ti, si = iotas((W, W))
    strict = ti > si
    upper = jnp.where(si >= ti, 1.0, 0.0)
    t8, h8 = iotas((W, 8))
    none = jnp.zeros((W, 8), F32)
    cterm, fterm, eterm, dball = none, none, none, none
    gqs, gks, gvs = [], [], []
    for i in range(GROUP):
        head = head0 + i
        s0, g1 = back_ref[i, 0], back_ref[i, 1]
        k, q, v, do = k_ref[i], q_ref[i], v_ref[i], do_ref[i]
        pmat, wkk, weight = p_ref[i], wkk_ref[i], w_ref[i]
        col = col_ref[i]
        beta, carried, closing, inv_k, inv_q = (col[:, j:j + 1] for j in range(5))
        u = uv_ref[i] - mm3(kw_ref[i], s0, NT)
        du = mm3(pmat, do, TN) + mm3(closing * k, g1, NT)
        dr = mm3(l_ref[i], du, TN)
        dpa = mm3(jnp.concatenate([do, dr], axis=0), u, NT)
        dp = dpa[:W]
        da = -dpa[W:]
        ds = mm3(jnp.concatenate([carried * do, dr], axis=0), s0)
        dq_state = ds[:W]
        dr_s = carried * ds[W:]
        ug = closing * mm3(u, g1)
        dqk = weight * dp
        dkk = jnp.where(strict, weight, 0.0) * da * beta
        front = mm3(jnp.concatenate([dqk, dkk], axis=0), k)
        dq = front[:W] + dq_state
        dk = front[W:] + mm3(jnp.concatenate([dkk, dqk], axis=0), jnp.concatenate([k, q], axis=0), TN)
        dk = dk - beta * dr_s + ug
        known = jnp.sum(dr_s * k, axis=1, keepdims=True)
        dbeta = jnp.sum(dr * v, axis=1, keepdims=True) - known + jnp.sum(da * wkk, axis=1, keepdims=True)
        dlogit = dbeta * beta * (1.0 - beta)
        pairs = dp * pmat + da * wkk * beta
        ph, plow = halves(pairs)
        ub = upper.astype(BF16)
        across = dot(ub, ph) + dot(ub, plow)
        evec = jnp.sum(jnp.where(strict, across, 0.0), axis=1, keepdims=True)
        fvec = jnp.sum(ug * k, axis=1, keepdims=True)
        cvec = jnp.sum(dq_state * q, axis=1, keepdims=True) - beta * known
        ends = carried[W - 1:W, :] * jnp.sum(jnp.sum(g1 * s0, axis=1, keepdims=True), axis=0, keepdims=True)
        cvec = cvec + jnp.where(t8[:, :1] == W - 1, ends, 0.0)
        here = h8 == head
        cterm = jnp.where(here, cvec, cterm)
        fterm = jnp.where(here, fvec, fterm)
        eterm = jnp.where(here, evec, eterm)
        dball = jnp.where(here, dlogit, dball)
        gk = inv_k * (dk - k * jnp.sum(k * dk, axis=1, keepdims=True))
        gq = (inv_q * (W ** -0.5)) * (dq - (q * float(W)) * jnp.sum(q * dq, axis=1, keepdims=True))
        gqs.append(gq.astype(BF16))
        gks.append(gk.astype(BF16))
        gvs.append((beta * dr).astype(BF16))
    part = dot(jnp.concatenate(gqs, axis=1), wq_ref[...], NT)
    part = part + dot(jnp.concatenate(gks, axis=1), wk_ref[...], NT)
    part = part + dot(jnp.concatenate(gvs, axis=1), wv_ref[...], NT)
    part = part + dot(dball.astype(BF16), wb_ref[...])
    chunks, _, wide = total_ref.shape
    for c in range(chunks):
        piece = part[:, c * wide:(c + 1) * wide]
        total_ref[c] = before_ref[c] + piece if chained else piece
    lower = jnp.where(strict, 1.0, 0.0)
    eye = jnp.where(ti == si, 1.0, 0.0)
    turn = (((0,), (1,)), ((), ()))
    decays = exact(cterm, upper, turn) + exact(fterm, lower, turn) + exact(eterm, eye, turn)
    gd_ref[...] = gd_before_ref[...] + decays if chained else decays


SMEM = pl.BlockSpec(memory_space=pltpu.SMEM)
VMEM = pl.BlockSpec(memory_space=pltpu.VMEM)
HBM = pl.BlockSpec(memory_space=pltpu.HBM)


def shape(*dims):
    return jax.ShapeDtypeStruct(dims, F32)


def in_hbm(*arrays):
    return [pltpu.with_memory_space_constraint(a, pltpu.HBM) for a in arrays]


def block_shapes():
    return [shape(GROUP, 3, W, W)] + [shape(GROUP, W, W)] * 11


def run_give(give0, keep0, base, lengths, inputs, grad_out, beta_t, decay_t, w_key, w_query, w_out, w_value):
    rows, width = inputs.shape
    heads, span = beta_t.shape[0], GROUP * W
    wide = jax.ShapeDtypeStruct((rows, width), BF16)
    tall = jax.ShapeDtypeStruct((width, span), BF16)
    out = pl.pallas_call(
        give_kernel,
        in_specs=[SMEM] * 3 + [HBM] * 9,
        out_specs=[VMEM] * 24,
        out_shape=block_shapes() + [wide, wide, shape(rows, heads), shape(rows, heads), shape(heads, rows), shape(W, W), shape(W, heads)] + [tall] * 5,
        scratch_shapes=[
            pltpu.SMEM(lengths.shape, jnp.int32), pltpu.VMEM(beta_t.shape, BF16), pltpu.VMEM(decay_t.shape, F32),
            pltpu.VMEM((span, width), BF16), pltpu.SemaphoreType.DMA((11,)),
        ],
        compiler_params=pltpu.CompilerParams(vmem_limit_bytes=28 << 20),
        name="block_forward_give",
    )(give0, keep0, base, *in_hbm(lengths, inputs, grad_out, beta_t, decay_t, w_key, w_query, w_out, w_value))
    return out[0], out[1:12], out[12:19], out[19:22], out[22:]


def run_keep(keep0, shared, w_key2, w_query2, w_out, w_value):
    width, span = w_key2.shape
    out = pl.pallas_call(
        keep_kernel,
        in_specs=[SMEM] + [VMEM] * 9 + [HBM] * 2,
        out_specs=[VMEM] * 13,
        out_shape=block_shapes() + [jax.ShapeDtypeStruct((width, span), BF16)],
        scratch_shapes=[pltpu.VMEM((span, width), BF16), pltpu.SemaphoreType.DMA((2,))],
        compiler_params=pltpu.CompilerParams(vmem_limit_bytes=24 << 20),
        name="block_forward_keep",
    )(keep0, *shared, w_key2, w_query2, *in_hbm(w_out, w_value))
    return out[0], out[1:12], out[12]


def run_backward(sides, head0, back, kept, beta_t, w_key, w_query, w_value, before):
    heads, width = beta_t.shape
    return pl.pallas_call(
        partial(second_kernel, bool(before)),
        in_specs=[SMEM] + [VMEM] * 16 + [VMEM] * len(before),
        out_specs=[VMEM] * 2,
        out_shape=[shape(sides, W, width // sides), shape(heads, W)],
        compiler_params=pltpu.CompilerParams(vmem_limit_bytes=24 << 20),
        name="block_backward",
    )(head0, back, *kept, beta_t, w_query, w_key, w_value, *before)


def per_device(inputs, grad_out, w_query, w_key, w_value, w_beta, w_out, log_decay, lengths):
    rows, width = inputs.shape
    heads = w_beta.shape[1]
    size = lax.axis_size("ctx")
    sides = lax.axis_size("head")
    place = lax.axis_index("ctx").astype(jnp.int32)
    core = (place & 1).reshape(1)
    keep0 = core * GROUP
    give0 = GROUP - keep0
    base = (place * rows).reshape(1)
    beta_t, decay_t = w_beta.T, log_decay.T
    small = pltpu.CompilerParams(vmem_limit_bytes=8 << 20)

    pair = [(j, j ^ 1) for j in range(size)]
    groups = [[z + j * 2 + c for j in range(GROUP)] for z in range(0, size, 2 * GROUP) for c in range(2)]
    give, give_kept, shared, give_w, keep_w = run_give(
        give0, keep0, base, lengths, inputs, grad_out, beta_t, decay_t, w_key, w_query, w_out, w_value
    )
    other = lax.ppermute(give, "ctx", pair)
    own, own_kept, keep_v = run_keep(keep0, shared, *keep_w, w_out, w_value)
    whole = pl.pallas_call(
        join_kernel, in_specs=[SMEM] + [VMEM] * 2, out_shape=shape(GROUP, 3, W, W), compiler_params=small, name="chip_join"
    )(core, own, other)
    mine = lax.all_to_all(whole, "ctx", 0, 0, axis_index_groups=groups, tiled=True)
    ends = pl.pallas_call(
        row_kernel, out_shape=[shape(W, W)] * 2, compiler_params=small, name="row_ends"
    )(mine)
    step = 2 * GROUP
    state = lax.ppermute(ends[0], "ctx", [(j, j + step) for j in range(size - step)])
    grad = lax.ppermute(ends[1], "ctx", [(j + step, j) for j in range(size - step)])
    spread = pl.pallas_call(
        spread_kernel, out_shape=shape(GROUP, 2, W, W), compiler_params=small, name="row_states"
    )(mine, state, grad)
    chips = lax.all_to_all(spread, "ctx", 0, 0, axis_index_groups=groups, tiled=True)
    own_back, give_back = pl.pallas_call(
        part_kernel, in_specs=[SMEM] + [VMEM] * 3, out_shape=[shape(GROUP, 2, W, W)] * 2, compiler_params=small, name="chip_part"
    )(core, own, other, chips)
    other_back = lax.ppermute(give_back, "ctx", pair)
    before = run_backward(sides, keep0, own_back, own_kept, beta_t, *keep_w, keep_v, ())
    total, grad_d = run_backward(sides, give0, other_back, give_kept, beta_t, *give_w, before)
    grad_x = jnp.sum(lax.all_to_all(total, "head", 0, 0, tiled=True), axis=0).astype(BF16)
    return (grad_x, grad_d.T)


def solution(mesh):
    placed = (
        P("ctx", None),
        P("ctx", None),
        P(None, "head"),
        P(None, "head"),
        P(None, "head"),
        P(None, "head"),
        P("head", None),
        P("ctx", "head"),
        P(),
    )
    return jax.shard_map(
        per_device,
        mesh=mesh,
        in_specs=placed,
        out_specs=(P("ctx", "head"), P("ctx", "head")),
        check_vma=False,
    )
```

```python
from functools import partial

import jax
import jax.numpy as jnp
from jax import lax
from jax.experimental import pallas as pl
from jax.experimental.pallas import tpu as pltpu
from jax.sharding import PartitionSpec as P

F32 = jnp.float32
BF16 = jnp.bfloat16
W = 128
GROUP = 4
SIDES = 4
NN = (((1,), (0,)), ((), ()))
NT = (((1,), (1,)), ((), ()))
TN = (((0,), (0,)), ((), ()))


def dot(a, b, dims=NN):
    return lax.dot_general(a, b, dims, preferred_element_type=F32)


def exact(a, b, dims=NN):
    return lax.dot_general(a, b, dims, precision=lax.Precision.HIGHEST, preferred_element_type=F32)


def halves(a):
    high = a.astype(BF16)
    return high, (a - high.astype(F32)).astype(BF16)


def mm3(a, b, dims=NN):
    ah, al = halves(a)
    bh, bl = halves(b)
    (ca,), (cb,) = dims[0]
    return dot(jnp.concatenate([ah, al], axis=ca), jnp.concatenate([bh, bh], axis=cb), dims) + dot(ah, bl, dims)


def iotas(shape):
    return lax.broadcasted_iota(jnp.int32, shape, 0), lax.broadcasted_iota(jnp.int32, shape, 1)


def column(array, index):
    lanes = lax.broadcasted_iota(jnp.int32, array.shape, 1)
    return jnp.sum(jnp.where(lanes == index, array, 0.0), axis=1, keepdims=True)


def inverse_all(mixes):
    ti, si = iotas((W, W))
    eye = jnp.where(ti == si, 1.0, 0.0)
    below = jnp.logical_and((ti >> 1) == (si >> 1), ti > si)
    done = [eye - jnp.where(below, a, 0.0) for a in mixes]
    for shift in range(1, 7):
        below = jnp.logical_and((ti >> (shift + 1)) == (si >> (shift + 1)), (ti >> shift) > (si >> shift))
        parts = [jnp.where(below, a, 0.0) for a in mixes]
        inner = [mm3(p, d) for p, d in zip(parts, done)]
        done = [d - mm3(d, i) for d, i in zip(done, inner)]
    return done


def head_columns(head0):
    return pl.ds(pl.multiple_of(head0 * W, GROUP * W), GROUP * W)


def give_kernel(
    place_ref, side_ref, len_hbm, x_hbm, go_hbm, wb_hbm, dec_hbm, wk_hbm, wq_hbm, wo_hbm, wv_hbm, *refs
):
    ids_ref, outs, refs = refs[0], refs[1:3], refs[3:]
    x_ref, go_ref, beta_ref, run_ref, rows_ref, keep_ref, first_ref, wkq_ref, wv_ref, wkq2_ref = refs[:10]
    len_ref, wb_ref, dec_ref, wo_ref, sems = refs[10:]
    keep0 = (place_ref[0] & 1) * GROUP
    head0 = GROUP - keep0
    ids_ref[0] = place_ref[0]
    ids_ref[1] = side_ref[0]
    base = place_ref[0] * W
    at = head_columns(head0)
    at2 = head_columns(keep0)
    pairs = (
        (wk_hbm.at[:, at], wkq_ref.at[0]), (x_hbm, x_ref), (len_hbm, len_ref), (dec_hbm, dec_ref), (wb_hbm, wb_ref),
        (wq_hbm.at[:, at], wkq_ref.at[1]), (wv_hbm.at[:, at], wv_ref), (go_hbm, go_ref), (wo_hbm.at[at, :], wo_ref),
        (wk_hbm.at[:, at2], wkq2_ref.at[0]), (wq_hbm.at[:, at2], wkq2_ref.at[1]),
    )
    gets = [pltpu.make_async_copy(src, dst, sems.at[j]) for j, (src, dst) in enumerate(pairs)]
    for get in gets:
        get.start()
    gets[2].wait()
    ti, si = iotas((W, W))
    begin = jnp.int32(0)
    seg_t = jnp.zeros((W, 1), jnp.int32)
    seg_s = jnp.zeros((1, W), jnp.int32)
    seg_in = jnp.int32(0)
    for j in range(len_ref.shape[0]):
        seg_t = seg_t + (ti[:, :1] + base >= begin).astype(jnp.int32)
        seg_s = seg_s + (si[:1, :] + base >= begin).astype(jnp.int32)
        seg_in = seg_in + (base - 1 >= begin).astype(jnp.int32)
        begin = begin + len_ref[j]
    keep_ref[...] = jnp.where(jnp.logical_and(seg_t == seg_s, ti >= si), 1.0, 0.0)
    first_ref[...] = jnp.broadcast_to(jnp.where(seg_t == seg_in, 1.0, 0.0), first_ref.shape)
    gets[3].wait()
    tril = jnp.where(ti >= si, 1.0, 0.0)
    run_ref[...] = exact(tril, dec_ref[...], NT)
    rows_ref[...] = exact(dec_ref[...], tril, NT)
    gets[4].wait()
    gets[1].wait()
    beta_ref[...] = 1.0 / (1.0 + jnp.exp(-dot(x_ref[...], wb_ref[...], NT)))
    block_body(
        head0, x_ref, go_ref, beta_ref, run_ref, rows_ref, keep_ref, first_ref, wkq_ref, wv_ref, wo_ref,
        (gets[0], gets[5], gets[6], gets[7], gets[8]), outs,
    )
    gets[9].wait()
    gets[10].wait()


def keep_kernel(
    ids_ref, x_ref, go_ref, beta_ref, run_ref, rows_ref, keep_ref, first_ref, wkq_ref, wo_hbm, wv_hbm, *refs
):
    outs = refs[:2]
    wv_ref, wo_ref, sems = refs[2:]
    head0 = (ids_ref[0] & 1) * GROUP
    at = head_columns(head0)
    get_v = pltpu.make_async_copy(wv_hbm.at[:, at], wv_ref, sems.at[0])
    get_o = pltpu.make_async_copy(wo_hbm.at[at, :], wo_ref, sems.at[1])
    get_v.start()
    get_o.start()
    block_body(
        head0, x_ref, go_ref, beta_ref, run_ref, rows_ref, keep_ref, first_ref, wkq_ref, wv_ref, wo_ref,
        (None, None, get_v, None, get_o), outs,
    )


def block_body(
    head0, x_ref, go_ref, beta_ref, run_ref, rows_ref, keep_ref, first_ref, wkq_ref, wv_ref, wo_ref, gets, outs
):
    send_ref, kept_ref = outs

    def ready(*which):
        for j in which:
            if gets[j] is not None:
                gets[j].wait()

    ti, si = iotas((W, W))
    strict = ti > si
    keep = keep_ref[...] > 0.0
    first = first_ref[...][:, :1] > 0.0
    beta_all, run_all, run_rows = beta_ref[...], run_ref[...], rows_ref[...]
    heads = range(GROUP)
    cut = lambda a, i: a[:, i * W:(i + 1) * W]
    ready(0)
    x = x_ref[...]
    raw_k = dot(x, wkq_ref[0])
    ready(1)
    raw_q = dot(x, wkq_ref[1])
    ks, qs, betas, carries, wkks, mixes, pmats = [], [], [], [], [], [], []
    for i in heads:
        head = head0 + i
        rk = cut(raw_k, i)
        rq = cut(raw_q, i)
        inv_k = lax.rsqrt(jnp.sum(rk * rk, axis=1, keepdims=True) + 1e-06)
        inv_q = lax.rsqrt(jnp.sum(rq * rq, axis=1, keepdims=True) + 1e-06)
        k = rk * inv_k
        q = rq * inv_q * (W ** -0.5)
        beta = column(beta_all, head)
        run = column(run_all, head)
        heads_at = lax.broadcasted_iota(jnp.int32, run_rows.shape, 0)
        spread = run - jnp.sum(jnp.where(heads_at == head, run_rows, 0.0), axis=0, keepdims=True)
        weight = jnp.where(keep, jnp.exp(jnp.where(keep, spread, 0.0)), 0.0)
        carried = jnp.where(first, jnp.exp(run), 0.0)
        both = mm3(jnp.concatenate([k, q], axis=0), k, NT)
        wkk = jnp.where(strict, weight, 0.0) * both[:W]
        pmat = weight * both[W:]
        ks.append(k)
        qs.append(q)
        betas.append(beta)
        carries.append(carried)
        wkks.append(wkk)
        mixes.append(wkk * beta)
        pmats.append(pmat)
        lanes = si
        closing = jnp.sum(jnp.where(ti == si, jnp.broadcast_to(weight[W - 1:W, :], (W, W)), 0.0), axis=1, keepdims=True)
        col = jnp.where(lanes == 0, beta, jnp.where(lanes == 1, carried, jnp.where(lanes == 2, closing, jnp.where(lanes == 3, inv_k, inv_q))))
        kept_ref[i, 10] = col
        kept_ref[i, 0] = k
        kept_ref[i, 1] = q
        kept_ref[i, 4] = pmat
        kept_ref[i, 6] = wkk
        kept_ref[i, 7] = weight
    ready(2)
    raw_v = dot(x, wv_ref[...])
    ready(3, 4)
    grad_o = dot(go_ref[...], wo_ref[...], NT)
    solved = inverse_all(mixes)
    for i in heads:
        k, q, beta, carried = ks[i], qs[i], betas[i], carries[i]
        kept_ref[i, 5] = solved[i]
        kept_ref[i, 2] = cut(raw_v, i)
        kept_ref[i, 3] = cut(grad_o, i)
        right = jnp.concatenate([beta * cut(raw_v, i), (beta * carried) * k], axis=1)
        both = mm3(solved[i], right)
        uv = both[:, :W]
        kw = both[:, W:]
        kept_ref[i, 8] = uv
        kept_ref[i, 9] = kw
        eff = carried * q - mm3(pmats[i], kw)
        closing = kept_ref[i, 10][:, 2:3]
        ends = mm3(jnp.concatenate([kw, uv], axis=1), closing * k, TN)
        last = carried[W - 1:W, :]
        send_ref[i, 0] = jnp.where(ti == si, last, 0.0) - ends[:W]
        send_ref[i, 1] = ends[W:]
        send_ref[i, 2] = mm3(cut(grad_o, i), eff, TN)


def join_kernel(place_ref, own_ref, other_ref, *out_refs):
    second = (place_ref[0] & 1) == 1
    x = place_ref[0] >> 1
    for d in range(GROUP):
        i = (x + d) & (GROUP - 1)
        out_ref = out_refs[d]
        ta = jnp.where(second, other_ref[i, 0], own_ref[i, 0])
        tb = jnp.where(second, own_ref[i, 0], other_ref[i, 0])
        oa = jnp.where(second, other_ref[i, 1], own_ref[i, 1])
        ob = jnp.where(second, own_ref[i, 1], other_ref[i, 1])
        ga = jnp.where(second, other_ref[i, 2], own_ref[i, 2])
        gb = jnp.where(second, own_ref[i, 2], other_ref[i, 2])
        front = mm3(jnp.concatenate([ta, oa], axis=0), tb)
        out_ref[0] = front[:W]
        out_ref[1] = front[W:] + ob
        out_ref[2] = mm3(gb, ta, NT) + ga


def row_kernel(place_ref, *refs):
    x = place_ref[0] >> 1
    parts, (r_ref, state_ref, grad_ref) = refs[:GROUP], refs[GROUP:]
    for d, part in enumerate(parts):
        r_ref[(x - d) & (GROUP - 1)] = part[...]
    state = r_ref[0, 1]
    grad = r_ref[GROUP - 1, 2]
    for j in range(1, GROUP):
        state = mm3(state, r_ref[j, 0]) + r_ref[j, 1]
        b = GROUP - 1 - j
        grad = mm3(grad, r_ref[b, 0], NT) + r_ref[b, 2]
    state_ref[...] = state
    grad_ref[...] = grad


def spread_kernel(place_ref, r_ref, s_ref, g_ref, *refs):
    x = place_ref[0] >> 1
    outs, all_ref = refs[:GROUP], refs[GROUP]
    state = s_ref[...]
    grad = g_ref[...]
    all_ref[0, 0] = state
    all_ref[GROUP - 1, 1] = grad
    for j in range(1, GROUP):
        state = mm3(state, r_ref[j - 1, 0]) + r_ref[j - 1, 1]
        all_ref[j, 0] = state
        b = GROUP - j
        grad = mm3(grad, r_ref[b, 0], NT) + r_ref[b, 2]
        all_ref[b - 1, 1] = grad
    for d, out in enumerate(outs):
        out[...] = all_ref[(x + d) & (GROUP - 1)]


def part_kernel(place_ref, own_ref, other_ref, *refs):
    chips, (mine_ref, give_ref) = refs[:GROUP], refs[GROUP:]
    second = (place_ref[0] & 1) == 1
    x = place_ref[0] >> 1
    for d, chip_ref in enumerate(chips):
        i = (x - d) & (GROUP - 1)
        ta = jnp.where(second, other_ref[i, 0], own_ref[i, 0])
        tb = jnp.where(second, own_ref[i, 0], other_ref[i, 0])
        oa = jnp.where(second, other_ref[i, 1], own_ref[i, 1])
        gb = jnp.where(second, own_ref[i, 2], other_ref[i, 2])
        s_in, g_end = chip_ref[0], chip_ref[1]
        s_mid = mm3(s_in, ta) + oa
        g_mid = mm3(g_end, tb, NT) + gb
        mine_ref[i, 0] = jnp.where(second, s_mid, s_in)
        mine_ref[i, 1] = jnp.where(second, g_end, g_mid)
        give_ref[i, 0] = jnp.where(second, s_in, s_mid)
        give_ref[i, 1] = jnp.where(second, g_mid, g_end)


def back_project(side, grads, db, wkq_ref, wv_ref, wb_ref, wide):
    at = pl.ds(pl.multiple_of(side * wide, wide), wide)
    n = grads.shape[1] // 3
    piece = dot(grads[:, :n], wkq_ref[1, at, :], NT) + dot(grads[:, n:2 * n], wkq_ref[0, at, :], NT)
    return piece + dot(grads[:, 2 * n:], wv_ref[at, :], NT) + dot(db, wb_ref[:, at])


def chunk_kernel(distance, ids_ref, grads_ref, db_ref, before_ref, wb_ref, wkq_ref, wv_ref, out_ref):
    side = (ids_ref[1] + distance) & (SIDES - 1)
    piece = back_project(side, grads_ref[...], db_ref[...], wkq_ref, wv_ref, wb_ref, out_ref.shape[1])
    out_ref[...] = before_ref[distance] + piece


def second_kernel(chained, *refs):
    ids_ref, back_ref, kept_ref, wb_ref, wkq_ref, wv_ref = refs[:6]
    refs = refs[6:]
    if chained:
        before_ref, gd_before_ref, total_ref, gd_ref, grads_ref, db_ref = refs
    else:
        total_ref, gd_ref = refs
    keep0 = (ids_ref[0] & 1) * GROUP
    head0 = GROUP - keep0 if chained else keep0
    side = ids_ref[1]
    ti, si = iotas((W, W))
    strict = ti > si
    upper = jnp.where(si >= ti, 1.0, 0.0)
    t8, h8 = iotas((W, 8))
    none = jnp.zeros((W, 8), F32)
    cterm, fterm, eterm, dball = none, none, none, none
    gqs, gks, gvs = [], [], []
    for i in range(GROUP):
        head = head0 + i
        s0, g1 = back_ref[i, 0], back_ref[i, 1]
        k, q, v, do = kept_ref[i, 0], kept_ref[i, 1], kept_ref[i, 2], kept_ref[i, 3]
        pmat, wkk, weight = kept_ref[i, 4], kept_ref[i, 6], kept_ref[i, 7]
        col = kept_ref[i, 10]
        beta, carried, closing, inv_k, inv_q = (col[:, j:j + 1] for j in range(5))
        u = kept_ref[i, 8] - mm3(kept_ref[i, 9], s0, NT)
        du = mm3(pmat, do, TN) + mm3(closing * k, g1, NT)
        dr = mm3(kept_ref[i, 5], du, TN)
        dpa = mm3(jnp.concatenate([do, dr], axis=0), u, NT)
        dp = dpa[:W]
        da = -dpa[W:]
        ds = mm3(jnp.concatenate([carried * do, dr], axis=0), s0)
        dq_state = ds[:W]
        dr_s = carried * ds[W:]
        ug = closing * mm3(u, g1)
        dqk = weight * dp
        dkk = jnp.where(strict, weight, 0.0) * da * beta
        front = mm3(jnp.concatenate([dqk, dkk], axis=0), k)
        dq = front[:W] + dq_state
        dk = front[W:] + mm3(jnp.concatenate([dkk, dqk], axis=0), jnp.concatenate([k, q], axis=0), TN)
        dk = dk - beta * dr_s + ug
        known = jnp.sum(dr_s * k, axis=1, keepdims=True)
        dbeta = jnp.sum(dr * v, axis=1, keepdims=True) - known + jnp.sum(da * wkk, axis=1, keepdims=True)
        dlogit = dbeta * beta * (1.0 - beta)
        pairs = dp * pmat + da * wkk * beta
        ph, plow = halves(pairs)
        ub = upper.astype(BF16)
        across = dot(ub, ph) + dot(ub, plow)
        evec = jnp.sum(jnp.where(strict, across, 0.0), axis=1, keepdims=True)
        fvec = jnp.sum(ug * k, axis=1, keepdims=True)
        cvec = jnp.sum(dq_state * q, axis=1, keepdims=True) - beta * known
        ends = carried[W - 1:W, :] * jnp.sum(jnp.sum(g1 * s0, axis=1, keepdims=True), axis=0, keepdims=True)
        cvec = cvec + jnp.where(t8[:, :1] == W - 1, ends, 0.0)
        here = h8 == head
        cterm = jnp.where(here, cvec, cterm)
        fterm = jnp.where(here, fvec, fterm)
        eterm = jnp.where(here, evec, eterm)
        dball = jnp.where(here, dlogit, dball)
        gk = inv_k * (dk - k * jnp.sum(k * dk, axis=1, keepdims=True))
        gq = (inv_q * (W ** -0.5)) * (dq - (q * float(W)) * jnp.sum(q * dq, axis=1, keepdims=True))
        gqs.append(gq.astype(BF16))
        gks.append(gk.astype(BF16))
        gvs.append((beta * dr).astype(BF16))
    grads = jnp.concatenate(gqs + gks + gvs, axis=1)
    db = dball.astype(BF16)
    wide = total_ref.shape[-1]
    project = lambda d: back_project((side + d) & (SIDES - 1), grads, db, wkq_ref, wv_ref, wb_ref, wide)
    if chained:
        total_ref[...] = before_ref[2] + project(2)
        grads_ref[...] = grads
        db_ref[...] = db
    else:
        for d in range(SIDES):
            total_ref[d] = project(d)
    lower = jnp.where(strict, 1.0, 0.0)
    eye = jnp.where(ti == si, 1.0, 0.0)
    turn = (((0,), (1,)), ((), ()))
    decays = exact(cterm, upper, turn) + exact(fterm, lower, turn) + exact(eterm, eye, turn)
    gd_ref[...] = gd_before_ref[...] + decays if chained else decays


SMEM = pl.BlockSpec(memory_space=pltpu.SMEM)
VMEM = pl.BlockSpec(memory_space=pltpu.VMEM)
HBM = pl.BlockSpec(memory_space=pltpu.HBM)


def shape(*dims):
    return jax.ShapeDtypeStruct(dims, F32)


def in_hbm(*arrays):
    return [pltpu.with_memory_space_constraint(a, pltpu.HBM) for a in arrays]


def block_shapes():
    return [shape(GROUP, 3, W, W), shape(GROUP, 11, W, W)]


def run_give(place, side, lengths, inputs, grad_out, beta_t, decay_t, w_key, w_query, w_out, w_value):
    rows, width = inputs.shape
    heads, span = beta_t.shape[0], GROUP * W
    wide = jax.ShapeDtypeStruct((rows, width), BF16)
    tall = jax.ShapeDtypeStruct((width, span), BF16)
    two = jax.ShapeDtypeStruct((2, width, span), BF16)
    out = pl.pallas_call(
        give_kernel,
        in_specs=[SMEM] * 2 + [HBM] * 9,
        out_specs=[SMEM] + [VMEM] * 12,
        out_shape=[jax.ShapeDtypeStruct((2,), jnp.int32)] + block_shapes() + [wide, wide, shape(rows, heads), shape(rows, heads), shape(heads, rows), shape(W, W), shape(W, heads)] + [two, tall, two],
        scratch_shapes=[
            pltpu.SMEM(lengths.shape, jnp.int32), pltpu.VMEM(beta_t.shape, BF16), pltpu.VMEM(decay_t.shape, F32),
            pltpu.VMEM((span, width), BF16), pltpu.SemaphoreType.DMA((11,)),
        ],
        compiler_params=pltpu.CompilerParams(vmem_limit_bytes=28 << 20),
        name="block_forward_give",
    )(place, side, *in_hbm(lengths, inputs, grad_out, beta_t, decay_t, w_key, w_query, w_out, w_value))
    return out[0], out[1], out[2], out[3:10], out[10:12], out[12]


def run_keep(ids, shared, w_keep, w_out, w_value):
    _, width, span = w_keep.shape
    out = pl.pallas_call(
        keep_kernel,
        in_specs=[SMEM] + [VMEM] * 8 + [HBM] * 2,
        out_specs=[VMEM] * 3,
        out_shape=block_shapes() + [jax.ShapeDtypeStruct((width, span), BF16)],
        scratch_shapes=[pltpu.VMEM((span, width), BF16), pltpu.SemaphoreType.DMA((2,))],
        compiler_params=pltpu.CompilerParams(vmem_limit_bytes=24 << 20),
        name="block_forward_keep",
    )(ids, *shared, w_keep, *in_hbm(w_out, w_value))
    return out


def run_backward(ids, back, kept, beta_t, w_both, w_value, before):
    heads, width = beta_t.shape
    wide = width // SIDES
    if before:
        out_shape = [shape(W, wide), shape(heads, W), jax.ShapeDtypeStruct((W, 3 * GROUP * W), BF16), jax.ShapeDtypeStruct((W, heads), BF16)]
    else:
        out_shape = [shape(SIDES, W, wide), shape(heads, W)]
    return pl.pallas_call(
        partial(second_kernel, bool(before)),
        in_specs=[SMEM] + [VMEM] * 5 + [VMEM] * len(before),
        out_specs=[VMEM] * len(out_shape),
        out_shape=out_shape,
        compiler_params=pltpu.CompilerParams(vmem_limit_bytes=24 << 20),
        name="block_backward",
    )(ids, back, kept, beta_t, w_both, w_value, *before)


def run_chunk(distance, ids, grads, db, before, beta_t, w_both, w_value):
    return pl.pallas_call(
        partial(chunk_kernel, distance),
        in_specs=[SMEM] + [VMEM] * 6,
        out_specs=VMEM,
        out_shape=shape(*before.shape[1:]),
        compiler_params=pltpu.CompilerParams(vmem_limit_bytes=16 << 20),
        name="chunk",
    )(ids, grads, db, before, beta_t, w_both, w_value)


def per_device(inputs, grad_out, w_query, w_key, w_value, w_beta, w_out, log_decay, lengths):
    size = lax.axis_size("ctx")
    place = lax.axis_index("ctx").astype(jnp.int32).reshape(1)
    side = lax.axis_index("head").astype(jnp.int32).reshape(1)
    beta_t, decay_t = w_beta.T, log_decay.T
    small = pltpu.CompilerParams(vmem_limit_bytes=8 << 20)

    pair = [(j, j ^ 1) for j in range(size)]
    ids, give, give_kept, shared, give_w, keep_w = run_give(
        place, side, lengths, inputs, grad_out, beta_t, decay_t, w_key, w_query, w_out, w_value
    )
    other = lax.ppermute(give, "ctx", pair)
    own, own_kept, keep_v = run_keep(ids, shared, keep_w, w_out, w_value)
    row = 2 * GROUP

    def call(kernel, name, scalars, arrays, out_shape, scratch=()):
        return pl.pallas_call(
            kernel,
            in_specs=[SMEM] * len(scalars) + [VMEM] * len(arrays),
            out_specs=[VMEM] * len(out_shape),
            out_shape=out_shape,
            scratch_shapes=list(scratch),
            compiler_params=small,
            name=name,
        )(*scalars, *arrays)

    def along_x(parts):
        got = {0: parts[0]}
        for d in (2, 1, 3):
            moves = [(j, j - j % row + (j + 2 * d) % row) for j in range(size)]
            got[d] = lax.ppermute(parts[d], "ctx", moves)
        return [got[d] for d in range(GROUP)]

    whole = call(join_kernel, "chip_join", (ids,), (own, other), [shape(3, W, W)] * GROUP)
    mine, state, grad = call(
        row_kernel, "row_ends", (ids,), along_x(whole), [shape(GROUP, 3, W, W), shape(W, W), shape(W, W)]
    )
    state = lax.ppermute(state, "ctx", [(j, j + row) for j in range(size - row)])
    grad = lax.ppermute(grad, "ctx", [(j + row, j) for j in range(size - row)])
    spread = call(
        spread_kernel, "row_states", (ids,), (mine, state, grad), [shape(2, W, W)] * GROUP, [pltpu.VMEM((GROUP, 2, W, W), F32)]
    )
    own_back, give_back = call(
        part_kernel, "chip_part", (ids,), (own, other, *along_x(spread)), [shape(GROUP, 2, W, W)] * 2
    )
    other_back = lax.ppermute(give_back, "ctx", pair)
    before = run_backward(ids, own_back, own_kept, beta_t, keep_w, keep_v, ())
    far, grad_d, grads, db = run_backward(ids, other_back, give_kept, beta_t, *give_w, before)
    total = 0.0
    for d in (2, 1, 3, 0):
        chunk = far if d == 2 else run_chunk(d, ids, grads, db, before[0], beta_t, *give_w)
        if d:
            chunk = lax.ppermute(chunk, "head", [(j, (j + d) % SIDES) for j in range(SIDES)])
        total = total + chunk
    return (total.astype(BF16), grad_d.T)


def solution(mesh):
    placed = (
        P("ctx", None),
        P("ctx", None),
        P(None, "head"),
        P(None, "head"),
        P(None, "head"),
        P(None, "head"),
        P("head", None),
        P("ctx", "head"),
        P(),
    )
    return jax.shard_map(
        per_device,
        mesh=mesh,
        in_specs=placed,
        out_specs=(P("ctx", "head"), P("ctx", "head")),
        check_vma=False,
    )
```

```python
from functools import partial

import jax
import jax.numpy as jnp
from jax import lax
from jax.experimental import pallas as pl
from jax.experimental.pallas import tpu as pltpu
from jax.sharding import PartitionSpec as P

F32 = jnp.float32
BF16 = jnp.bfloat16
W = 128
GROUP = 4
SIDES = 4
ORDER = (2, 1, 3)
NN = (((1,), (0,)), ((), ()))
NT = (((1,), (1,)), ((), ()))
TN = (((0,), (0,)), ((), ()))


def dot(a, b, dims=NN):
    return lax.dot_general(a, b, dims, preferred_element_type=F32)


def exact(a, b, dims=NN):
    return lax.dot_general(a, b, dims, precision=lax.Precision.HIGHEST, preferred_element_type=F32)


def halves(a):
    high = a.astype(BF16)
    return high, (a - high.astype(F32)).astype(BF16)


def mm3(a, b, dims=NN):
    ah, al = halves(a)
    bh, bl = halves(b)
    (ca,), (cb,) = dims[0]
    return dot(jnp.concatenate([ah, al], axis=ca), jnp.concatenate([bh, bh], axis=cb), dims) + dot(ah, bl, dims)


def iotas(shape):
    return lax.broadcasted_iota(jnp.int32, shape, 0), lax.broadcasted_iota(jnp.int32, shape, 1)


def column(array, index):
    lanes = lax.broadcasted_iota(jnp.int32, array.shape, 1)
    return jnp.sum(jnp.where(lanes == index, array, 0.0), axis=1, keepdims=True)


def inverse_all(mixes):
    ti, si = iotas((W, W))
    eye = jnp.where(ti == si, 1.0, 0.0)
    below = jnp.logical_and((ti >> 1) == (si >> 1), ti > si)
    done = [eye - jnp.where(below, a, 0.0) for a in mixes]
    for shift in range(1, 7):
        below = jnp.logical_and((ti >> (shift + 1)) == (si >> (shift + 1)), (ti >> shift) > (si >> shift))
        parts = [jnp.where(below, a, 0.0) for a in mixes]
        inner = [mm3(p, d) for p, d in zip(parts, done)]
        done = [d - mm3(d, i) for d, i in zip(done, inner)]
    return done


def head_columns(head0):
    return pl.ds(pl.multiple_of(head0 * W, GROUP * W), GROUP * W)


def give_kernel(
    place_ref, side_ref, len_hbm, x_hbm, go_hbm, wb_hbm, dec_hbm, wk_hbm, wq_hbm, wo_hbm, wv_hbm, *refs
):
    outs, refs = refs[:2], refs[2:]
    x_ref, go_ref, beta_ref, run_ref, rows_ref, keep_ref, first_ref, wkq_ref, wv_ref, wkq2_ref = refs[:10]
    len_ref, wb_ref, dec_ref, wo_ref, sems = refs[10:]
    keep0 = (place_ref[0] & 1) * GROUP
    head0 = GROUP - keep0
    base = place_ref[0] * W
    at = head_columns(head0)
    at2 = head_columns(keep0)
    pairs = (
        (wk_hbm.at[:, at], wkq_ref.at[0]), (x_hbm, x_ref), (len_hbm, len_ref), (dec_hbm, dec_ref), (wb_hbm, wb_ref),
        (wq_hbm.at[:, at], wkq_ref.at[1]), (wv_hbm.at[:, at], wv_ref), (go_hbm, go_ref), (wo_hbm.at[at, :], wo_ref),
        (wk_hbm.at[:, at2], wkq2_ref.at[0]), (wq_hbm.at[:, at2], wkq2_ref.at[1]),
    )
    gets = [pltpu.make_async_copy(src, dst, sems.at[j]) for j, (src, dst) in enumerate(pairs)]
    for get in gets:
        get.start()
    gets[2].wait()
    ti, si = iotas((W, W))
    begin = jnp.int32(0)
    seg_t = jnp.zeros((W, 1), jnp.int32)
    seg_s = jnp.zeros((1, W), jnp.int32)
    seg_in = jnp.int32(0)
    for j in range(len_ref.shape[0]):
        seg_t = seg_t + (ti[:, :1] + base >= begin).astype(jnp.int32)
        seg_s = seg_s + (si[:1, :] + base >= begin).astype(jnp.int32)
        seg_in = seg_in + (base - 1 >= begin).astype(jnp.int32)
        begin = begin + len_ref[j]
    keep_ref[...] = jnp.where(jnp.logical_and(seg_t == seg_s, ti >= si), 1.0, 0.0)
    first_ref[...] = jnp.broadcast_to(jnp.where(seg_t == seg_in, 1.0, 0.0), first_ref.shape)
    gets[3].wait()
    tril = jnp.where(ti >= si, 1.0, 0.0)
    run_ref[...] = exact(tril, dec_ref[...], NT)
    rows_ref[...] = exact(dec_ref[...], tril, NT)
    gets[4].wait()
    gets[1].wait()
    beta_ref[...] = 1.0 / (1.0 + jnp.exp(-dot(x_ref[...], wb_ref[...], NT)))
    block_body(
        head0, x_ref, go_ref, beta_ref, run_ref, rows_ref, keep_ref, first_ref, wkq_ref, wv_ref, wo_ref,
        (gets[0], gets[5], gets[6], gets[7], gets[8]), outs,
    )
    gets[9].wait()
    gets[10].wait()


def keep_kernel(
    place_ref, x_ref, go_ref, beta_ref, run_ref, rows_ref, keep_ref, first_ref, wkq_ref, wo_hbm, wv_hbm, *refs
):
    outs = refs[:2]
    wv_ref, wo_ref, sems = refs[2:]
    head0 = (place_ref[0] & 1) * GROUP
    at = head_columns(head0)
    get_v = pltpu.make_async_copy(wv_hbm.at[:, at], wv_ref, sems.at[0])
    get_o = pltpu.make_async_copy(wo_hbm.at[at, :], wo_ref, sems.at[1])
    get_v.start()
    get_o.start()
    block_body(
        head0, x_ref, go_ref, beta_ref, run_ref, rows_ref, keep_ref, first_ref, wkq_ref, wv_ref, wo_ref,
        (None, None, get_v, None, get_o), outs,
    )


def block_body(
    head0, x_ref, go_ref, beta_ref, run_ref, rows_ref, keep_ref, first_ref, wkq_ref, wv_ref, wo_ref, gets, outs
):
    send_ref, kept_ref = outs

    def ready(*which):
        for j in which:
            if gets[j] is not None:
                gets[j].wait()

    ti, si = iotas((W, W))
    strict = ti > si
    keep = keep_ref[...] > 0.0
    first = first_ref[...][:, :1] > 0.0
    beta_all, run_all, run_rows = beta_ref[...], run_ref[...], rows_ref[...]
    heads = range(GROUP)
    cut = lambda a, i: a[:, i * W:(i + 1) * W]
    ready(0)
    x = x_ref[...]
    raw_k = dot(x, wkq_ref[0])
    ready(1)
    raw_q = dot(x, wkq_ref[1])
    ks, qs, betas, carries, wkks, mixes, pmats = [], [], [], [], [], [], []
    for i in heads:
        head = head0 + i
        rk = cut(raw_k, i)
        rq = cut(raw_q, i)
        inv_k = lax.rsqrt(jnp.sum(rk * rk, axis=1, keepdims=True) + 1e-06)
        inv_q = lax.rsqrt(jnp.sum(rq * rq, axis=1, keepdims=True) + 1e-06)
        k = rk * inv_k
        q = rq * inv_q * (W ** -0.5)
        beta = column(beta_all, head)
        run = column(run_all, head)
        heads_at = lax.broadcasted_iota(jnp.int32, run_rows.shape, 0)
        spread = run - jnp.sum(jnp.where(heads_at == head, run_rows, 0.0), axis=0, keepdims=True)
        weight = jnp.where(keep, jnp.exp(jnp.where(keep, spread, 0.0)), 0.0)
        carried = jnp.where(first, jnp.exp(run), 0.0)
        both = mm3(jnp.concatenate([k, q], axis=0), k, NT)
        wkk = jnp.where(strict, weight, 0.0) * both[:W]
        pmat = weight * both[W:]
        ks.append(k)
        qs.append(q)
        betas.append(beta)
        carries.append(carried)
        wkks.append(wkk)
        mixes.append(wkk * beta)
        pmats.append(pmat)
        lanes = si
        closing = jnp.sum(jnp.where(ti == si, jnp.broadcast_to(weight[W - 1:W, :], (W, W)), 0.0), axis=1, keepdims=True)
        col = jnp.where(lanes == 0, beta, jnp.where(lanes == 1, carried, jnp.where(lanes == 2, closing, jnp.where(lanes == 3, inv_k, inv_q))))
        kept_ref[i, 10] = col
        kept_ref[i, 0] = k
        kept_ref[i, 1] = q
        kept_ref[i, 4] = pmat
        kept_ref[i, 6] = wkk
        kept_ref[i, 7] = weight
    ready(2)
    raw_v = dot(x, wv_ref[...])
    ready(3, 4)
    grad_o = dot(go_ref[...], wo_ref[...], NT)
    solved = inverse_all(mixes)
    for i in heads:
        k, q, beta, carried = ks[i], qs[i], betas[i], carries[i]
        kept_ref[i, 5] = solved[i]
        kept_ref[i, 2] = cut(raw_v, i)
        kept_ref[i, 3] = cut(grad_o, i)
        right = jnp.concatenate([beta * cut(raw_v, i), (beta * carried) * k], axis=1)
        both = mm3(solved[i], right)
        uv = both[:, :W]
        kw = both[:, W:]
        kept_ref[i, 8] = uv
        kept_ref[i, 9] = kw
        eff = carried * q - mm3(pmats[i], kw)
        closing = kept_ref[i, 10][:, 2:3]
        ends = mm3(jnp.concatenate([kw, uv], axis=1), closing * k, TN)
        last = carried[W - 1:W, :]
        send_ref[i, 0] = jnp.where(ti == si, last, 0.0) - ends[:W]
        send_ref[i, 1] = ends[W:]
        send_ref[i, 2] = mm3(cut(grad_o, i), eff, TN)


def join_kernel(place_ref, own_ref, other_ref, *out_refs):
    second = (place_ref[0] & 1) == 1
    x = place_ref[0] >> 1
    for d in range(GROUP):
        i = (x + d) & (GROUP - 1)
        out_ref = out_refs[d]
        ta = jnp.where(second, other_ref[i, 0], own_ref[i, 0])
        tb = jnp.where(second, own_ref[i, 0], other_ref[i, 0])
        oa = jnp.where(second, other_ref[i, 1], own_ref[i, 1])
        ob = jnp.where(second, own_ref[i, 1], other_ref[i, 1])
        ga = jnp.where(second, other_ref[i, 2], own_ref[i, 2])
        gb = jnp.where(second, own_ref[i, 2], other_ref[i, 2])
        front = mm3(jnp.concatenate([ta, oa], axis=0), tb)
        out_ref[0] = front[:W]
        out_ref[1] = front[W:] + ob
        out_ref[2] = mm3(gb, ta, NT) + ga


def row_kernel(place_ref, *refs):
    x = place_ref[0] >> 1
    parts, (r_ref, state_ref, grad_ref) = refs[:GROUP], refs[GROUP:]
    for d, part in enumerate(parts):
        r_ref[(x - d) & (GROUP - 1)] = part[...]
    state = r_ref[0, 1]
    grad = r_ref[GROUP - 1, 2]
    for j in range(1, GROUP):
        state = mm3(state, r_ref[j, 0]) + r_ref[j, 1]
        b = GROUP - 1 - j
        grad = mm3(grad, r_ref[b, 0], NT) + r_ref[b, 2]
    state_ref[...] = state
    grad_ref[...] = grad


def spread_kernel(size, place_ref, r_ref, s_ref, g_ref, *refs):
    x = place_ref[0] >> 1
    outs, all_ref = refs[:GROUP], refs[GROUP]
    state = jnp.where(place_ref[0] < 2 * GROUP, 0.0, s_ref[...])
    grad = jnp.where(place_ref[0] >= size - 2 * GROUP, 0.0, g_ref[...])
    all_ref[0, 0] = state
    all_ref[GROUP - 1, 1] = grad
    for j in range(1, GROUP):
        state = mm3(state, r_ref[j - 1, 0]) + r_ref[j - 1, 1]
        all_ref[j, 0] = state
        b = GROUP - j
        grad = mm3(grad, r_ref[b, 0], NT) + r_ref[b, 2]
        all_ref[b - 1, 1] = grad
    for d, out in enumerate(outs):
        out[...] = all_ref[(x + d) & (GROUP - 1)]


def part_kernel(place_ref, own_ref, other_ref, *refs):
    chips, (mine_ref, give_ref) = refs[:GROUP], refs[GROUP:]
    second = (place_ref[0] & 1) == 1
    x = place_ref[0] >> 1
    for d, chip_ref in enumerate(chips):
        i = (x - d) & (GROUP - 1)
        ta = jnp.where(second, other_ref[i, 0], own_ref[i, 0])
        tb = jnp.where(second, own_ref[i, 0], other_ref[i, 0])
        oa = jnp.where(second, other_ref[i, 1], own_ref[i, 1])
        gb = jnp.where(second, own_ref[i, 2], other_ref[i, 2])
        s_in, g_end = chip_ref[0], chip_ref[1]
        s_mid = mm3(s_in, ta) + oa
        g_mid = mm3(g_end, tb, NT) + gb
        mine_ref[i, 0] = jnp.where(second, s_mid, s_in)
        mine_ref[i, 1] = jnp.where(second, g_end, g_mid)
        give_ref[i, 0] = jnp.where(second, s_in, s_mid)
        give_ref[i, 1] = jnp.where(second, g_mid, g_end)


def back_project(side, grads, db, wkq_ref, wv_ref, wb_ref, wide):
    at = pl.ds(pl.multiple_of(side * wide, wide), wide)
    n = grads.shape[1] // 3
    piece = dot(grads[:, :n], wkq_ref[1, at, :], NT) + dot(grads[:, n:2 * n], wkq_ref[0, at, :], NT)
    return piece + dot(grads[:, 2 * n:], wv_ref[at, :], NT) + dot(db, wb_ref[:, at])


def chunk_kernel(side_ref, grads_ref, db_ref, before_ref, wb_ref, wkq_ref, wv_ref, out_ref):
    piece = back_project(side_ref[0], grads_ref[...], db_ref[...], wkq_ref, wv_ref, wb_ref, out_ref.shape[1])
    out_ref[...] = before_ref[0] + piece


def second_kernel(chained, *refs):
    place_ref, side_ref, back_ref, kept_ref, wb_ref, wkq_ref, wv_ref = refs[:7]
    refs = refs[7:]
    if chained:
        before_ref, gd_before_ref, *total_refs, gd_ref, grads_ref, db_ref = refs
        wide = total_refs[0].shape[-1]
    else:
        total_ref, gd_ref = refs
        wide = total_ref.shape[-1]
    keep0 = (place_ref[0] & 1) * GROUP
    head0 = GROUP - keep0 if chained else keep0
    side = side_ref[0]
    ti, si = iotas((W, W))
    strict = ti > si
    upper = jnp.where(si >= ti, 1.0, 0.0)
    t8, h8 = iotas((W, 8))
    none = jnp.zeros((W, 8), F32)
    cterm, fterm, eterm, dball = none, none, none, none
    gqs, gks, gvs = [], [], []
    for i in range(GROUP):
        head = head0 + i
        s0, g1 = back_ref[i, 0], back_ref[i, 1]
        k, q, v, do = kept_ref[i, 0], kept_ref[i, 1], kept_ref[i, 2], kept_ref[i, 3]
        pmat, wkk, weight = kept_ref[i, 4], kept_ref[i, 6], kept_ref[i, 7]
        col = kept_ref[i, 10]
        beta, carried, closing, inv_k, inv_q = (col[:, j:j + 1] for j in range(5))
        u = kept_ref[i, 8] - mm3(kept_ref[i, 9], s0, NT)
        du = mm3(pmat, do, TN) + mm3(closing * k, g1, NT)
        dr = mm3(kept_ref[i, 5], du, TN)
        dpa = mm3(jnp.concatenate([do, dr], axis=0), u, NT)
        dp = dpa[:W]
        da = -dpa[W:]
        ds = mm3(jnp.concatenate([carried * do, dr], axis=0), s0)
        dq_state = ds[:W]
        dr_s = carried * ds[W:]
        ug = closing * mm3(u, g1)
        dqk = weight * dp
        dkk = jnp.where(strict, weight, 0.0) * da * beta
        front = mm3(jnp.concatenate([dqk, dkk], axis=0), k)
        dq = front[:W] + dq_state
        dk = front[W:] + mm3(jnp.concatenate([dkk, dqk], axis=0), jnp.concatenate([k, q], axis=0), TN)
        dk = dk - beta * dr_s + ug
        known = jnp.sum(dr_s * k, axis=1, keepdims=True)
        dbeta = jnp.sum(dr * v, axis=1, keepdims=True) - known + jnp.sum(da * wkk, axis=1, keepdims=True)
        dlogit = dbeta * beta * (1.0 - beta)
        pairs = dp * pmat + da * wkk * beta
        ph, plow = halves(pairs)
        ub = upper.astype(BF16)
        across = dot(ub, ph) + dot(ub, plow)
        evec = jnp.sum(jnp.where(strict, across, 0.0), axis=1, keepdims=True)
        fvec = jnp.sum(ug * k, axis=1, keepdims=True)
        cvec = jnp.sum(dq_state * q, axis=1, keepdims=True) - beta * known
        ends = carried[W - 1:W, :] * jnp.sum(jnp.sum(g1 * s0, axis=1, keepdims=True), axis=0, keepdims=True)
        cvec = cvec + jnp.where(t8[:, :1] == W - 1, ends, 0.0)
        here = h8 == head
        cterm = jnp.where(here, cvec, cterm)
        fterm = jnp.where(here, fvec, fterm)
        eterm = jnp.where(here, evec, eterm)
        dball = jnp.where(here, dlogit, dball)
        gk = inv_k * (dk - k * jnp.sum(k * dk, axis=1, keepdims=True))
        gq = (inv_q * (W ** -0.5)) * (dq - (q * float(W)) * jnp.sum(q * dq, axis=1, keepdims=True))
        gqs.append(gq.astype(BF16))
        gks.append(gk.astype(BF16))
        gvs.append((beta * dr).astype(BF16))
    grads = jnp.concatenate(gqs + gks + gvs, axis=1)
    db = dball.astype(BF16)
    project = lambda d: back_project((side + d) & (SIDES - 1), grads, db, wkq_ref, wv_ref, wb_ref, wide)
    if chained:
        for d, total_ref in zip(ORDER, total_refs):
            total_ref[...] = before_ref[d] + project(d)
        grads_ref[...] = grads
        db_ref[...] = db
    else:
        for d in range(SIDES):
            total_ref[d] = project(d)
    lower = jnp.where(strict, 1.0, 0.0)
    eye = jnp.where(ti == si, 1.0, 0.0)
    turn = (((0,), (1,)), ((), ()))
    decays = exact(cterm, upper, turn) + exact(fterm, lower, turn) + exact(eterm, eye, turn)
    gd_ref[...] = gd_before_ref[...] + decays if chained else decays


SMEM = pl.BlockSpec(memory_space=pltpu.SMEM)
VMEM = pl.BlockSpec(memory_space=pltpu.VMEM)
HBM = pl.BlockSpec(memory_space=pltpu.HBM)


def shape(*dims):
    return jax.ShapeDtypeStruct(dims, F32)


def in_hbm(*arrays):
    return [pltpu.with_memory_space_constraint(a, pltpu.HBM) for a in arrays]


def block_shapes():
    return [shape(GROUP, 3, W, W), shape(GROUP, 11, W, W)]


def run_give(place, side, lengths, inputs, grad_out, beta_t, decay_t, w_key, w_query, w_out, w_value):
    rows, width = inputs.shape
    heads, span = beta_t.shape[0], GROUP * W
    wide = jax.ShapeDtypeStruct((rows, width), BF16)
    tall = jax.ShapeDtypeStruct((width, span), BF16)
    two = jax.ShapeDtypeStruct((2, width, span), BF16)
    out = pl.pallas_call(
        give_kernel,
        in_specs=[SMEM] * 2 + [HBM] * 9,
        out_specs=[VMEM] * 12,
        out_shape=block_shapes() + [wide, wide, shape(rows, heads), shape(rows, heads), shape(heads, rows), shape(W, W), shape(W, heads)] + [two, tall, two],
        scratch_shapes=[
            pltpu.SMEM(lengths.shape, jnp.int32), pltpu.VMEM(beta_t.shape, BF16), pltpu.VMEM(decay_t.shape, F32),
            pltpu.VMEM((span, width), BF16), pltpu.SemaphoreType.DMA((11,)),
        ],
        compiler_params=pltpu.CompilerParams(vmem_limit_bytes=28 << 20),
        name="block_forward_give",
    )(place, side, *in_hbm(lengths, inputs, grad_out, beta_t, decay_t, w_key, w_query, w_out, w_value))
    return out[0], out[1], out[2:9], out[9:11], out[11]


def run_keep(place, shared, w_keep, w_out, w_value):
    _, width, span = w_keep.shape
    out = pl.pallas_call(
        keep_kernel,
        in_specs=[SMEM] + [VMEM] * 8 + [HBM] * 2,
        out_specs=[VMEM] * 3,
        out_shape=block_shapes() + [jax.ShapeDtypeStruct((width, span), BF16)],
        scratch_shapes=[pltpu.VMEM((span, width), BF16), pltpu.SemaphoreType.DMA((2,))],
        compiler_params=pltpu.CompilerParams(vmem_limit_bytes=24 << 20),
        name="block_forward_keep",
    )(place, *shared, w_keep, *in_hbm(w_out, w_value))
    return out


def run_backward(place, side, back, kept, beta_t, w_both, w_value, before):
    heads, width = beta_t.shape
    wide = width // SIDES
    if before:
        out_shape = [shape(W, wide)] * 3 + [shape(heads, W), jax.ShapeDtypeStruct((W, 3 * GROUP * W), BF16), jax.ShapeDtypeStruct((W, heads), BF16)]
    else:
        out_shape = [shape(SIDES, W, wide), shape(heads, W)]
    return pl.pallas_call(
        partial(second_kernel, bool(before)),
        in_specs=[SMEM] * 2 + [VMEM] * 5 + [VMEM] * len(before),
        out_specs=[VMEM] * len(out_shape),
        out_shape=out_shape,
        compiler_params=pltpu.CompilerParams(vmem_limit_bytes=24 << 20),
        name="block_backward",
    )(place, side, back, kept, beta_t, w_both, w_value, *before)


def run_chunk(side, grads, db, before, beta_t, w_both, w_value):
    return pl.pallas_call(
        chunk_kernel,
        in_specs=[SMEM] + [VMEM] * 6,
        out_specs=VMEM,
        out_shape=shape(*before.shape[1:]),
        compiler_params=pltpu.CompilerParams(vmem_limit_bytes=16 << 20),
        name="own_chunk",
    )(side, grads, db, before, beta_t, w_both, w_value)


def per_device(inputs, grad_out, w_query, w_key, w_value, w_beta, w_out, log_decay, lengths):
    size = lax.axis_size("ctx")
    place = lax.axis_index("ctx").astype(jnp.int32).reshape(1)
    side = lax.axis_index("head").astype(jnp.int32).reshape(1)
    beta_t, decay_t = w_beta.T, log_decay.T
    small = pltpu.CompilerParams(vmem_limit_bytes=8 << 20)

    pair = [(j, j ^ 1) for j in range(size)]
    give, give_kept, shared, give_w, keep_w = run_give(
        place, side, lengths, inputs, grad_out, beta_t, decay_t, w_key, w_query, w_out, w_value
    )
    other = lax.ppermute(give, "ctx", pair)
    own, own_kept, keep_v = run_keep(place, shared, keep_w, w_out, w_value)
    row = 2 * GROUP

    def call(kernel, name, scalars, arrays, out_shape, scratch=()):
        return pl.pallas_call(
            kernel,
            in_specs=[SMEM] * len(scalars) + [VMEM] * len(arrays),
            out_specs=[VMEM] * len(out_shape),
            out_shape=out_shape,
            scratch_shapes=list(scratch),
            compiler_params=small,
            name=name,
        )(*scalars, *arrays)

    def along_x(parts):
        got = {0: parts[0]}
        for d in (2, 1, 3):
            moves = [(j, j - j % row + (j + 2 * d) % row) for j in range(size)]
            got[d] = lax.ppermute(parts[d], "ctx", moves)
        return [got[d] for d in range(GROUP)]

    whole = call(join_kernel, "chip_join", (place,), (own, other), [shape(3, W, W)] * GROUP)
    mine, state, grad = call(
        row_kernel, "row_ends", (place,), along_x(whole), [shape(GROUP, 3, W, W), shape(W, W), shape(W, W)]
    )
    state = lax.ppermute(state, "ctx", [(j, (j + row) % size) for j in range(size)])
    grad = lax.ppermute(grad, "ctx", [((j + row) % size, j) for j in range(size)])
    spread = call(
        partial(spread_kernel, size), "row_states", (place,), (mine, state, grad), [shape(2, W, W)] * GROUP, [pltpu.VMEM((GROUP, 2, W, W), F32)]
    )
    own_back, give_back = call(
        part_kernel, "chip_part", (place,), (own, other, *along_x(spread)), [shape(GROUP, 2, W, W)] * 2
    )
    other_back = lax.ppermute(give_back, "ctx", pair)
    before = run_backward(place, side, own_back, own_kept, beta_t, keep_w, keep_v, ())
    *chunks, grad_d, grads, db = run_backward(place, side, other_back, give_kept, beta_t, *give_w, before)
    total = run_chunk(side, grads, db, before[0], beta_t, *give_w)
    for d, chunk in zip(ORDER, chunks):
        total = total + lax.ppermute(chunk, "head", [(j, (j + d) % SIDES) for j in range(SIDES)])
    return (total.astype(BF16), grad_d.T)


def solution(mesh):
    placed = (
        P("ctx", None),
        P("ctx", None),
        P(None, "head"),
        P(None, "head"),
        P(None, "head"),
        P(None, "head"),
        P("head", None),
        P("ctx", "head"),
        P(),
    )
    return jax.shard_map(
        per_device,
        mesh=mesh,
        in_specs=placed,
        out_specs=(P("ctx", "head"), P("ctx", "head")),
        check_vma=False,
    )
```

```python
from functools import partial

import jax
import jax.numpy as jnp
from jax import lax
from jax.experimental import pallas as pl
from jax.experimental.pallas import tpu as pltpu
from jax.sharding import PartitionSpec as P

F32 = jnp.float32
BF16 = jnp.bfloat16
W = 128
GROUP = 4
SIDES = 4
ORDER = (2, 1, 3)
NN = (((1,), (0,)), ((), ()))
NT = (((1,), (1,)), ((), ()))
TN = (((0,), (0,)), ((), ()))


def dot(a, b, dims=NN):
    return lax.dot_general(a, b, dims, preferred_element_type=F32)


def exact(a, b, dims=NN):
    return lax.dot_general(a, b, dims, precision=lax.Precision.HIGHEST, preferred_element_type=F32)


def halves(a):
    high = a.astype(BF16)
    return high, (a - high.astype(F32)).astype(BF16)


def mm3(a, b, dims=NN):
    ah, al = halves(a)
    bh, bl = halves(b)
    (ca,), (cb,) = dims[0]
    return dot(jnp.concatenate([ah, al], axis=ca), jnp.concatenate([bh, bh], axis=cb), dims) + dot(ah, bl, dims)


def iotas(shape):
    return lax.broadcasted_iota(jnp.int32, shape, 0), lax.broadcasted_iota(jnp.int32, shape, 1)


def column(array, index):
    lanes = lax.broadcasted_iota(jnp.int32, array.shape, 1)
    return jnp.sum(jnp.where(lanes == index, array, 0.0), axis=1, keepdims=True)


def inverse_all(mixes):
    ti, si = iotas((W, W))
    eye = jnp.where(ti == si, 1.0, 0.0)
    below = jnp.logical_and((ti >> 1) == (si >> 1), ti > si)
    done = [eye - jnp.where(below, a, 0.0) for a in mixes]
    for shift in range(1, 7):
        below = jnp.logical_and((ti >> (shift + 1)) == (si >> (shift + 1)), (ti >> shift) > (si >> shift))
        parts = [jnp.where(below, a, 0.0) for a in mixes]
        inner = [mm3(p, d) for p, d in zip(parts, done)]
        done = [d - mm3(d, i) for d, i in zip(done, inner)]
    return done


def head_columns(head0):
    return pl.ds(pl.multiple_of(head0 * W, GROUP * W), GROUP * W)


def give_kernel(
    place_ref, side_ref, len_hbm, x_hbm, go_hbm, wb_hbm, dec_hbm, wk_hbm, wq_hbm, wo_hbm, wv_hbm, *refs
):
    outs, refs = refs[:2], refs[2:]
    x_ref, go_ref, beta_ref, run_ref, rows_ref, keep_ref, first_ref, wkq_ref, wv_ref, wkq2_ref = refs[:10]
    len_ref, wb_ref, dec_ref, wo_ref, sems = refs[10:]
    keep0 = (place_ref[0] & 1) * GROUP
    head0 = GROUP - keep0
    base = place_ref[0] * W
    at = head_columns(head0)
    at2 = head_columns(keep0)
    pairs = (
        (wk_hbm.at[:, at], wkq_ref.at[0]), (x_hbm, x_ref), (len_hbm, len_ref), (dec_hbm, dec_ref), (wb_hbm, wb_ref),
        (wq_hbm.at[:, at], wkq_ref.at[1]), (wv_hbm.at[:, at], wv_ref), (go_hbm, go_ref), (wo_hbm.at[at, :], wo_ref),
        (wk_hbm.at[:, at2], wkq2_ref.at[0]), (wq_hbm.at[:, at2], wkq2_ref.at[1]),
    )
    gets = [pltpu.make_async_copy(src, dst, sems.at[j]) for j, (src, dst) in enumerate(pairs)]
    for get in (gets[2], gets[3], gets[4], gets[1], gets[0], gets[5], gets[6], gets[7], gets[8], gets[9], gets[10]):
        get.start()
    gets[2].wait()
    ti, si = iotas((W, W))
    begin = jnp.int32(0)
    seg_t = jnp.zeros((W, 1), jnp.int32)
    seg_s = jnp.zeros((1, W), jnp.int32)
    seg_in = jnp.int32(0)
    for j in range(len_ref.shape[0]):
        seg_t = seg_t + (ti[:, :1] + base >= begin).astype(jnp.int32)
        seg_s = seg_s + (si[:1, :] + base >= begin).astype(jnp.int32)
        seg_in = seg_in + (base - 1 >= begin).astype(jnp.int32)
        begin = begin + len_ref[j]
    keep_ref[...] = jnp.where(jnp.logical_and(seg_t == seg_s, ti >= si), 1.0, 0.0)
    lane = iotas(first_ref.shape)[1]
    marked = jnp.where(lane == 0, seg_in, seg_t[W - 1:W, :])
    first_ref[...] = jnp.where(seg_t == marked, 1.0, 0.0)
    gets[3].wait()
    tril = jnp.where(ti >= si, 1.0, 0.0)
    run_ref[...] = exact(tril, dec_ref[...], NT)
    rows_ref[...] = exact(dec_ref[...], tril, NT)
    gets[4].wait()
    gets[1].wait()
    beta_ref[...] = 1.0 / (1.0 + jnp.exp(-dot(x_ref[...], wb_ref[...], NT)))
    block_body(
        head0, x_ref, go_ref, beta_ref, run_ref, rows_ref, keep_ref, first_ref, wkq_ref, wv_ref, wo_ref,
        (gets[0], gets[5], gets[6], gets[7], gets[8]), outs,
    )
    gets[9].wait()
    gets[10].wait()


def keep_kernel(
    place_ref, x_ref, go_ref, beta_ref, run_ref, rows_ref, keep_ref, first_ref, wkq_ref, wo_hbm, wv_hbm, *refs
):
    outs = refs[:2]
    wv_ref, wo_ref, sems = refs[2:]
    head0 = (place_ref[0] & 1) * GROUP
    at = head_columns(head0)
    get_v = pltpu.make_async_copy(wv_hbm.at[:, at], wv_ref, sems.at[0])
    get_o = pltpu.make_async_copy(wo_hbm.at[at, :], wo_ref, sems.at[1])
    get_v.start()
    get_o.start()
    block_body(
        head0, x_ref, go_ref, beta_ref, run_ref, rows_ref, keep_ref, first_ref, wkq_ref, wv_ref, wo_ref,
        (None, None, get_v, None, get_o), outs,
    )


def block_body(
    head0, x_ref, go_ref, beta_ref, run_ref, rows_ref, keep_ref, first_ref, wkq_ref, wv_ref, wo_ref, gets, outs
):
    send_ref, kept_ref = outs

    def ready(*which):
        for j in which:
            if gets[j] is not None:
                gets[j].wait()

    ti, si = iotas((W, W))
    strict = ti > si
    keep = keep_ref[...] > 0.0
    first = first_ref[...][:, :1] > 0.0
    final = first_ref[...][:, 1:2] > 0.0
    beta_all, run_all, run_rows = beta_ref[...], run_ref[...], rows_ref[...]
    heads = range(GROUP)
    cut = lambda a, i: a[:, i * W:(i + 1) * W]
    ready(0)
    x = x_ref[...]
    raw_k = dot(x, wkq_ref[0])
    ready(1)
    raw_q = dot(x, wkq_ref[1])
    ks, qs, betas, carries, wkks, mixes, pmats = [], [], [], [], [], [], []
    for i in heads:
        head = head0 + i
        rk = cut(raw_k, i)
        rq = cut(raw_q, i)
        inv_k = lax.rsqrt(jnp.sum(rk * rk, axis=1, keepdims=True) + 1e-06)
        inv_q = lax.rsqrt(jnp.sum(rq * rq, axis=1, keepdims=True) + 1e-06)
        k = rk * inv_k
        q = rq * inv_q * (W ** -0.5)
        beta = column(beta_all, head)
        run = column(run_all, head)
        heads_at = lax.broadcasted_iota(jnp.int32, run_rows.shape, 0)
        spread = run - jnp.sum(jnp.where(heads_at == head, run_rows, 0.0), axis=0, keepdims=True)
        weight = jnp.where(keep, jnp.exp(jnp.where(keep, spread, 0.0)), 0.0)
        carried = jnp.where(first, jnp.exp(run), 0.0)
        both = mm3(jnp.concatenate([k, q], axis=0), k, NT)
        wkk = jnp.where(strict, weight, 0.0) * both[:W]
        pmat = weight * both[W:]
        ks.append(k)
        qs.append(q)
        betas.append(beta)
        carries.append(carried)
        wkks.append(wkk)
        mixes.append(wkk * beta)
        pmats.append(pmat)
        lanes = si
        closing = jnp.where(final, jnp.exp(jnp.where(final, run[W - 1:W, :] - run, 0.0)), 0.0)
        col = jnp.where(lanes == 0, beta, jnp.where(lanes == 1, carried, jnp.where(lanes == 2, closing, jnp.where(lanes == 3, inv_k, inv_q))))
        kept_ref[i, 10] = col
        kept_ref[i, 0] = k
        kept_ref[i, 1] = q
        kept_ref[i, 4] = pmat
        kept_ref[i, 6] = wkk
        kept_ref[i, 7] = weight
    solved = inverse_all(mixes)
    ready(2)
    raw_v = dot(x, wv_ref[...])
    ready(3, 4)
    grad_o = dot(go_ref[...], wo_ref[...], NT)
    for i in heads:
        k, q, beta, carried = ks[i], qs[i], betas[i], carries[i]
        kept_ref[i, 5] = solved[i]
        kept_ref[i, 2] = cut(raw_v, i)
        kept_ref[i, 3] = cut(grad_o, i)
        right = jnp.concatenate([beta * cut(raw_v, i), (beta * carried) * k], axis=1)
        both = mm3(solved[i], right)
        uv = both[:, :W]
        kw = both[:, W:]
        kept_ref[i, 8] = uv
        kept_ref[i, 9] = kw
        eff = carried * q - mm3(pmats[i], kw)
        closing = kept_ref[i, 10][:, 2:3]
        ends = mm3(jnp.concatenate([kw, uv], axis=1), closing * k, TN)
        last = carried[W - 1:W, :]
        send_ref[i, 0] = jnp.where(ti == si, last, 0.0) - ends[:W]
        send_ref[i, 1] = ends[W:]
        send_ref[i, 2] = mm3(cut(grad_o, i), eff, TN)


def join_kernel(place_ref, own_ref, other_ref, *out_refs):
    second = (place_ref[0] & 1) == 1
    x = place_ref[0] >> 1
    for d in range(GROUP):
        i = (x + d) & (GROUP - 1)
        out_ref = out_refs[d]
        ta = jnp.where(second, other_ref[i, 0], own_ref[i, 0])
        tb = jnp.where(second, own_ref[i, 0], other_ref[i, 0])
        oa = jnp.where(second, other_ref[i, 1], own_ref[i, 1])
        ob = jnp.where(second, own_ref[i, 1], other_ref[i, 1])
        ga = jnp.where(second, other_ref[i, 2], own_ref[i, 2])
        gb = jnp.where(second, own_ref[i, 2], other_ref[i, 2])
        front = mm3(jnp.concatenate([ta, oa], axis=0), tb)
        out_ref[0] = front[:W]
        out_ref[1] = front[W:] + ob
        out_ref[2] = mm3(gb, ta, NT) + ga


def row_kernel(place_ref, *refs):
    x = place_ref[0] >> 1
    parts, (r_ref, state_ref, grad_ref) = refs[:GROUP], refs[GROUP:]
    for d, part in enumerate(parts):
        r_ref[(x - d) & (GROUP - 1)] = part[...]
    state = r_ref[0, 1]
    grad = r_ref[GROUP - 1, 2]
    for j in range(1, GROUP):
        state = mm3(state, r_ref[j, 0]) + r_ref[j, 1]
        b = GROUP - 1 - j
        grad = mm3(grad, r_ref[b, 0], NT) + r_ref[b, 2]
    state_ref[...] = state
    grad_ref[...] = grad


def spread_kernel(size, place_ref, r_ref, s_ref, g_ref, *refs):
    x = place_ref[0] >> 1
    outs, all_ref = refs[:GROUP], refs[GROUP]
    state = jnp.where(place_ref[0] < 2 * GROUP, 0.0, s_ref[...])
    grad = jnp.where(place_ref[0] >= size - 2 * GROUP, 0.0, g_ref[...])
    all_ref[0, 0] = state
    all_ref[GROUP - 1, 1] = grad
    for j in range(1, GROUP):
        state = mm3(state, r_ref[j - 1, 0]) + r_ref[j - 1, 1]
        all_ref[j, 0] = state
        b = GROUP - j
        grad = mm3(grad, r_ref[b, 0], NT) + r_ref[b, 2]
        all_ref[b - 1, 1] = grad
    for d, out in enumerate(outs):
        out[...] = all_ref[(x + d) & (GROUP - 1)]


def part_kernel(place_ref, own_ref, other_ref, *refs):
    chips, (mine_ref, give_ref) = refs[:GROUP], refs[GROUP:]
    second = (place_ref[0] & 1) == 1
    x = place_ref[0] >> 1
    for d, chip_ref in enumerate(chips):
        i = (x - d) & (GROUP - 1)
        ta = jnp.where(second, other_ref[i, 0], own_ref[i, 0])
        tb = jnp.where(second, own_ref[i, 0], other_ref[i, 0])
        oa = jnp.where(second, other_ref[i, 1], own_ref[i, 1])
        gb = jnp.where(second, own_ref[i, 2], other_ref[i, 2])
        s_in, g_end = chip_ref[0], chip_ref[1]
        s_mid = mm3(s_in, ta) + oa
        g_mid = mm3(g_end, tb, NT) + gb
        mine_ref[i, 0] = jnp.where(second, s_mid, s_in)
        mine_ref[i, 1] = jnp.where(second, g_end, g_mid)
        give_ref[i, 0] = jnp.where(second, s_in, s_mid)
        give_ref[i, 1] = jnp.where(second, g_mid, g_end)


def back_project(side, grads, db, wkq_ref, wv_ref, wb_ref, wide):
    at = pl.ds(pl.multiple_of(side * wide, wide), wide)
    n = grads.shape[1] // 3
    piece = dot(grads[:, :n], wkq_ref[1, at, :], NT) + dot(grads[:, n:2 * n], wkq_ref[0, at, :], NT)
    return piece + dot(grads[:, 2 * n:], wv_ref[at, :], NT) + dot(db, wb_ref[:, at])


def chunk_kernel(side_ref, grads_ref, db_ref, before_ref, wb_ref, wkq_ref, wv_ref, out_ref):
    piece = back_project(side_ref[0], grads_ref[...], db_ref[...], wkq_ref, wv_ref, wb_ref, out_ref.shape[1])
    out_ref[...] = before_ref[0] + piece


def second_kernel(chained, *refs):
    place_ref, side_ref, back_ref, kept_ref, wb_ref, wkq_ref, wv_ref = refs[:7]
    refs = refs[7:]
    if chained:
        before_ref, gd_before_ref, *total_refs, gd_ref, grads_ref, db_ref = refs
        wide = total_refs[0].shape[-1]
    else:
        total_ref, gd_ref = refs
        wide = total_ref.shape[-1]
    keep0 = (place_ref[0] & 1) * GROUP
    head0 = GROUP - keep0 if chained else keep0
    side = side_ref[0]
    ti, si = iotas((W, W))
    strict = ti > si
    upper = jnp.where(si >= ti, 1.0, 0.0)
    t8, h8 = iotas((W, 8))
    none = jnp.zeros((W, 8), F32)
    cterm, fterm, eterm, dball = none, none, none, none
    gqs, gks, gvs = [], [], []
    for i in range(GROUP):
        head = head0 + i
        s0, g1 = back_ref[i, 0], back_ref[i, 1]
        k, q, v, do = kept_ref[i, 0], kept_ref[i, 1], kept_ref[i, 2], kept_ref[i, 3]
        pmat, wkk, weight = kept_ref[i, 4], kept_ref[i, 6], kept_ref[i, 7]
        col = kept_ref[i, 10]
        beta, carried, closing, inv_k, inv_q = (col[:, j:j + 1] for j in range(5))
        u = kept_ref[i, 8] - mm3(kept_ref[i, 9], s0, NT)
        du = mm3(pmat, do, TN) + mm3(closing * k, g1, NT)
        dr = mm3(kept_ref[i, 5], du, TN)
        dpa = mm3(jnp.concatenate([do, dr], axis=0), u, NT)
        dp = dpa[:W]
        da = -dpa[W:]
        ds = mm3(jnp.concatenate([carried * do, dr], axis=0), s0)
        dq_state = ds[:W]
        dr_s = carried * ds[W:]
        ug = closing * mm3(u, g1)
        dqk = weight * dp
        dkk = jnp.where(strict, weight, 0.0) * da * beta
        front = mm3(jnp.concatenate([dqk, dkk], axis=0), k)
        dq = front[:W] + dq_state
        dk = front[W:] + mm3(jnp.concatenate([dkk, dqk], axis=0), jnp.concatenate([k, q], axis=0), TN)
        dk = dk - beta * dr_s + ug
        known = jnp.sum(dr_s * k, axis=1, keepdims=True)
        dbeta = jnp.sum(dr * v, axis=1, keepdims=True) - known + jnp.sum(da * wkk, axis=1, keepdims=True)
        dlogit = dbeta * beta * (1.0 - beta)
        pairs = dp * pmat + da * wkk * beta
        ph, plow = halves(pairs)
        ub = upper.astype(BF16)
        across = dot(ub, ph) + dot(ub, plow)
        evec = jnp.sum(jnp.where(strict, across, 0.0), axis=1, keepdims=True)
        fvec = jnp.sum(ug * k, axis=1, keepdims=True)
        cvec = jnp.sum(dq_state * q, axis=1, keepdims=True) - beta * known
        ends = carried[W - 1:W, :] * jnp.sum(jnp.sum(g1 * s0, axis=1, keepdims=True), axis=0, keepdims=True)
        cvec = cvec + jnp.where(t8[:, :1] == W - 1, ends, 0.0)
        here = h8 == head
        cterm = jnp.where(here, cvec, cterm)
        fterm = jnp.where(here, fvec, fterm)
        eterm = jnp.where(here, evec, eterm)
        dball = jnp.where(here, dlogit, dball)
        gk = inv_k * (dk - k * jnp.sum(k * dk, axis=1, keepdims=True))
        gq = (inv_q * (W ** -0.5)) * (dq - (q * float(W)) * jnp.sum(q * dq, axis=1, keepdims=True))
        gqs.append(gq.astype(BF16))
        gks.append(gk.astype(BF16))
        gvs.append((beta * dr).astype(BF16))
    grads = jnp.concatenate(gqs + gks + gvs, axis=1)
    db = dball.astype(BF16)
    project = lambda d: back_project((side + d) & (SIDES - 1), grads, db, wkq_ref, wv_ref, wb_ref, wide)
    if chained:
        for d, total_ref in zip(ORDER, total_refs):
            total_ref[...] = before_ref[d] + project(d)
        grads_ref[...] = grads
        db_ref[...] = db
    else:
        for d in range(SIDES):
            total_ref[d] = project(d)
    eye = jnp.where(ti == si, 1.0, 0.0)
    terms = jnp.concatenate([cterm, fterm, eterm], axis=0)
    top = terms.astype(BF16)
    middle, bottom = halves(terms - top.astype(F32))
    sums = dot(jnp.concatenate([top, middle, bottom], axis=1), jnp.concatenate([jnp.where(ti >= si, 1.0, 0.0), jnp.where(si > ti, 1.0, 0.0), eye], axis=0).astype(BF16), TN)
    decays = sums[:8] + sums[8:16] + sums[16:]
    gd_ref[...] = gd_before_ref[...] + decays if chained else decays


SMEM = pl.BlockSpec(memory_space=pltpu.SMEM)
VMEM = pl.BlockSpec(memory_space=pltpu.VMEM)
HBM = pl.BlockSpec(memory_space=pltpu.HBM)


def shape(*dims):
    return jax.ShapeDtypeStruct(dims, F32)


def in_hbm(*arrays):
    return [pltpu.with_memory_space_constraint(a, pltpu.HBM) for a in arrays]


def block_shapes():
    return [shape(GROUP, 3, W, W), shape(GROUP, 11, W, W)]


def run_give(place, side, lengths, inputs, grad_out, beta_t, decay_t, w_key, w_query, w_out, w_value):
    rows, width = inputs.shape
    heads, span = beta_t.shape[0], GROUP * W
    wide = jax.ShapeDtypeStruct((rows, width), BF16)
    tall = jax.ShapeDtypeStruct((width, span), BF16)
    two = jax.ShapeDtypeStruct((2, width, span), BF16)
    out = pl.pallas_call(
        give_kernel,
        in_specs=[SMEM] * 2 + [HBM] * 9,
        out_specs=[VMEM] * 12,
        out_shape=block_shapes() + [wide, wide, shape(rows, heads), shape(rows, heads), shape(heads, rows), shape(W, W), shape(W, heads)] + [two, tall, two],
        scratch_shapes=[
            pltpu.SMEM(lengths.shape, jnp.int32), pltpu.VMEM(beta_t.shape, BF16), pltpu.VMEM(decay_t.shape, F32),
            pltpu.VMEM((span, width), BF16), pltpu.SemaphoreType.DMA((11,)),
        ],
        compiler_params=pltpu.CompilerParams(vmem_limit_bytes=28 << 20),
        name="block_forward_give",
    )(place, side, *in_hbm(lengths, inputs, grad_out, beta_t, decay_t, w_key, w_query, w_out, w_value))
    return out[0], out[1], out[2:9], out[9:11], out[11]


def run_keep(place, shared, w_keep, w_out, w_value):
    _, width, span = w_keep.shape
    out = pl.pallas_call(
        keep_kernel,
        in_specs=[SMEM] + [VMEM] * 8 + [HBM] * 2,
        out_specs=[VMEM] * 3,
        out_shape=block_shapes() + [jax.ShapeDtypeStruct((width, span), BF16)],
        scratch_shapes=[pltpu.VMEM((span, width), BF16), pltpu.SemaphoreType.DMA((2,))],
        compiler_params=pltpu.CompilerParams(vmem_limit_bytes=24 << 20),
        name="block_forward_keep",
    )(place, *shared, w_keep, *in_hbm(w_out, w_value))
    return out


def run_backward(place, side, back, kept, beta_t, w_both, w_value, before):
    heads, width = beta_t.shape
    wide = width // SIDES
    if before:
        out_shape = [shape(W, wide)] * 3 + [shape(heads, W), jax.ShapeDtypeStruct((W, 3 * GROUP * W), BF16), jax.ShapeDtypeStruct((W, heads), BF16)]
    else:
        out_shape = [shape(SIDES, W, wide), shape(heads, W)]
    return pl.pallas_call(
        partial(second_kernel, bool(before)),
        in_specs=[SMEM] * 2 + [VMEM] * 5 + [VMEM] * len(before),
        out_specs=[VMEM] * len(out_shape),
        out_shape=out_shape,
        compiler_params=pltpu.CompilerParams(vmem_limit_bytes=24 << 20),
        name="block_backward",
    )(place, side, back, kept, beta_t, w_both, w_value, *before)


def run_chunk(side, grads, db, before, beta_t, w_both, w_value):
    return pl.pallas_call(
        chunk_kernel,
        in_specs=[SMEM] + [VMEM] * 6,
        out_specs=VMEM,
        out_shape=shape(*before.shape[1:]),
        compiler_params=pltpu.CompilerParams(vmem_limit_bytes=16 << 20),
        name="own_chunk",
    )(side, grads, db, before, beta_t, w_both, w_value)


def per_device(inputs, grad_out, w_query, w_key, w_value, w_beta, w_out, log_decay, lengths):
    size = lax.axis_size("ctx")
    place = lax.axis_index("ctx").astype(jnp.int32).reshape(1)
    side = lax.axis_index("head").astype(jnp.int32).reshape(1)
    beta_t, decay_t = w_beta.T, log_decay.T
    small = pltpu.CompilerParams(vmem_limit_bytes=8 << 20)

    pair = [(j, j ^ 1) for j in range(size)]
    give, give_kept, shared, give_w, keep_w = run_give(
        place, side, lengths, inputs, grad_out, beta_t, decay_t, w_key, w_query, w_out, w_value
    )
    other = lax.ppermute(give, "ctx", pair)
    own, own_kept, keep_v = run_keep(place, shared, keep_w, w_out, w_value)
    row = 2 * GROUP

    def call(kernel, name, scalars, arrays, out_shape, scratch=()):
        return pl.pallas_call(
            kernel,
            in_specs=[SMEM] * len(scalars) + [VMEM] * len(arrays),
            out_specs=[VMEM] * len(out_shape),
            out_shape=out_shape,
            scratch_shapes=list(scratch),
            compiler_params=small,
            name=name,
        )(*scalars, *arrays)

    def along_x(parts):
        got = {0: parts[0]}
        for d in (2, 1, 3):
            moves = [(j, j - j % row + (j + 2 * d) % row) for j in range(size)]
            got[d] = lax.ppermute(parts[d], "ctx", moves)
        return [got[d] for d in range(GROUP)]

    whole = call(join_kernel, "chip_join", (place,), (own, other), [shape(3, W, W)] * GROUP)
    mine, state, grad = call(
        row_kernel, "row_ends", (place,), along_x(whole), [shape(GROUP, 3, W, W), shape(W, W), shape(W, W)]
    )
    state = lax.ppermute(state, "ctx", [(j, (j + row) % size) for j in range(size)])
    grad = lax.ppermute(grad, "ctx", [((j + row) % size, j) for j in range(size)])
    spread = call(
        partial(spread_kernel, size), "row_states", (place,), (mine, state, grad), [shape(2, W, W)] * GROUP, [pltpu.VMEM((GROUP, 2, W, W), F32)]
    )
    own_back, give_back = call(
        part_kernel, "chip_part", (place,), (own, other, *along_x(spread)), [shape(GROUP, 2, W, W)] * 2
    )
    other_back = lax.ppermute(give_back, "ctx", pair)
    before = run_backward(place, side, own_back, own_kept, beta_t, keep_w, keep_v, ())
    *chunks, grad_d, grads, db = run_backward(place, side, other_back, give_kept, beta_t, *give_w, before)
    total = run_chunk(side, grads, db, before[0], beta_t, *give_w)
    for d, chunk in zip(ORDER, chunks):
        total = total + lax.ppermute(chunk, "head", [(j, (j + d) % SIDES) for j in range(SIDES)])
    return (total.astype(BF16), grad_d.T)


def solution(mesh):
    placed = (
        P("ctx", None),
        P("ctx", None),
        P(None, "head"),
        P(None, "head"),
        P(None, "head"),
        P(None, "head"),
        P("head", None),
        P("ctx", "head"),
        P(),
    )
    return jax.shard_map(
        per_device,
        mesh=mesh,
        in_specs=placed,
        out_specs=(P("ctx", "head"), P("ctx", "head")),
        check_vma=False,
    )
```

```python
from functools import partial

import jax
import jax.numpy as jnp
from jax import lax
from jax.experimental import pallas as pl
from jax.experimental.pallas import tpu as pltpu
from jax.sharding import PartitionSpec as P

F32 = jnp.float32
BF16 = jnp.bfloat16
W = 128
GROUP = 4
SIDES = 4
ORDER = (2, 1, 3)
NN = (((1,), (0,)), ((), ()))
NT = (((1,), (1,)), ((), ()))
TN = (((0,), (0,)), ((), ()))


def dot(a, b, dims=NN):
    return lax.dot_general(a, b, dims, preferred_element_type=F32)


def exact(a, b, dims=NN):
    return lax.dot_general(a, b, dims, precision=lax.Precision.HIGHEST, preferred_element_type=F32)


def halves(a):
    high = a.astype(BF16)
    return high, (a - high.astype(F32)).astype(BF16)


def mm3(a, b, dims=NN):
    ah, al = halves(a)
    bh, bl = halves(b)
    (ca,), (cb,) = dims[0]
    return dot(jnp.concatenate([ah, al], axis=ca), jnp.concatenate([bh, bh], axis=cb), dims) + dot(ah, bl, dims)


def iotas(shape):
    return lax.broadcasted_iota(jnp.int32, shape, 0), lax.broadcasted_iota(jnp.int32, shape, 1)


def column(array, index):
    lanes = lax.broadcasted_iota(jnp.int32, array.shape, 1)
    return jnp.sum(jnp.where(lanes == index, array, 0.0), axis=1, keepdims=True)


def inverse_all(mixes):
    ti, si = iotas((W, W))
    eye = jnp.where(ti == si, 1.0, 0.0)
    below = jnp.logical_and((ti >> 1) == (si >> 1), ti > si)
    done = [eye - jnp.where(below, a, 0.0) for a in mixes]
    for shift in range(1, 7):
        below = jnp.logical_and((ti >> (shift + 1)) == (si >> (shift + 1)), (ti >> shift) > (si >> shift))
        parts = [jnp.where(below, a, 0.0) for a in mixes]
        inner = [mm3(p, d) for p, d in zip(parts, done)]
        done = [d - mm3(d, i) for d, i in zip(done, inner)]
    return done


def head_columns(head0):
    return pl.ds(pl.multiple_of(head0 * W, GROUP * W), GROUP * W)


def give_kernel(
    place_ref, side_ref, len_hbm, x_hbm, go_hbm, wb_hbm, dec_hbm, wk_hbm, wq_hbm, wo_hbm, wv_hbm, *refs
):
    outs, refs = refs[:2], refs[2:]
    x_ref, go_ref, beta_ref, run_ref, rows_ref, keep_ref, first_ref, wkq_ref, wv_ref, wkq2_ref = refs[:10]
    len_ref, wb_ref, dec_ref, wo_ref, sems = refs[10:]
    keep0 = (place_ref[0] & 1) * GROUP
    head0 = GROUP - keep0
    base = place_ref[0] * W
    at = head_columns(head0)
    at2 = head_columns(keep0)
    pairs = (
        (wk_hbm.at[:, at], wkq_ref.at[0]), (x_hbm, x_ref), (len_hbm, len_ref), (dec_hbm, dec_ref), (wb_hbm, wb_ref),
        (wq_hbm.at[:, at], wkq_ref.at[1]), (wv_hbm.at[:, at], wv_ref), (go_hbm, go_ref), (wo_hbm.at[at, :], wo_ref),
        (wk_hbm.at[:, at2], wkq2_ref.at[0]), (wq_hbm.at[:, at2], wkq2_ref.at[1]),
    )
    gets = [pltpu.make_async_copy(src, dst, sems.at[j]) for j, (src, dst) in enumerate(pairs)]
    for get in (gets[2], gets[3], gets[4], gets[1], gets[0], gets[5], gets[6], gets[7], gets[8], gets[9], gets[10]):
        get.start()
    gets[2].wait()
    ti, si = iotas((W, W))
    begin = jnp.int32(0)
    seg_t = jnp.zeros((W, 1), jnp.int32)
    seg_s = jnp.zeros((1, W), jnp.int32)
    seg_in = jnp.int32(0)
    for j in range(len_ref.shape[0]):
        seg_t = seg_t + (ti[:, :1] + base >= begin).astype(jnp.int32)
        seg_s = seg_s + (si[:1, :] + base >= begin).astype(jnp.int32)
        seg_in = seg_in + (base - 1 >= begin).astype(jnp.int32)
        begin = begin + len_ref[j]
    keep_ref[...] = jnp.where(jnp.logical_and(seg_t == seg_s, ti >= si), 1.0, 0.0)
    lane = iotas(first_ref.shape)[1]
    marked = jnp.where(lane == 0, seg_in, seg_t[W - 1:W, :])
    first_ref[...] = jnp.where(seg_t == marked, 1.0, 0.0)
    gets[3].wait()
    tril = jnp.where(ti >= si, 1.0, 0.0)
    run_ref[...] = exact(tril, dec_ref[...], NT)
    rows_ref[...] = exact(dec_ref[...], tril, NT)
    gets[4].wait()
    gets[1].wait()
    beta_ref[...] = 1.0 / (1.0 + jnp.exp(-dot(x_ref[...], wb_ref[...], NT)))
    block_body(
        head0, x_ref, go_ref, beta_ref, run_ref, rows_ref, keep_ref, first_ref, wkq_ref, wv_ref, wo_ref,
        (gets[0], gets[5], gets[6], gets[7], gets[8]), outs,
    )
    gets[9].wait()
    gets[10].wait()


def keep_kernel(
    place_ref, x_ref, go_ref, beta_ref, run_ref, rows_ref, keep_ref, first_ref, wkq_ref, wo_hbm, wv_hbm, *refs
):
    outs = refs[:2]
    wv_ref, wo_ref, sems = refs[2:]
    head0 = (place_ref[0] & 1) * GROUP
    at = head_columns(head0)
    get_v = pltpu.make_async_copy(wv_hbm.at[:, at], wv_ref, sems.at[0])
    get_o = pltpu.make_async_copy(wo_hbm.at[at, :], wo_ref, sems.at[1])
    get_v.start()
    get_o.start()
    block_body(
        head0, x_ref, go_ref, beta_ref, run_ref, rows_ref, keep_ref, first_ref, wkq_ref, wv_ref, wo_ref,
        (None, None, get_v, None, get_o), outs,
    )


def block_body(
    head0, x_ref, go_ref, beta_ref, run_ref, rows_ref, keep_ref, first_ref, wkq_ref, wv_ref, wo_ref, gets, outs
):
    send_ref, kept_ref = outs

    def ready(*which):
        for j in which:
            if gets[j] is not None:
                gets[j].wait()

    ti, si = iotas((W, W))
    strict = ti > si
    keep = keep_ref[...] > 0.0
    first = first_ref[...][:, :1] > 0.0
    final = first_ref[...][:, 1:2] > 0.0
    beta_all, run_all, run_rows = beta_ref[...], run_ref[...], rows_ref[...]
    heads = range(GROUP)
    cut = lambda a, i: a[:, i * W:(i + 1) * W]
    ready(0)
    x = x_ref[...]
    raw_k = dot(x, wkq_ref[0])
    ready(1)
    raw_q = dot(x, wkq_ref[1])
    ks, qs, betas, carries, wkks, mixes, pmats = [], [], [], [], [], [], []
    for i in heads:
        head = head0 + i
        rk = cut(raw_k, i)
        rq = cut(raw_q, i)
        inv_k = lax.rsqrt(jnp.sum(rk * rk, axis=1, keepdims=True) + 1e-06)
        inv_q = lax.rsqrt(jnp.sum(rq * rq, axis=1, keepdims=True) + 1e-06)
        k = rk * inv_k
        q = rq * inv_q * (W ** -0.5)
        beta = column(beta_all, head)
        run = column(run_all, head)
        heads_at = lax.broadcasted_iota(jnp.int32, run_rows.shape, 0)
        spread = run - jnp.sum(jnp.where(heads_at == head, run_rows, 0.0), axis=0, keepdims=True)
        weight = jnp.where(keep, jnp.exp(jnp.where(keep, spread, 0.0)), 0.0)
        carried = jnp.where(first, jnp.exp(run), 0.0)
        both = mm3(jnp.concatenate([k, q], axis=0), k, NT)
        wkk = jnp.where(strict, weight, 0.0) * both[:W]
        pmat = weight * both[W:]
        ks.append(k)
        qs.append(q)
        betas.append(beta)
        carries.append(carried)
        wkks.append(wkk)
        mixes.append(wkk * beta)
        pmats.append(pmat)
        lanes = si
        closing = jnp.where(final, jnp.exp(jnp.where(final, run[W - 1:W, :] - run, 0.0)), 0.0)
        col = jnp.where(lanes == 0, beta, jnp.where(lanes == 1, carried, jnp.where(lanes == 2, closing, jnp.where(lanes == 3, inv_k, inv_q))))
        kept_ref[i, 10] = col
        kept_ref[i, 0] = k
        kept_ref[i, 1] = q
        kept_ref[i, 4] = pmat
        kept_ref[i, 6] = wkk
        kept_ref[i, 7] = weight
    solved = inverse_all(mixes)
    ready(2)
    raw_v = dot(x, wv_ref[...])
    ready(3, 4)
    grad_o = dot(go_ref[...], wo_ref[...], NT)
    for i in heads:
        k, q, beta, carried = ks[i], qs[i], betas[i], carries[i]
        kept_ref[i, 5] = solved[i]
        kept_ref[i, 2] = cut(raw_v, i)
        kept_ref[i, 3] = cut(grad_o, i)
        right = jnp.concatenate([beta * cut(raw_v, i), (beta * carried) * k], axis=1)
        both = mm3(solved[i], right)
        uv = both[:, :W]
        kw = both[:, W:]
        kept_ref[i, 8] = uv
        kept_ref[i, 9] = kw
        eff = carried * q - mm3(pmats[i], kw)
        closing = kept_ref[i, 10][:, 2:3]
        ends = mm3(jnp.concatenate([kw, uv], axis=1), closing * k, TN)
        last = carried[W - 1:W, :]
        send_ref[i, 0] = jnp.where(ti == si, last, 0.0) - ends[:W]
        send_ref[i, 1] = ends[W:]
        send_ref[i, 2] = mm3(cut(grad_o, i), eff, TN)


def join_kernel(place_ref, own_ref, other_ref, *out_refs):
    second = (place_ref[0] & 1) == 1
    x = place_ref[0] >> 1
    for d in range(GROUP):
        i = (x + d) & (GROUP - 1)
        out_ref = out_refs[d]
        ta = jnp.where(second, other_ref[i, 0], own_ref[i, 0])
        tb = jnp.where(second, own_ref[i, 0], other_ref[i, 0])
        oa = jnp.where(second, other_ref[i, 1], own_ref[i, 1])
        ob = jnp.where(second, own_ref[i, 1], other_ref[i, 1])
        ga = jnp.where(second, other_ref[i, 2], own_ref[i, 2])
        gb = jnp.where(second, own_ref[i, 2], other_ref[i, 2])
        front = mm3(jnp.concatenate([ta, oa], axis=0), tb)
        out_ref[0] = front[:W]
        out_ref[1] = front[W:] + ob
        out_ref[2] = mm3(gb, ta, NT) + ga


def row_kernel(place_ref, *refs):
    x = place_ref[0] >> 1
    parts, (r_ref, state_ref, grad_ref) = refs[:GROUP], refs[GROUP:]
    for d, part in enumerate(parts):
        r_ref[(x - d) & (GROUP - 1)] = part[...]
    state = r_ref[0, 1]
    grad = r_ref[GROUP - 1, 2]
    for j in range(1, GROUP):
        state = mm3(state, r_ref[j, 0]) + r_ref[j, 1]
        b = GROUP - 1 - j
        grad = mm3(grad, r_ref[b, 0], NT) + r_ref[b, 2]
    state_ref[...] = state
    grad_ref[...] = grad


def spread_kernel(size, place_ref, r_ref, s_ref, g_ref, *refs):
    x = place_ref[0] >> 1
    outs, all_ref = refs[:GROUP], refs[GROUP]
    state = jnp.where(place_ref[0] < 2 * GROUP, 0.0, s_ref[...])
    grad = jnp.where(place_ref[0] >= size - 2 * GROUP, 0.0, g_ref[...])
    all_ref[0, 0] = state
    all_ref[GROUP - 1, 1] = grad
    for j in range(1, GROUP):
        state = mm3(state, r_ref[j - 1, 0]) + r_ref[j - 1, 1]
        all_ref[j, 0] = state
        b = GROUP - j
        grad = mm3(grad, r_ref[b, 0], NT) + r_ref[b, 2]
        all_ref[b - 1, 1] = grad
    for d, out in enumerate(outs):
        out[...] = all_ref[(x + d) & (GROUP - 1)]


def part_kernel(place_ref, own_ref, other_ref, *refs):
    chips, (mine_ref, give_ref) = refs[:GROUP], refs[GROUP:]
    second = (place_ref[0] & 1) == 1
    x = place_ref[0] >> 1
    for d, chip_ref in enumerate(chips):
        i = (x - d) & (GROUP - 1)
        ta = jnp.where(second, other_ref[i, 0], own_ref[i, 0])
        tb = jnp.where(second, own_ref[i, 0], other_ref[i, 0])
        oa = jnp.where(second, other_ref[i, 1], own_ref[i, 1])
        gb = jnp.where(second, own_ref[i, 2], other_ref[i, 2])
        s_in, g_end = chip_ref[0], chip_ref[1]
        s_mid = mm3(s_in, ta) + oa
        g_mid = mm3(g_end, tb, NT) + gb
        mine_ref[i, 0] = jnp.where(second, s_mid, s_in)
        mine_ref[i, 1] = jnp.where(second, g_end, g_mid)
        give_ref[i, 0] = jnp.where(second, s_in, s_mid)
        give_ref[i, 1] = jnp.where(second, g_mid, g_end)


def back_project(side, grads, db, wkq_ref, wv_ref, wb_ref, wide):
    at = pl.ds(pl.multiple_of(side * wide, wide), wide)
    n = grads.shape[1] // 3
    piece = dot(grads[:, :n], wkq_ref[1, at, :], NT) + dot(grads[:, n:2 * n], wkq_ref[0, at, :], NT)
    return piece + dot(grads[:, 2 * n:], wv_ref[at, :], NT) + dot(db, wb_ref[:, at])


def chunk_kernel(side_ref, grads_ref, db_ref, before_ref, wb_ref, wkq_ref, wv_ref, out_ref):
    piece = back_project(side_ref[0], grads_ref[...], db_ref[...], wkq_ref, wv_ref, wb_ref, out_ref.shape[1])
    out_ref[...] = before_ref[0] + piece


def early_kernel(kept_ref, out_ref):
    heads = range(GROUP)
    k, do, uv = ([kept_ref[i, j] for i in heads] for j in (0, 3, 8))
    ends = [kept_ref[i, 10][:, 2:3] * k[i] for i in heads]
    inner = [mm3(kept_ref[i, 4], do[i], TN) for i in heads]
    both = [mm3(kept_ref[i, 5], jnp.concatenate([inner[i], ends[i]], axis=1), TN) for i in heads]
    for i in heads:
        out_ref[i, 0] = both[i][:, :W]
        out_ref[i, 1] = both[i][:, W:]
        out_ref[i, 2] = mm3(do[i], uv[i], NT)


def second_kernel(chained, *refs):
    place_ref, side_ref, back_ref, kept_ref, early_ref, wb_ref, wkq_ref, wv_ref = refs[:8]
    refs = refs[8:]
    if chained:
        before_ref, gd_before_ref, *total_refs, gd_ref, grads_ref, db_ref = refs
        wide = total_refs[0].shape[-1]
    else:
        total_ref, gd_ref = refs
        wide = total_ref.shape[-1]
    keep0 = (place_ref[0] & 1) * GROUP
    head0 = GROUP - keep0 if chained else keep0
    side = side_ref[0]
    ti, si = iotas((W, W))
    strict = ti > si
    upper = jnp.where(si >= ti, 1.0, 0.0)
    t8, h8 = iotas((W, 8))
    none = jnp.zeros((W, 8), F32)
    cterm, fterm, eterm, dball = none, none, none, none
    gqs, gks, gvs = [], [], []
    for i in range(GROUP):
        head = head0 + i
        s0, g1 = back_ref[i, 0], back_ref[i, 1]
        k, q, v, do = kept_ref[i, 0], kept_ref[i, 1], kept_ref[i, 2], kept_ref[i, 3]
        pmat, wkk, weight = kept_ref[i, 4], kept_ref[i, 6], kept_ref[i, 7]
        col = kept_ref[i, 10]
        beta, carried, closing, inv_k, inv_q = (col[:, j:j + 1] for j in range(5))
        kw = kept_ref[i, 9]
        u = kept_ref[i, 8] - mm3(kw, s0, NT)
        dr = early_ref[i, 0] + mm3(early_ref[i, 1], g1, NT)
        ds = mm3(jnp.concatenate([do, dr], axis=0), s0)
        dq_state = carried * ds[:W]
        dr_s = carried * ds[W:]
        dp = early_ref[i, 2] - mm3(ds[:W], kw, NT)
        da = -mm3(dr, u, NT)
        ug = closing * mm3(u, g1)
        dqk = weight * dp
        dkk = jnp.where(strict, weight, 0.0) * da * beta
        front = mm3(jnp.concatenate([dqk, dkk], axis=0), k)
        dq = front[:W] + dq_state
        dk = front[W:] + mm3(jnp.concatenate([dkk, dqk], axis=0), jnp.concatenate([k, q], axis=0), TN)
        dk = dk - beta * dr_s + ug
        known = jnp.sum(dr_s * k, axis=1, keepdims=True)
        dbeta = jnp.sum(dr * v, axis=1, keepdims=True) - known + jnp.sum(da * wkk, axis=1, keepdims=True)
        dlogit = dbeta * beta * (1.0 - beta)
        pairs = dp * pmat + da * wkk * beta
        ph, plow = halves(pairs)
        ub = upper.astype(BF16)
        across = dot(ub, ph) + dot(ub, plow)
        evec = jnp.sum(jnp.where(strict, across, 0.0), axis=1, keepdims=True)
        fvec = jnp.sum(ug * k, axis=1, keepdims=True)
        cvec = jnp.sum(dq_state * q, axis=1, keepdims=True) - beta * known
        ends = carried[W - 1:W, :] * jnp.sum(jnp.sum(g1 * s0, axis=1, keepdims=True), axis=0, keepdims=True)
        cvec = cvec + jnp.where(t8[:, :1] == W - 1, ends, 0.0)
        here = h8 == head
        cterm = jnp.where(here, cvec, cterm)
        fterm = jnp.where(here, fvec, fterm)
        eterm = jnp.where(here, evec, eterm)
        dball = jnp.where(here, dlogit, dball)
        gk = inv_k * (dk - k * jnp.sum(k * dk, axis=1, keepdims=True))
        gq = (inv_q * (W ** -0.5)) * (dq - (q * float(W)) * jnp.sum(q * dq, axis=1, keepdims=True))
        gqs.append(gq.astype(BF16))
        gks.append(gk.astype(BF16))
        gvs.append((beta * dr).astype(BF16))
    grads = jnp.concatenate(gqs + gks + gvs, axis=1)
    db = dball.astype(BF16)
    project = lambda d: back_project((side + d) & (SIDES - 1), grads, db, wkq_ref, wv_ref, wb_ref, wide)
    if chained:
        for d, total_ref in zip(ORDER, total_refs):
            total_ref[...] = before_ref[d] + project(d)
        grads_ref[...] = grads
        db_ref[...] = db
    else:
        for d in range(SIDES):
            total_ref[d] = project(d)
    eye = jnp.where(ti == si, 1.0, 0.0)
    terms = jnp.concatenate([cterm, fterm, eterm], axis=0)
    top = terms.astype(BF16)
    middle, bottom = halves(terms - top.astype(F32))
    sums = dot(jnp.concatenate([top, middle, bottom], axis=1), jnp.concatenate([jnp.where(ti >= si, 1.0, 0.0), jnp.where(si > ti, 1.0, 0.0), eye], axis=0).astype(BF16), TN)
    decays = sums[:8] + sums[8:16] + sums[16:]
    gd_ref[...] = gd_before_ref[...] + decays if chained else decays


SMEM = pl.BlockSpec(memory_space=pltpu.SMEM)
VMEM = pl.BlockSpec(memory_space=pltpu.VMEM)
HBM = pl.BlockSpec(memory_space=pltpu.HBM)


def shape(*dims):
    return jax.ShapeDtypeStruct(dims, F32)


def in_hbm(*arrays):
    return [pltpu.with_memory_space_constraint(a, pltpu.HBM) for a in arrays]


def block_shapes():
    return [shape(GROUP, 3, W, W), shape(GROUP, 11, W, W)]


def run_give(place, side, lengths, inputs, grad_out, beta_t, decay_t, w_key, w_query, w_out, w_value):
    rows, width = inputs.shape
    heads, span = beta_t.shape[0], GROUP * W
    wide = jax.ShapeDtypeStruct((rows, width), BF16)
    tall = jax.ShapeDtypeStruct((width, span), BF16)
    two = jax.ShapeDtypeStruct((2, width, span), BF16)
    out = pl.pallas_call(
        give_kernel,
        in_specs=[SMEM] * 2 + [HBM] * 9,
        out_specs=[VMEM] * 12,
        out_shape=block_shapes() + [wide, wide, shape(rows, heads), shape(rows, heads), shape(heads, rows), shape(W, W), shape(W, heads)] + [two, tall, two],
        scratch_shapes=[
            pltpu.SMEM(lengths.shape, jnp.int32), pltpu.VMEM(beta_t.shape, BF16), pltpu.VMEM(decay_t.shape, F32),
            pltpu.VMEM((span, width), BF16), pltpu.SemaphoreType.DMA((11,)),
        ],
        compiler_params=pltpu.CompilerParams(vmem_limit_bytes=28 << 20),
        name="block_forward_give",
    )(place, side, *in_hbm(lengths, inputs, grad_out, beta_t, decay_t, w_key, w_query, w_out, w_value))
    return out[0], out[1], out[2:9], out[9:11], out[11]


def run_keep(place, shared, w_keep, w_out, w_value):
    _, width, span = w_keep.shape
    out = pl.pallas_call(
        keep_kernel,
        in_specs=[SMEM] + [VMEM] * 8 + [HBM] * 2,
        out_specs=[VMEM] * 3,
        out_shape=block_shapes() + [jax.ShapeDtypeStruct((width, span), BF16)],
        scratch_shapes=[pltpu.VMEM((span, width), BF16), pltpu.SemaphoreType.DMA((2,))],
        compiler_params=pltpu.CompilerParams(vmem_limit_bytes=24 << 20),
        name="block_forward_keep",
    )(place, *shared, w_keep, *in_hbm(w_out, w_value))
    return out


def run_backward(place, side, back, kept, early, beta_t, w_both, w_value, before):
    heads, width = beta_t.shape
    wide = width // SIDES
    if before:
        out_shape = [shape(W, wide)] * 3 + [shape(heads, W), jax.ShapeDtypeStruct((W, 3 * GROUP * W), BF16), jax.ShapeDtypeStruct((W, heads), BF16)]
    else:
        out_shape = [shape(SIDES, W, wide), shape(heads, W)]
    return pl.pallas_call(
        partial(second_kernel, bool(before)),
        in_specs=[SMEM] * 2 + [VMEM] * 6 + [VMEM] * len(before),
        out_specs=[VMEM] * len(out_shape),
        out_shape=out_shape,
        compiler_params=pltpu.CompilerParams(vmem_limit_bytes=24 << 20),
        name="block_backward",
    )(place, side, back, kept, early, beta_t, w_both, w_value, *before)


def run_chunk(side, grads, db, before, beta_t, w_both, w_value):
    return pl.pallas_call(
        chunk_kernel,
        in_specs=[SMEM] + [VMEM] * 6,
        out_specs=VMEM,
        out_shape=shape(*before.shape[1:]),
        compiler_params=pltpu.CompilerParams(vmem_limit_bytes=16 << 20),
        name="own_chunk",
    )(side, grads, db, before, beta_t, w_both, w_value)


def per_device(inputs, grad_out, w_query, w_key, w_value, w_beta, w_out, log_decay, lengths):
    size = lax.axis_size("ctx")
    place = lax.axis_index("ctx").astype(jnp.int32).reshape(1)
    side = lax.axis_index("head").astype(jnp.int32).reshape(1)
    beta_t, decay_t = w_beta.T, log_decay.T
    small = pltpu.CompilerParams(vmem_limit_bytes=8 << 20)

    pair = [(j, j ^ 1) for j in range(size)]
    give, give_kept, shared, give_w, keep_w = run_give(
        place, side, lengths, inputs, grad_out, beta_t, decay_t, w_key, w_query, w_out, w_value
    )
    other = lax.ppermute(give, "ctx", pair)
    own, own_kept, keep_v = run_keep(place, shared, keep_w, w_out, w_value)
    row = 2 * GROUP

    def call(kernel, name, scalars, arrays, out_shape, scratch=()):
        return pl.pallas_call(
            kernel,
            in_specs=[SMEM] * len(scalars) + [VMEM] * len(arrays),
            out_specs=[VMEM] * len(out_shape),
            out_shape=out_shape,
            scratch_shapes=list(scratch),
            compiler_params=small,
            name=name,
        )(*scalars, *arrays)

    def along_x(parts):
        got = {0: parts[0]}
        for d in (2, 1, 3):
            moves = [(j, j - j % row + (j + 2 * d) % row) for j in range(size)]
            got[d] = lax.ppermute(parts[d], "ctx", moves)
        return [got[d] for d in range(GROUP)]

    def early(kept):
        return pl.pallas_call(
            early_kernel, in_specs=[VMEM], out_specs=VMEM, out_shape=shape(GROUP, 3, W, W), name="early",
            compiler_params=pltpu.CompilerParams(vmem_limit_bytes=12 << 20),
            cost_estimate=pl.CostEstimate(flops=1 << 30, bytes_accessed=4 << 20, transcendentals=0),
        )(kept)

    whole = call(join_kernel, "chip_join", (place,), (own, other), [shape(3, W, W)] * GROUP)
    *whole, give_kept, own_kept = lax.optimization_barrier((*whole, give_kept, own_kept))
    *arrived, own_early, give_early = lax.optimization_barrier((*along_x(whole), early(own_kept), early(give_kept)))
    mine, state, grad = call(
        row_kernel, "row_ends", (place,), arrived, [shape(GROUP, 3, W, W), shape(W, W), shape(W, W)]
    )
    state = lax.ppermute(state, "ctx", [(j, (j + row) % size) for j in range(size)])
    grad = lax.ppermute(grad, "ctx", [((j + row) % size, j) for j in range(size)])
    spread = call(
        partial(spread_kernel, size), "row_states", (place,), (mine, state, grad), [shape(2, W, W)] * GROUP, [pltpu.VMEM((GROUP, 2, W, W), F32)]
    )
    own_back, give_back = call(
        part_kernel, "chip_part", (place,), (own, other, *along_x(spread)), [shape(GROUP, 2, W, W)] * 2
    )
    other_back = lax.ppermute(give_back, "ctx", pair)
    before = run_backward(place, side, own_back, own_kept, own_early, beta_t, keep_w, keep_v, ())
    *chunks, grad_d, grads, db = run_backward(place, side, other_back, give_kept, give_early, beta_t, *give_w, before)
    total = run_chunk(side, grads, db, before[0], beta_t, *give_w)
    for d, chunk in zip(ORDER, chunks):
        total = total + lax.ppermute(chunk, "head", [(j, (j + d) % SIDES) for j in range(SIDES)])
    return (total.astype(BF16), grad_d.T)


def solution(mesh):
    placed = (
        P("ctx", None),
        P("ctx", None),
        P(None, "head"),
        P(None, "head"),
        P(None, "head"),
        P(None, "head"),
        P("head", None),
        P("ctx", "head"),
        P(),
    )
    return jax.shard_map(
        per_device,
        mesh=mesh,
        in_specs=placed,
        out_specs=(P("ctx", "head"), P("ctx", "head")),
        check_vma=False,
    )
```

```python
from functools import partial

import jax
import jax.numpy as jnp
from jax import lax
from jax.experimental import pallas as pl
from jax.experimental.pallas import tpu as pltpu
from jax.sharding import PartitionSpec as P

F32 = jnp.float32
BF16 = jnp.bfloat16
W = 128
GROUP = 4
SIDES = 4
ORDER = (2, 1, 3)
NN = (((1,), (0,)), ((), ()))
NT = (((1,), (1,)), ((), ()))
TN = (((0,), (0,)), ((), ()))


def dot(a, b, dims=NN):
    return lax.dot_general(a, b, dims, preferred_element_type=F32)


def exact(a, b, dims=NN):
    return lax.dot_general(a, b, dims, precision=lax.Precision.HIGHEST, preferred_element_type=F32)


def halves(a):
    high = a.astype(BF16)
    return high, (a - high.astype(F32)).astype(BF16)


def mm3(a, b, dims=NN):
    ah, al = halves(a)
    bh, bl = halves(b)
    (ca,), (cb,) = dims[0]
    return dot(jnp.concatenate([ah, al], axis=ca), jnp.concatenate([bh, bh], axis=cb), dims) + dot(ah, bl, dims)


def iotas(shape):
    return lax.broadcasted_iota(jnp.int32, shape, 0), lax.broadcasted_iota(jnp.int32, shape, 1)


def column(array, index):
    lanes = lax.broadcasted_iota(jnp.int32, array.shape, 1)
    return jnp.sum(jnp.where(lanes == index, array, 0.0), axis=1, keepdims=True)


def inverse_all(mixes):
    ti, si = iotas((W, W))
    eye = jnp.where(ti == si, 1.0, 0.0)
    below = jnp.logical_and((ti >> 1) == (si >> 1), ti > si)
    done = [eye - jnp.where(below, a, 0.0) for a in mixes]
    for shift in range(1, 7):
        below = jnp.logical_and((ti >> (shift + 1)) == (si >> (shift + 1)), (ti >> shift) > (si >> shift))
        parts = [jnp.where(below, a, 0.0) for a in mixes]
        inner = [mm3(p, d) for p, d in zip(parts, done)]
        done = [d - mm3(d, i) for d, i in zip(done, inner)]
    return done


def head_columns(head0):
    return pl.ds(pl.multiple_of(head0 * W, GROUP * W), GROUP * W)


def give_kernel(
    place_ref, side_ref, len_hbm, x_hbm, go_hbm, wb_hbm, dec_hbm, wk_hbm, wq_hbm, wo_hbm, wv_hbm, *refs
):
    outs, refs = refs[:2], refs[2:]
    x_ref, go_ref, beta_ref, run_ref, rows_ref, keep_ref, first_ref, wkq_ref, wv_ref, wkq2_ref = refs[:10]
    len_ref, wb_ref, dec_ref, wo_ref, sems = refs[10:]
    keep0 = (place_ref[0] & 1) * GROUP
    head0 = GROUP - keep0
    base = place_ref[0] * W
    at = head_columns(head0)
    at2 = head_columns(keep0)
    pairs = (
        (wk_hbm.at[:, at], wkq_ref.at[0]), (x_hbm, x_ref), (len_hbm, len_ref), (dec_hbm, dec_ref), (wb_hbm, wb_ref),
        (wq_hbm.at[:, at], wkq_ref.at[1]), (wv_hbm.at[:, at], wv_ref), (go_hbm, go_ref), (wo_hbm.at[at, :], wo_ref),
        (wk_hbm.at[:, at2], wkq2_ref.at[0]), (wq_hbm.at[:, at2], wkq2_ref.at[1]),
    )
    gets = [pltpu.make_async_copy(src, dst, sems.at[j]) for j, (src, dst) in enumerate(pairs)]
    for get in (gets[2], gets[3], gets[4], gets[1], gets[0], gets[5], gets[6], gets[7], gets[8], gets[9], gets[10]):
        get.start()
    gets[2].wait()
    ti, si = iotas((W, W))
    begin = jnp.int32(0)
    seg_t = jnp.zeros((W, 1), jnp.int32)
    seg_s = jnp.zeros((1, W), jnp.int32)
    seg_in = jnp.int32(0)
    for j in range(len_ref.shape[0]):
        seg_t = seg_t + (ti[:, :1] + base >= begin).astype(jnp.int32)
        seg_s = seg_s + (si[:1, :] + base >= begin).astype(jnp.int32)
        seg_in = seg_in + (base - 1 >= begin).astype(jnp.int32)
        begin = begin + len_ref[j]
    keep_ref[...] = jnp.where(jnp.logical_and(seg_t == seg_s, ti >= si), 1.0, 0.0)
    lane = iotas(first_ref.shape)[1]
    marked = jnp.where(lane == 0, seg_in, seg_t[W - 1:W, :])
    first_ref[...] = jnp.where(seg_t == marked, 1.0, 0.0)
    gets[3].wait()
    tril = jnp.where(ti >= si, 1.0, 0.0)
    run_ref[...] = exact(tril, dec_ref[...], NT)
    rows_ref[...] = exact(dec_ref[...], tril, NT)
    gets[4].wait()
    gets[1].wait()
    beta_ref[...] = 1.0 / (1.0 + jnp.exp(-dot(x_ref[...], wb_ref[...], NT)))
    block_body(
        head0, x_ref, go_ref, beta_ref, run_ref, rows_ref, keep_ref, first_ref, wkq_ref, wv_ref, wo_ref,
        (gets[0], gets[5], gets[6], gets[7], gets[8]), outs,
    )
    gets[9].wait()
    gets[10].wait()


def keep_kernel(
    place_ref, x_ref, go_ref, beta_ref, run_ref, rows_ref, keep_ref, first_ref, wkq_ref, wo_hbm, wv_hbm, *refs
):
    outs = refs[:2]
    wv_ref, wo_ref, sems = refs[2:]
    head0 = (place_ref[0] & 1) * GROUP
    at = head_columns(head0)
    get_v = pltpu.make_async_copy(wv_hbm.at[:, at], wv_ref, sems.at[0])
    get_o = pltpu.make_async_copy(wo_hbm.at[at, :], wo_ref, sems.at[1])
    get_v.start()
    get_o.start()
    block_body(
        head0, x_ref, go_ref, beta_ref, run_ref, rows_ref, keep_ref, first_ref, wkq_ref, wv_ref, wo_ref,
        (None, None, get_v, None, get_o), outs,
    )


def block_body(
    head0, x_ref, go_ref, beta_ref, run_ref, rows_ref, keep_ref, first_ref, wkq_ref, wv_ref, wo_ref, gets, outs
):
    send_ref, kept_ref = outs

    def ready(*which):
        for j in which:
            if gets[j] is not None:
                gets[j].wait()

    ti, si = iotas((W, W))
    strict = ti > si
    keep = keep_ref[...] > 0.0
    first = first_ref[...][:, :1] > 0.0
    final = first_ref[...][:, 1:2] > 0.0
    beta_all, run_all, run_rows = beta_ref[...], run_ref[...], rows_ref[...]
    heads = range(GROUP)
    cut = lambda a, i: a[:, i * W:(i + 1) * W]
    ready(0)
    x = x_ref[...]
    raw_k = dot(x, wkq_ref[0])
    ready(1)
    raw_q = dot(x, wkq_ref[1])
    ks, qs, betas, carries, closings, mixes, pmats = [], [], [], [], [], [], []
    for i in heads:
        head = head0 + i
        rk = cut(raw_k, i)
        rq = cut(raw_q, i)
        inv_k = lax.rsqrt(jnp.sum(rk * rk, axis=1, keepdims=True) + 1e-06)
        inv_q = lax.rsqrt(jnp.sum(rq * rq, axis=1, keepdims=True) + 1e-06)
        k = rk * inv_k
        q = rq * inv_q * (W ** -0.5)
        beta = column(beta_all, head)
        run = column(run_all, head)
        heads_at = lax.broadcasted_iota(jnp.int32, run_rows.shape, 0)
        spread = run - jnp.sum(jnp.where(heads_at == head, run_rows, 0.0), axis=0, keepdims=True)
        weight = jnp.where(keep, jnp.exp(jnp.where(keep, spread, 0.0)), 0.0)
        carried = jnp.where(first, jnp.exp(run), 0.0)
        both = mm3(jnp.concatenate([k, q], axis=0), k, NT)
        wkk = jnp.where(strict, weight, 0.0) * both[:W]
        pmat = weight * both[W:]
        ks.append(k)
        qs.append(q)
        betas.append(beta)
        carries.append(carried)
        mixes.append(wkk * beta)
        pmats.append(pmat)
        lanes = si
        closing = jnp.where(final, jnp.exp(jnp.where(final, run[W - 1:W, :] - run, 0.0)), 0.0)
        closings.append(closing)
        col = jnp.where(lanes == 0, beta, jnp.where(lanes == 1, carried, jnp.where(lanes == 2, closing, jnp.where(lanes == 3, inv_k, inv_q))))
        kept_ref[i, 10] = col
        kept_ref[i, 0] = k
        kept_ref[i, 1] = q
        kept_ref[i, 4] = pmat
        kept_ref[i, 6] = wkk
        kept_ref[i, 7] = weight
    solved = inverse_all(mixes)
    ready(2)
    raw_v = dot(x, wv_ref[...])
    ready(3, 4)
    grad_o = dot(go_ref[...], wo_ref[...], NT)
    vs = [cut(raw_v, i) for i in heads]
    dos = [cut(grad_o, i) for i in heads]
    rights = [jnp.concatenate([betas[i] * vs[i], (betas[i] * carries[i]) * ks[i]], axis=1) for i in heads]
    boths = [mm3(solved[i], rights[i]) for i in heads]
    kws = [both[:, W:] for both in boths]
    inner = [mm3(pmats[i], kws[i]) for i in heads]
    flipped = [jnp.concatenate([both[:, W:], both[:, :W]], axis=1) for both in boths]
    ends = [mm3(flipped[i], closings[i] * ks[i], TN) for i in heads]
    effs = [carries[i] * qs[i] - inner[i] for i in heads]
    grads = [mm3(dos[i], effs[i], TN) for i in heads]
    for i in heads:
        kept_ref[i, 5] = solved[i]
        kept_ref[i, 2] = vs[i]
        kept_ref[i, 3] = dos[i]
        kept_ref[i, 8] = boths[i][:, :W]
        kept_ref[i, 9] = kws[i]
        send_ref[i, 0] = jnp.where(ti == si, carries[i][W - 1:W, :], 0.0) - ends[i][:W]
        send_ref[i, 1] = ends[i][W:]
        send_ref[i, 2] = grads[i]


def join_kernel(place_ref, own_ref, other_ref, *out_refs):
    second = (place_ref[0] & 1) == 1
    x = place_ref[0] >> 1
    for d in range(GROUP):
        i = (x + d) & (GROUP - 1)
        out_ref = out_refs[d]
        ta = jnp.where(second, other_ref[i, 0], own_ref[i, 0])
        tb = jnp.where(second, own_ref[i, 0], other_ref[i, 0])
        oa = jnp.where(second, other_ref[i, 1], own_ref[i, 1])
        ob = jnp.where(second, own_ref[i, 1], other_ref[i, 1])
        ga = jnp.where(second, other_ref[i, 2], own_ref[i, 2])
        gb = jnp.where(second, own_ref[i, 2], other_ref[i, 2])
        front = mm3(jnp.concatenate([ta, oa], axis=0), tb)
        out_ref[0] = front[:W]
        out_ref[1] = front[W:] + ob
        out_ref[2] = mm3(gb, ta, NT) + ga


def row_kernel(place_ref, *refs):
    x = place_ref[0] >> 1
    parts, (r_ref, state_ref, grad_ref) = refs[:GROUP], refs[GROUP:]
    for d, part in enumerate(parts):
        r_ref[(x - d) & (GROUP - 1)] = part[...]
    state = r_ref[0, 1]
    grad = r_ref[GROUP - 1, 2]
    for j in range(1, GROUP):
        state = mm3(state, r_ref[j, 0]) + r_ref[j, 1]
        b = GROUP - 1 - j
        grad = mm3(grad, r_ref[b, 0], NT) + r_ref[b, 2]
    state_ref[...] = state
    grad_ref[...] = grad


def spread_kernel(size, place_ref, r_ref, s_ref, g_ref, *refs):
    x = place_ref[0] >> 1
    outs, all_ref = refs[:GROUP], refs[GROUP]
    state = jnp.where(place_ref[0] < 2 * GROUP, 0.0, s_ref[...])
    grad = jnp.where(place_ref[0] >= size - 2 * GROUP, 0.0, g_ref[...])
    all_ref[0, 0] = state
    all_ref[GROUP - 1, 1] = grad
    for j in range(1, GROUP):
        state = mm3(state, r_ref[j - 1, 0]) + r_ref[j - 1, 1]
        all_ref[j, 0] = state
        b = GROUP - j
        grad = mm3(grad, r_ref[b, 0], NT) + r_ref[b, 2]
        all_ref[b - 1, 1] = grad
    for d, out in enumerate(outs):
        out[...] = all_ref[(x + d) & (GROUP - 1)]


def part_kernel(place_ref, own_ref, other_ref, *refs):
    chips, (mine_ref, give_ref) = refs[:GROUP], refs[GROUP:]
    second = (place_ref[0] & 1) == 1
    x = place_ref[0] >> 1
    for d, chip_ref in enumerate(chips):
        i = (x - d) & (GROUP - 1)
        ta = jnp.where(second, other_ref[i, 0], own_ref[i, 0])
        tb = jnp.where(second, own_ref[i, 0], other_ref[i, 0])
        oa = jnp.where(second, other_ref[i, 1], own_ref[i, 1])
        gb = jnp.where(second, own_ref[i, 2], other_ref[i, 2])
        s_in, g_end = chip_ref[0], chip_ref[1]
        s_mid = mm3(s_in, ta) + oa
        g_mid = mm3(g_end, tb, NT) + gb
        mine_ref[i, 0] = jnp.where(second, s_mid, s_in)
        mine_ref[i, 1] = jnp.where(second, g_end, g_mid)
        give_ref[i, 0] = jnp.where(second, s_in, s_mid)
        give_ref[i, 1] = jnp.where(second, g_mid, g_end)


def back_project(side, grads, db, wkq_ref, wv_ref, wb_ref, wide):
    at = pl.ds(pl.multiple_of(side * wide, wide), wide)
    n = grads.shape[1] // 3
    piece = dot(grads[:, :n], wkq_ref[1, at, :], NT) + dot(grads[:, n:2 * n], wkq_ref[0, at, :], NT)
    return piece + dot(grads[:, 2 * n:], wv_ref[at, :], NT) + dot(db, wb_ref[:, at])


def chunk_kernel(side_ref, grads_ref, db_ref, before_ref, wb_ref, wkq_ref, wv_ref, out_ref):
    piece = back_project(side_ref[0], grads_ref[...], db_ref[...], wkq_ref, wv_ref, wb_ref, out_ref.shape[1])
    out_ref[...] = before_ref[0] + piece


def early_kernel(kept_ref, out_ref):
    heads = range(GROUP)
    k, do, uv = ([kept_ref[i, j] for i in heads] for j in (0, 3, 8))
    ends = [kept_ref[i, 10][:, 2:3] * k[i] for i in heads]
    inner = [mm3(kept_ref[i, 4], do[i], TN) for i in heads]
    both = [mm3(kept_ref[i, 5], jnp.concatenate([inner[i], ends[i]], axis=1), TN) for i in heads]
    for i in heads:
        out_ref[i, 0] = both[i][:, :W]
        out_ref[i, 1] = both[i][:, W:]
        out_ref[i, 2] = mm3(do[i], uv[i], NT)


def second_kernel(chained, *refs):
    place_ref, side_ref, back_ref, kept_ref, early_ref, wb_ref, wkq_ref, wv_ref = refs[:8]
    refs = refs[8:]
    if chained:
        before_ref, gd_before_ref, *total_refs, gd_ref, grads_ref, db_ref = refs
        wide = total_refs[0].shape[-1]
    else:
        total_ref, gd_ref = refs
        wide = total_ref.shape[-1]
    keep0 = (place_ref[0] & 1) * GROUP
    head0 = GROUP - keep0 if chained else keep0
    side = side_ref[0]
    ti, si = iotas((W, W))
    strict = ti > si
    upper = jnp.where(si >= ti, 1.0, 0.0)
    t8, h8 = iotas((W, 8))
    none = jnp.zeros((W, 8), F32)
    heads = range(GROUP)
    s0, g1 = ([back_ref[i, j] for i in heads] for j in range(2))
    k, q, v, do, pmat, wkk, weight, uv, kw, col = ([kept_ref[i, j] for i in heads] for j in (0, 1, 2, 3, 4, 6, 7, 8, 9, 10))
    beta, carried, closing, inv_k, inv_q = ([c[:, j:j + 1] for c in col] for j in range(5))
    dr = [early_ref[i, 0] + mm3(early_ref[i, 1], g1[i], NT) for i in heads]
    u = [uv[i] - mm3(kw[i], s0[i], NT) for i in heads]
    ds = [mm3(jnp.concatenate([do[i], dr[i]], axis=0), s0[i]) for i in heads]
    da = [-mm3(dr[i], u[i], NT) for i in heads]
    ug = [closing[i] * mm3(u[i], g1[i]) for i in heads]
    dp = [early_ref[i, 2] - mm3(ds[i][:W], kw[i], NT) for i in heads]
    dkk = [jnp.where(strict, weight[i], 0.0) * da[i] * beta[i] for i in heads]
    dqk = [weight[i] * dp[i] for i in heads]
    pairs = [halves(dp[i] * pmat[i] + da[i] * wkk[i] * beta[i]) for i in heads]
    ub = upper.astype(BF16)
    front = [mm3(jnp.concatenate([dqk[i], dkk[i]], axis=0), k[i]) for i in heads]
    under = [mm3(jnp.concatenate([dkk[i], dqk[i]], axis=0), jnp.concatenate([k[i], q[i]], axis=0), TN) for i in heads]
    across = [dot(ub, high) + dot(ub, low) for high, low in pairs]
    dq_state = [carried[i] * ds[i][:W] for i in heads]
    dr_s = [carried[i] * ds[i][W:] for i in heads]
    total = lambda a: jnp.sum(a, axis=1, keepdims=True)
    known = [total(dr_s[i] * k[i]) for i in heads]
    dbeta = [total(dr[i] * v[i] + da[i] * wkk[i]) - known[i] for i in heads]
    evec = [total(jnp.where(strict, across[i], 0.0)) for i in heads]
    fvec = [total(ug[i] * k[i]) for i in heads]
    cvec = [total(dq_state[i] * q[i]) - beta[i] * known[i] for i in heads]
    ends = [carried[i][W - 1:W, :] * jnp.sum(total(g1[i] * s0[i]), axis=0, keepdims=True) for i in heads]
    cvec = [cvec[i] + jnp.where(t8[:, :1] == W - 1, ends[i], 0.0) for i in heads]
    dq = [front[i][:W] + dq_state[i] for i in heads]
    dk = [front[i][W:] + under[i] - beta[i] * dr_s[i] + ug[i] for i in heads]
    along_k = [total(k[i] * dk[i]) for i in heads]
    along_q = [total(q[i] * dq[i]) for i in heads]
    gks = [(inv_k[i] * (dk[i] - k[i] * along_k[i])).astype(BF16) for i in heads]
    gqs = [((inv_q[i] * (W ** -0.5)) * (dq[i] - (q[i] * float(W)) * along_q[i])).astype(BF16) for i in heads]
    gvs = [(beta[i] * dr[i]).astype(BF16) for i in heads]
    cterm, fterm, eterm, dball = none, none, none, none
    for i in heads:
        here = h8 == head0 + i
        cterm = jnp.where(here, cvec[i], cterm)
        fterm = jnp.where(here, fvec[i], fterm)
        eterm = jnp.where(here, evec[i], eterm)
        dball = jnp.where(here, dbeta[i] * beta[i] * (1.0 - beta[i]), dball)
    grads = jnp.concatenate(gqs + gks + gvs, axis=1)
    db = dball.astype(BF16)
    project = lambda d: back_project((side + d) & (SIDES - 1), grads, db, wkq_ref, wv_ref, wb_ref, wide)
    if chained:
        for d, total_ref in zip(ORDER, total_refs):
            total_ref[...] = before_ref[d] + project(d)
        grads_ref[...] = grads
        db_ref[...] = db
    else:
        for d in range(SIDES):
            total_ref[d] = project(d)
    eye = jnp.where(ti == si, 1.0, 0.0)
    terms = jnp.concatenate([cterm, fterm, eterm], axis=0)
    top = terms.astype(BF16)
    middle, bottom = halves(terms - top.astype(F32))
    sums = dot(jnp.concatenate([top, middle, bottom], axis=1), jnp.concatenate([jnp.where(ti >= si, 1.0, 0.0), jnp.where(si > ti, 1.0, 0.0), eye], axis=0).astype(BF16), TN)
    decays = sums[:8] + sums[8:16] + sums[16:]
    gd_ref[...] = gd_before_ref[...] + decays if chained else decays


SMEM = pl.BlockSpec(memory_space=pltpu.SMEM)
VMEM = pl.BlockSpec(memory_space=pltpu.VMEM)
HBM = pl.BlockSpec(memory_space=pltpu.HBM)


def shape(*dims):
    return jax.ShapeDtypeStruct(dims, F32)


def in_hbm(*arrays):
    return [pltpu.with_memory_space_constraint(a, pltpu.HBM) for a in arrays]


def block_shapes():
    return [shape(GROUP, 3, W, W), shape(GROUP, 11, W, W)]


def run_give(place, side, lengths, inputs, grad_out, beta_t, decay_t, w_key, w_query, w_out, w_value):
    rows, width = inputs.shape
    heads, span = beta_t.shape[0], GROUP * W
    wide = jax.ShapeDtypeStruct((rows, width), BF16)
    tall = jax.ShapeDtypeStruct((width, span), BF16)
    two = jax.ShapeDtypeStruct((2, width, span), BF16)
    out = pl.pallas_call(
        give_kernel,
        in_specs=[SMEM] * 2 + [HBM] * 9,
        out_specs=[VMEM] * 12,
        out_shape=block_shapes() + [wide, wide, shape(rows, heads), shape(rows, heads), shape(heads, rows), shape(W, W), shape(W, heads)] + [two, tall, two],
        scratch_shapes=[
            pltpu.SMEM(lengths.shape, jnp.int32), pltpu.VMEM(beta_t.shape, BF16), pltpu.VMEM(decay_t.shape, F32),
            pltpu.VMEM((span, width), BF16), pltpu.SemaphoreType.DMA((11,)),
        ],
        compiler_params=pltpu.CompilerParams(vmem_limit_bytes=28 << 20),
        name="block_forward_give",
    )(place, side, *in_hbm(lengths, inputs, grad_out, beta_t, decay_t, w_key, w_query, w_out, w_value))
    return out[0], out[1], out[2:9], out[9:11], out[11]


def run_keep(place, shared, w_keep, w_out, w_value):
    _, width, span = w_keep.shape
    out = pl.pallas_call(
        keep_kernel,
        in_specs=[SMEM] + [VMEM] * 8 + [HBM] * 2,
        out_specs=[VMEM] * 3,
        out_shape=block_shapes() + [jax.ShapeDtypeStruct((width, span), BF16)],
        scratch_shapes=[pltpu.VMEM((span, width), BF16), pltpu.SemaphoreType.DMA((2,))],
        compiler_params=pltpu.CompilerParams(vmem_limit_bytes=24 << 20),
        name="block_forward_keep",
    )(place, *shared, w_keep, *in_hbm(w_out, w_value))
    return out


def run_backward(place, side, back, kept, early, beta_t, w_both, w_value, before):
    heads, width = beta_t.shape
    wide = width // SIDES
    if before:
        out_shape = [shape(W, wide)] * 3 + [shape(heads, W), jax.ShapeDtypeStruct((W, 3 * GROUP * W), BF16), jax.ShapeDtypeStruct((W, heads), BF16)]
    else:
        out_shape = [shape(SIDES, W, wide), shape(heads, W)]
    return pl.pallas_call(
        partial(second_kernel, bool(before)),
        in_specs=[SMEM] * 2 + [VMEM] * 6 + [VMEM] * len(before),
        out_specs=[VMEM] * len(out_shape),
        out_shape=out_shape,
        compiler_params=pltpu.CompilerParams(vmem_limit_bytes=24 << 20),
        name="block_backward",
    )(place, side, back, kept, early, beta_t, w_both, w_value, *before)


def run_chunk(side, grads, db, before, beta_t, w_both, w_value):
    return pl.pallas_call(
        chunk_kernel,
        in_specs=[SMEM] + [VMEM] * 6,
        out_specs=VMEM,
        out_shape=shape(*before.shape[1:]),
        compiler_params=pltpu.CompilerParams(vmem_limit_bytes=16 << 20),
        name="own_chunk",
    )(side, grads, db, before, beta_t, w_both, w_value)


def per_device(inputs, grad_out, w_query, w_key, w_value, w_beta, w_out, log_decay, lengths):
    size = lax.axis_size("ctx")
    place = lax.axis_index("ctx").astype(jnp.int32).reshape(1)
    side = lax.axis_index("head").astype(jnp.int32).reshape(1)
    beta_t, decay_t = w_beta.T, log_decay.T
    small = pltpu.CompilerParams(vmem_limit_bytes=8 << 20)

    pair = [(j, j ^ 1) for j in range(size)]
    give, give_kept, shared, give_w, keep_w = run_give(
        place, side, lengths, inputs, grad_out, beta_t, decay_t, w_key, w_query, w_out, w_value
    )
    other = lax.ppermute(give, "ctx", pair)
    own, own_kept, keep_v = run_keep(place, shared, keep_w, w_out, w_value)
    row = 2 * GROUP

    def call(kernel, name, scalars, arrays, out_shape, scratch=()):
        return pl.pallas_call(
            kernel,
            in_specs=[SMEM] * len(scalars) + [VMEM] * len(arrays),
            out_specs=[VMEM] * len(out_shape),
            out_shape=out_shape,
            scratch_shapes=list(scratch),
            compiler_params=small,
            name=name,
        )(*scalars, *arrays)

    def along_x(parts):
        got = {0: parts[0]}
        for d in (2, 1, 3):
            moves = [(j, j - j % row + (j + 2 * d) % row) for j in range(size)]
            got[d] = lax.ppermute(parts[d], "ctx", moves)
        return [got[d] for d in range(GROUP)]

    def early(kept):
        return pl.pallas_call(
            early_kernel, in_specs=[VMEM], out_specs=VMEM, out_shape=shape(GROUP, 3, W, W), name="early",
            compiler_params=pltpu.CompilerParams(vmem_limit_bytes=12 << 20),
            cost_estimate=pl.CostEstimate(flops=1 << 30, bytes_accessed=4 << 20, transcendentals=0),
        )(kept)

    whole = call(join_kernel, "chip_join", (place,), (own, other), [shape(3, W, W)] * GROUP)
    *whole, give_kept, own_kept = lax.optimization_barrier((*whole, give_kept, own_kept))
    *arrived, own_early, give_early = lax.optimization_barrier((*along_x(whole), early(own_kept), early(give_kept)))
    mine, state, grad = call(
        row_kernel, "row_ends", (place,), arrived, [shape(GROUP, 3, W, W), shape(W, W), shape(W, W)]
    )
    state = lax.ppermute(state, "ctx", [(j, (j + row) % size) for j in range(size)])
    grad = lax.ppermute(grad, "ctx", [((j + row) % size, j) for j in range(size)])
    spread = call(
        partial(spread_kernel, size), "row_states", (place,), (mine, state, grad), [shape(2, W, W)] * GROUP, [pltpu.VMEM((GROUP, 2, W, W), F32)]
    )
    own_back, give_back = call(
        part_kernel, "chip_part", (place,), (own, other, *along_x(spread)), [shape(GROUP, 2, W, W)] * 2
    )
    other_back = lax.ppermute(give_back, "ctx", pair)
    before = run_backward(place, side, own_back, own_kept, own_early, beta_t, keep_w, keep_v, ())
    *chunks, grad_d, grads, db = run_backward(place, side, other_back, give_kept, give_early, beta_t, *give_w, before)
    total = run_chunk(side, grads, db, before[0], beta_t, *give_w)
    for d, chunk in zip(ORDER, chunks):
        total = total + lax.ppermute(chunk, "head", [(j, (j + d) % SIDES) for j in range(SIDES)])
    return (total.astype(BF16), grad_d.T)


def solution(mesh):
    placed = (
        P("ctx", None),
        P("ctx", None),
        P(None, "head"),
        P(None, "head"),
        P(None, "head"),
        P(None, "head"),
        P("head", None),
        P("ctx", "head"),
        P(),
    )
    return jax.shard_map(
        per_device,
        mesh=mesh,
        in_specs=placed,
        out_specs=(P("ctx", "head"), P("ctx", "head")),
        check_vma=False,
    )
```

```python
from functools import partial

import jax
import jax.numpy as jnp
from jax import lax
from jax.experimental import pallas as pl
from jax.experimental.pallas import tpu as pltpu
from jax.sharding import PartitionSpec as P

F32 = jnp.float32
BF16 = jnp.bfloat16
W = 128
GROUP = 4
SIDES = 4
HALF = W // 2
NN = (((1,), (0,)), ((), ()))
NT = (((1,), (1,)), ((), ()))
TN = (((0,), (0,)), ((), ()))


def dot(a, b, dims=NN):
    return lax.dot_general(a, b, dims, preferred_element_type=F32)


def exact(a, b, dims=NN):
    return lax.dot_general(a, b, dims, precision=lax.Precision.HIGHEST, preferred_element_type=F32)


def halves(a):
    high = a.astype(BF16)
    return high, (a - high.astype(F32)).astype(BF16)


def mm3(a, b, dims=NN):
    ah, al = halves(a)
    bh, bl = halves(b)
    (ca,), (cb,) = dims[0]
    return dot(jnp.concatenate([ah, al], axis=ca), jnp.concatenate([bh, bh], axis=cb), dims) + dot(ah, bl, dims)


def iotas(shape):
    return lax.broadcasted_iota(jnp.int32, shape, 0), lax.broadcasted_iota(jnp.int32, shape, 1)


def column(array, index):
    lanes = lax.broadcasted_iota(jnp.int32, array.shape, 1)
    return jnp.sum(jnp.where(lanes == index, array, 0.0), axis=1, keepdims=True)


def inverse_all(mixes):
    ti, si = iotas((W, W))
    eye = jnp.where(ti == si, 1.0, 0.0)
    below = jnp.logical_and((ti >> 1) == (si >> 1), ti > si)
    done = [eye - jnp.where(below, a, 0.0) for a in mixes]
    for shift in range(1, 7):
        below = jnp.logical_and((ti >> (shift + 1)) == (si >> (shift + 1)), (ti >> shift) > (si >> shift))
        parts = [jnp.where(below, a, 0.0) for a in mixes]
        inner = [mm3(p, d) for p, d in zip(parts, done)]
        done = [d - mm3(d, i) for d, i in zip(done, inner)]
    return done


def head_columns(head0):
    return pl.ds(pl.multiple_of(head0 * W, GROUP * W), GROUP * W)


def give_kernel(
    place_ref, side_ref, len_hbm, x_hbm, go_hbm, wb_hbm, dec_hbm, wk_hbm, wq_hbm, wo_hbm, wv_hbm, *refs
):
    outs, refs = refs[:2], refs[2:]
    x_ref, go_ref, beta_ref, run_ref, rows_ref, keep_ref, first_ref, wkq_ref, wv_ref, wkq2_ref = refs[:10]
    len_ref, wb_ref, dec_ref, wo_ref, sems = refs[10:]
    keep0 = (place_ref[0] & 1) * GROUP
    head0 = GROUP - keep0
    base = place_ref[0] * W
    at = head_columns(head0)
    at2 = head_columns(keep0)
    pairs = (
        (wk_hbm.at[:, at], wkq_ref.at[0]), (x_hbm, x_ref), (len_hbm, len_ref), (dec_hbm, dec_ref), (wb_hbm, wb_ref),
        (wq_hbm.at[:, at], wkq_ref.at[1]), (wv_hbm.at[:, at], wv_ref), (go_hbm, go_ref), (wo_hbm.at[at, :], wo_ref),
        (wk_hbm.at[:, at2], wkq2_ref.at[0]), (wq_hbm.at[:, at2], wkq2_ref.at[1]),
    )
    gets = [pltpu.make_async_copy(src, dst, sems.at[j]) for j, (src, dst) in enumerate(pairs)]
    for get in (gets[2], gets[3], gets[4], gets[1], gets[0], gets[5], gets[6], gets[7], gets[8], gets[9], gets[10]):
        get.start()
    gets[2].wait()
    ti, si = iotas((W, W))
    begin = jnp.int32(0)
    seg_t = jnp.zeros((W, 1), jnp.int32)
    seg_s = jnp.zeros((1, W), jnp.int32)
    seg_in = jnp.int32(0)
    for j in range(len_ref.shape[0]):
        seg_t = seg_t + (ti[:, :1] + base >= begin).astype(jnp.int32)
        seg_s = seg_s + (si[:1, :] + base >= begin).astype(jnp.int32)
        seg_in = seg_in + (base - 1 >= begin).astype(jnp.int32)
        begin = begin + len_ref[j]
    keep_ref[...] = jnp.where(jnp.logical_and(seg_t == seg_s, ti >= si), 1.0, 0.0)
    lane = iotas(first_ref.shape)[1]
    marked = jnp.where(lane == 0, seg_in, seg_t[W - 1:W, :])
    first_ref[...] = jnp.where(seg_t == marked, 1.0, 0.0)
    gets[3].wait()
    tril = jnp.where(ti >= si, 1.0, 0.0)
    run_ref[...] = exact(tril, dec_ref[...], NT)
    rows_ref[...] = exact(dec_ref[...], tril, NT)
    gets[4].wait()
    gets[1].wait()
    beta_ref[...] = 1.0 / (1.0 + jnp.exp(-dot(x_ref[...], wb_ref[...], NT)))
    block_body(
        head0, x_ref, go_ref, beta_ref, run_ref, rows_ref, keep_ref, first_ref, wkq_ref, wv_ref, wo_ref,
        (gets[0], gets[5], gets[6], gets[7], gets[8]), outs,
    )
    gets[9].wait()
    gets[10].wait()


def keep_kernel(
    place_ref, x_ref, go_ref, beta_ref, run_ref, rows_ref, keep_ref, first_ref, wkq_ref, wo_hbm, wv_hbm, *refs
):
    outs = refs[:2]
    wv_ref, wo_ref, sems = refs[2:]
    head0 = (place_ref[0] & 1) * GROUP
    at = head_columns(head0)
    get_v = pltpu.make_async_copy(wv_hbm.at[:, at], wv_ref, sems.at[0])
    get_o = pltpu.make_async_copy(wo_hbm.at[at, :], wo_ref, sems.at[1])
    get_v.start()
    get_o.start()
    block_body(
        head0, x_ref, go_ref, beta_ref, run_ref, rows_ref, keep_ref, first_ref, wkq_ref, wv_ref, wo_ref,
        (None, None, get_v, None, get_o), outs,
    )


def block_body(
    head0, x_ref, go_ref, beta_ref, run_ref, rows_ref, keep_ref, first_ref, wkq_ref, wv_ref, wo_ref, gets, outs
):
    send_ref, kept_ref = outs

    def ready(*which):
        for j in which:
            if gets[j] is not None:
                gets[j].wait()

    ti, si = iotas((W, W))
    strict = ti > si
    keep = keep_ref[...] > 0.0
    first = first_ref[...][:, :1] > 0.0
    final = first_ref[...][:, 1:2] > 0.0
    beta_all, run_all, run_rows = beta_ref[...], run_ref[...], rows_ref[...]
    heads = range(GROUP)
    cut = lambda a, i: a[:, i * W:(i + 1) * W]
    ready(0)
    x = x_ref[...]
    raw_k = dot(x, wkq_ref[0])
    ready(1)
    raw_q = dot(x, wkq_ref[1])
    total = lambda a: jnp.sum(a, axis=1, keepdims=True)
    heads_at = lax.broadcasted_iota(jnp.int32, run_rows.shape, 0)
    betas = [column(beta_all, head0 + i) for i in heads]
    runs = [column(run_all, head0 + i) for i in heads]
    rows = [jnp.sum(jnp.where(heads_at == head0 + i, run_rows, 0.0), axis=0, keepdims=True) for i in heads]
    spreads = [runs[i] - rows[i] for i in heads]
    weights = [jnp.where(keep, jnp.exp(jnp.where(keep, spread, 0.0)), 0.0) for spread in spreads]
    carries = [jnp.where(first, jnp.exp(run), 0.0) for run in runs]
    closings = [jnp.where(final, jnp.exp(jnp.where(final, run[W - 1:W, :] - run, 0.0)), 0.0) for run in runs]
    rks = [cut(raw_k, i) for i in heads]
    inv_ks = [lax.rsqrt(total(rk * rk) + 1e-06) for rk in rks]
    ks = [rks[i] * inv_ks[i] for i in heads]
    key_keys = [mm3(k, k, NT) for k in ks]
    rqs = [cut(raw_q, i) for i in heads]
    inv_qs = [lax.rsqrt(total(rq * rq) + 1e-06) for rq in rqs]
    qs = [rqs[i] * inv_qs[i] * (W ** -0.5) for i in heads]
    query_keys = [mm3(qs[i], ks[i], NT) for i in heads]
    wkks = [jnp.where(strict, weights[i], 0.0) * key_keys[i] for i in heads]
    mixes = [wkks[i] * betas[i] for i in heads]
    pmats = [weights[i] * query_keys[i] for i in heads]
    for i in heads:
        last = jnp.where(si == 3, inv_ks[i], inv_qs[i])
        kept_ref[i, 10] = jnp.where(si == 0, betas[i], jnp.where(si == 1, carries[i], jnp.where(si == 2, closings[i], last)))
        kept_ref[i, 0] = ks[i]
        kept_ref[i, 1] = qs[i]
        kept_ref[i, 4] = pmats[i]
        kept_ref[i, 6] = wkks[i]
        kept_ref[i, 7] = weights[i]
    solved = inverse_all(mixes)
    ready(2)
    raw_v = dot(x, wv_ref[...])
    ready(3, 4)
    grad_o = dot(go_ref[...], wo_ref[...], NT)
    vs = [cut(raw_v, i) for i in heads]
    dos = [cut(grad_o, i) for i in heads]
    rights = [jnp.concatenate([betas[i] * vs[i], (betas[i] * carries[i]) * ks[i]], axis=1) for i in heads]
    boths = [mm3(solved[i], rights[i]) for i in heads]
    kws = [both[:, W:] for both in boths]
    inner = [mm3(pmats[i], kws[i]) for i in heads]
    flipped = [jnp.concatenate([both[:, W:], both[:, :W]], axis=1) for both in boths]
    ends = [mm3(flipped[i], closings[i] * ks[i], TN) for i in heads]
    effs = [carries[i] * qs[i] - inner[i] for i in heads]
    grads = [mm3(dos[i], effs[i], TN) for i in heads]
    for i in heads:
        kept_ref[i, 5] = solved[i]
        kept_ref[i, 2] = vs[i]
        kept_ref[i, 3] = dos[i]
        kept_ref[i, 8] = boths[i][:, :W]
        kept_ref[i, 9] = kws[i]
        send_ref[i, 0] = jnp.where(ti == si, carries[i][W - 1:W, :], 0.0) - ends[i][:W]
        send_ref[i, 1] = ends[i][W:]
        send_ref[i, 2] = grads[i]


def join_kernel(place_ref, own_ref, other_ref, *out_refs):
    second = (place_ref[0] & 1) == 1
    x = place_ref[0] >> 1
    for d in range(GROUP):
        i = (x + d) & (GROUP - 1)
        out_ref = out_refs[d]
        ta = jnp.where(second, other_ref[i, 0], own_ref[i, 0])
        tb = jnp.where(second, own_ref[i, 0], other_ref[i, 0])
        oa = jnp.where(second, other_ref[i, 1], own_ref[i, 1])
        ob = jnp.where(second, own_ref[i, 1], other_ref[i, 1])
        ga = jnp.where(second, other_ref[i, 2], own_ref[i, 2])
        gb = jnp.where(second, own_ref[i, 2], other_ref[i, 2])
        front = mm3(jnp.concatenate([ta, oa], axis=0), tb)
        out_ref[0] = front[:W]
        out_ref[1] = front[W:] + ob
        out_ref[2] = mm3(gb, ta, NT) + ga


def row_kernel(place_ref, *refs):
    x = place_ref[0] >> 1
    parts, (r_ref, state_ref, grad_ref) = refs[:GROUP], refs[GROUP:]
    for d, part in enumerate(parts):
        r_ref[(x - d) & (GROUP - 1)] = part[...]
    state = r_ref[0, 1]
    grad = r_ref[GROUP - 1, 2]
    for j in range(1, GROUP):
        state = mm3(state, r_ref[j, 0]) + r_ref[j, 1]
        b = GROUP - 1 - j
        grad = mm3(grad, r_ref[b, 0], NT) + r_ref[b, 2]
    state_ref[...] = state
    grad_ref[...] = grad


def spread_kernel(size, place_ref, r_ref, s_ref, g_ref, *refs):
    x = place_ref[0] >> 1
    outs, all_ref = refs[:GROUP], refs[GROUP]
    state = jnp.where(place_ref[0] < 2 * GROUP, 0.0, s_ref[...])
    grad = jnp.where(place_ref[0] >= size - 2 * GROUP, 0.0, g_ref[...])
    all_ref[0, 0] = state
    all_ref[GROUP - 1, 1] = grad
    for j in range(1, GROUP):
        state = mm3(state, r_ref[j - 1, 0]) + r_ref[j - 1, 1]
        all_ref[j, 0] = state
        b = GROUP - j
        grad = mm3(grad, r_ref[b, 0], NT) + r_ref[b, 2]
        all_ref[b - 1, 1] = grad
    for d, out in enumerate(outs):
        out[...] = all_ref[(x + d) & (GROUP - 1)]


def part_kernel(place_ref, own_ref, other_ref, *refs):
    chips, (mine_ref, give_ref) = refs[:GROUP], refs[GROUP:]
    second = (place_ref[0] & 1) == 1
    x = place_ref[0] >> 1
    for d, chip_ref in enumerate(chips):
        i = (x - d) & (GROUP - 1)
        ta = jnp.where(second, other_ref[i, 0], own_ref[i, 0])
        tb = jnp.where(second, own_ref[i, 0], other_ref[i, 0])
        oa = jnp.where(second, other_ref[i, 1], own_ref[i, 1])
        gb = jnp.where(second, own_ref[i, 2], other_ref[i, 2])
        s_in, g_end = chip_ref[0], chip_ref[1]
        s_mid = mm3(s_in, ta) + oa
        g_mid = mm3(g_end, tb, NT) + gb
        mine_ref[i, 0] = jnp.where(second, s_mid, s_in)
        mine_ref[i, 1] = jnp.where(second, g_end, g_mid)
        give_ref[i, 0] = jnp.where(second, s_in, s_mid)
        give_ref[i, 1] = jnp.where(second, g_mid, g_end)


def back_project(side, grads, db, wkq_ref, wv_ref, wb_ref, wide):
    at = pl.ds(pl.multiple_of(side * wide, wide), wide)
    n = grads.shape[1] // 3
    piece = dot(grads[:, :n], wkq_ref[1, at, :], NT) + dot(grads[:, n:2 * n], wkq_ref[0, at, :], NT)
    return piece + dot(grads[:, 2 * n:], wv_ref[at, :], NT) + dot(db, wb_ref[:, at])


def chunk_kernel(distances, side_ref, grads_ref, db_ref, before_ref, wb_ref, wkq_ref, wv_ref, *out_refs):
    for d, out_ref in zip(distances, out_refs):
        side = (side_ref[0] + d) & (SIDES - 1)
        piece = back_project(side, grads_ref[...], db_ref[...], wkq_ref, wv_ref, wb_ref, out_ref.shape[1])
        out_ref[...] = before_ref[d] + piece


def relay_kernel(next_ref, last_ref, up_ref, down_ref, next_out, last_out):
    next_out[:HALF] = next_ref[:HALF] + up_ref[...]
    next_out[HALF:] = next_ref[HALF:]
    last_out[:HALF] = last_ref[:HALF]
    last_out[HALF:] = last_ref[HALF:] + down_ref[...]


def early_kernel(kept_ref, out_ref):
    heads = range(GROUP)
    k, do, uv = ([kept_ref[i, j] for i in heads] for j in (0, 3, 8))
    ends = [kept_ref[i, 10][:, 2:3] * k[i] for i in heads]
    inner = [mm3(kept_ref[i, 4], do[i], TN) for i in heads]
    both = [mm3(kept_ref[i, 5], jnp.concatenate([inner[i], ends[i]], axis=1), TN) for i in heads]
    for i in heads:
        out_ref[i, 0] = both[i][:, :W]
        out_ref[i, 1] = both[i][:, W:]
        out_ref[i, 2] = mm3(do[i], uv[i], NT)


def second_kernel(chained, *refs):
    place_ref, side_ref, back_ref, kept_ref, early_ref, wb_ref, wkq_ref, wv_ref = refs[:8]
    refs = refs[8:]
    if chained:
        before_ref, gd_before_ref, up_ref, down_ref, gd_ref, grads_ref, db_ref = refs
        wide = up_ref.shape[-1]
    else:
        total_ref, gd_ref = refs
        wide = total_ref.shape[-1]
    keep0 = (place_ref[0] & 1) * GROUP
    head0 = GROUP - keep0 if chained else keep0
    side = side_ref[0]
    ti, si = iotas((W, W))
    strict = ti > si
    upper = jnp.where(si >= ti, 1.0, 0.0)
    t8, h8 = iotas((W, 8))
    none = jnp.zeros((W, 8), F32)
    heads = range(GROUP)
    s0, g1 = ([back_ref[i, j] for i in heads] for j in range(2))
    k, q, v, do, pmat, wkk, weight, uv, kw, col = ([kept_ref[i, j] for i in heads] for j in (0, 1, 2, 3, 4, 6, 7, 8, 9, 10))
    beta, carried, closing, inv_k, inv_q = ([c[:, j:j + 1] for c in col] for j in range(5))
    dr = [early_ref[i, 0] + mm3(early_ref[i, 1], g1[i], NT) for i in heads]
    u = [uv[i] - mm3(kw[i], s0[i], NT) for i in heads]
    ds = [mm3(jnp.concatenate([do[i], dr[i]], axis=0), s0[i]) for i in heads]
    da = [-mm3(dr[i], u[i], NT) for i in heads]
    ug = [closing[i] * mm3(u[i], g1[i]) for i in heads]
    dp = [early_ref[i, 2] - mm3(ds[i][:W], kw[i], NT) for i in heads]
    dkk = [jnp.where(strict, weight[i], 0.0) * da[i] * beta[i] for i in heads]
    dqk = [weight[i] * dp[i] for i in heads]
    pairs = [halves(dp[i] * pmat[i] + da[i] * wkk[i] * beta[i]) for i in heads]
    ub = upper.astype(BF16)
    front = [mm3(jnp.concatenate([dqk[i], dkk[i]], axis=0), k[i]) for i in heads]
    under = [mm3(jnp.concatenate([dkk[i], dqk[i]], axis=0), jnp.concatenate([k[i], q[i]], axis=0), TN) for i in heads]
    across = [dot(ub, high) + dot(ub, low) for high, low in pairs]
    dq_state = [carried[i] * ds[i][:W] for i in heads]
    dr_s = [carried[i] * ds[i][W:] for i in heads]
    total = lambda a: jnp.sum(a, axis=1, keepdims=True)
    known = [total(dr_s[i] * k[i]) for i in heads]
    dbeta = [total(dr[i] * v[i] + da[i] * wkk[i]) - known[i] for i in heads]
    evec = [total(jnp.where(strict, across[i], 0.0)) for i in heads]
    fvec = [total(ug[i] * k[i]) for i in heads]
    cvec = [total(dq_state[i] * q[i]) - beta[i] * known[i] for i in heads]
    ends = [carried[i][W - 1:W, :] * jnp.sum(total(g1[i] * s0[i]), axis=0, keepdims=True) for i in heads]
    cvec = [cvec[i] + jnp.where(t8[:, :1] == W - 1, ends[i], 0.0) for i in heads]
    dq = [front[i][:W] + dq_state[i] for i in heads]
    dk = [front[i][W:] + under[i] - beta[i] * dr_s[i] + ug[i] for i in heads]
    along_k = [total(k[i] * dk[i]) for i in heads]
    along_q = [total(q[i] * dq[i]) for i in heads]
    gks = [(inv_k[i] * (dk[i] - k[i] * along_k[i])).astype(BF16) for i in heads]
    gqs = [((inv_q[i] * (W ** -0.5)) * (dq[i] - (q[i] * float(W)) * along_q[i])).astype(BF16) for i in heads]
    gvs = [(beta[i] * dr[i]).astype(BF16) for i in heads]
    cterm, fterm, eterm, dball = none, none, none, none
    for i in heads:
        here = h8 == head0 + i
        cterm = jnp.where(here, cvec[i], cterm)
        fterm = jnp.where(here, fvec[i], fterm)
        eterm = jnp.where(here, evec[i], eterm)
        dball = jnp.where(here, dbeta[i] * beta[i] * (1.0 - beta[i]), dball)
    grads = jnp.concatenate(gqs + gks + gvs, axis=1)
    db = dball.astype(BF16)
    project = lambda d: back_project((side + d) & (SIDES - 1), grads, db, wkq_ref, wv_ref, wb_ref, wide)
    if chained:
        far = before_ref[2] + project(2)
        up_ref[...] = far[:HALF]
        down_ref[...] = far[HALF:]
        grads_ref[...] = grads
        db_ref[...] = db
    else:
        for d in range(SIDES):
            total_ref[d] = project(d)
    eye = jnp.where(ti == si, 1.0, 0.0)
    terms = jnp.concatenate([cterm, fterm, eterm], axis=0)
    top = terms.astype(BF16)
    middle, bottom = halves(terms - top.astype(F32))
    sums = dot(jnp.concatenate([top, middle, bottom], axis=1), jnp.concatenate([jnp.where(ti >= si, 1.0, 0.0), jnp.where(si > ti, 1.0, 0.0), eye], axis=0).astype(BF16), TN)
    decays = sums[:8] + sums[8:16] + sums[16:]
    gd_ref[...] = gd_before_ref[...] + decays if chained else decays


SMEM = pl.BlockSpec(memory_space=pltpu.SMEM)
VMEM = pl.BlockSpec(memory_space=pltpu.VMEM)
HBM = pl.BlockSpec(memory_space=pltpu.HBM)


def shape(*dims):
    return jax.ShapeDtypeStruct(dims, F32)


def in_hbm(*arrays):
    return [pltpu.with_memory_space_constraint(a, pltpu.HBM) for a in arrays]


def block_shapes():
    return [shape(GROUP, 3, W, W), shape(GROUP, 11, W, W)]


def run_give(place, side, lengths, inputs, grad_out, beta_t, decay_t, w_key, w_query, w_out, w_value):
    rows, width = inputs.shape
    heads, span = beta_t.shape[0], GROUP * W
    wide = jax.ShapeDtypeStruct((rows, width), BF16)
    tall = jax.ShapeDtypeStruct((width, span), BF16)
    two = jax.ShapeDtypeStruct((2, width, span), BF16)
    out = pl.pallas_call(
        give_kernel,
        in_specs=[SMEM] * 2 + [HBM] * 9,
        out_specs=[VMEM] * 12,
        out_shape=block_shapes() + [wide, wide, shape(rows, heads), shape(rows, heads), shape(heads, rows), shape(W, W), shape(W, heads)] + [two, tall, two],
        scratch_shapes=[
            pltpu.SMEM(lengths.shape, jnp.int32), pltpu.VMEM(beta_t.shape, BF16), pltpu.VMEM(decay_t.shape, F32),
            pltpu.VMEM((span, width), BF16), pltpu.SemaphoreType.DMA((11,)),
        ],
        compiler_params=pltpu.CompilerParams(vmem_limit_bytes=28 << 20),
        name="block_forward_give",
    )(place, side, *in_hbm(lengths, inputs, grad_out, beta_t, decay_t, w_key, w_query, w_out, w_value))
    return out[0], out[1], out[2:9], out[9:11], out[11]


def run_keep(place, shared, w_keep, w_out, w_value):
    _, width, span = w_keep.shape
    out = pl.pallas_call(
        keep_kernel,
        in_specs=[SMEM] + [VMEM] * 8 + [HBM] * 2,
        out_specs=[VMEM] * 3,
        out_shape=block_shapes() + [jax.ShapeDtypeStruct((width, span), BF16)],
        scratch_shapes=[pltpu.VMEM((span, width), BF16), pltpu.SemaphoreType.DMA((2,))],
        compiler_params=pltpu.CompilerParams(vmem_limit_bytes=24 << 20),
        name="block_forward_keep",
    )(place, *shared, w_keep, *in_hbm(w_out, w_value))
    return out


def run_backward(place, side, back, kept, early, beta_t, w_both, w_value, before):
    heads, width = beta_t.shape
    wide = width // SIDES
    if before:
        out_shape = [shape(HALF, wide)] * 2 + [shape(heads, W), jax.ShapeDtypeStruct((W, 3 * GROUP * W), BF16), jax.ShapeDtypeStruct((W, heads), BF16)]
    else:
        out_shape = [shape(SIDES, W, wide), shape(heads, W)]
    return pl.pallas_call(
        partial(second_kernel, bool(before)),
        in_specs=[SMEM] * 2 + [VMEM] * 6 + [VMEM] * len(before),
        out_specs=[VMEM] * len(out_shape),
        out_shape=out_shape,
        compiler_params=pltpu.CompilerParams(vmem_limit_bytes=24 << 20),
        name="block_backward",
    )(place, side, back, kept, early, beta_t, w_both, w_value, *before)


def run_chunk(distances, side, grads, db, before, beta_t, w_both, w_value):
    return pl.pallas_call(
        partial(chunk_kernel, distances),
        in_specs=[SMEM] + [VMEM] * 6,
        out_specs=[VMEM] * len(distances),
        out_shape=[shape(*before.shape[1:])] * len(distances),
        compiler_params=pltpu.CompilerParams(vmem_limit_bytes=16 << 20),
        name="near_chunks" if len(distances) > 1 else "own_chunk",
    )(side, grads, db, before, beta_t, w_both, w_value)


def per_device(inputs, grad_out, w_query, w_key, w_value, w_beta, w_out, log_decay, lengths):
    size = lax.axis_size("ctx")
    place = lax.axis_index("ctx").astype(jnp.int32).reshape(1)
    side = lax.axis_index("head").astype(jnp.int32).reshape(1)
    beta_t, decay_t = w_beta.T, log_decay.T
    small = pltpu.CompilerParams(vmem_limit_bytes=8 << 20)

    pair = [(j, j ^ 1) for j in range(size)]
    give, give_kept, shared, give_w, keep_w = run_give(
        place, side, lengths, inputs, grad_out, beta_t, decay_t, w_key, w_query, w_out, w_value
    )
    other = lax.ppermute(give, "ctx", pair)
    own, own_kept, keep_v = run_keep(place, shared, keep_w, w_out, w_value)
    row = 2 * GROUP

    def call(kernel, name, scalars, arrays, out_shape, scratch=()):
        return pl.pallas_call(
            kernel,
            in_specs=[SMEM] * len(scalars) + [VMEM] * len(arrays),
            out_specs=[VMEM] * len(out_shape),
            out_shape=out_shape,
            scratch_shapes=list(scratch),
            compiler_params=small,
            name=name,
        )(*scalars, *arrays)

    def along_x(parts):
        got = {0: parts[0]}
        for d in (2, 1, 3):
            moves = [(j, j - j % row + (j + 2 * d) % row) for j in range(size)]
            got[d] = lax.ppermute(parts[d], "ctx", moves)
        return [got[d] for d in range(GROUP)]

    def early(kept):
        return pl.pallas_call(
            early_kernel, in_specs=[VMEM], out_specs=VMEM, out_shape=shape(GROUP, 3, W, W), name="early",
            compiler_params=pltpu.CompilerParams(vmem_limit_bytes=12 << 20),
            cost_estimate=pl.CostEstimate(flops=1 << 30, bytes_accessed=4 << 20, transcendentals=0),
        )(kept)

    whole = call(join_kernel, "chip_join", (place,), (own, other), [shape(3, W, W)] * GROUP)
    *whole, give_kept, own_kept = lax.optimization_barrier((*whole, give_kept, own_kept))
    *arrived, own_early, give_early = lax.optimization_barrier((*along_x(whole), early(own_kept), early(give_kept)))
    mine, state, grad = call(
        row_kernel, "row_ends", (place,), arrived, [shape(GROUP, 3, W, W), shape(W, W), shape(W, W)]
    )
    state = lax.ppermute(state, "ctx", [(j, (j + row) % size) for j in range(size)])
    grad = lax.ppermute(grad, "ctx", [((j + row) % size, j) for j in range(size)])
    spread = call(
        partial(spread_kernel, size), "row_states", (place,), (mine, state, grad), [shape(2, W, W)] * GROUP, [pltpu.VMEM((GROUP, 2, W, W), F32)]
    )
    own_back, give_back = call(
        part_kernel, "chip_part", (place,), (own, other, *along_x(spread)), [shape(GROUP, 2, W, W)] * 2
    )
    other_back = lax.ppermute(give_back, "ctx", pair)
    before = run_backward(place, side, own_back, own_kept, own_early, beta_t, keep_w, keep_v, ())
    up, down, grad_d, grads, db = run_backward(place, side, other_back, give_kept, give_early, beta_t, *give_w, before)
    after = [(j, (j + 1) % SIDES) for j in range(SIDES)]
    ahead = [((j + 1) % SIDES, j) for j in range(SIDES)]
    near = run_chunk((1, 3), side, grads, db, before[0], beta_t, *give_w)
    halfway = (*near, lax.ppermute(up, "head", after), lax.ppermute(down, "head", ahead))
    near = call(relay_kernel, "relay", (), lax.optimization_barrier(halfway), [shape(*near[0].shape)] * 2)
    *near, grads = lax.optimization_barrier((*near, grads))
    (total,) = run_chunk((0,), side, grads, db, before[0], beta_t, *give_w)
    total = total + lax.ppermute(near[0], "head", after) + lax.ppermute(near[1], "head", ahead)
    return (total.astype(BF16), grad_d.T)


def solution(mesh):
    placed = (
        P("ctx", None),
        P("ctx", None),
        P(None, "head"),
        P(None, "head"),
        P(None, "head"),
        P(None, "head"),
        P("head", None),
        P("ctx", "head"),
        P(),
    )
    return jax.shard_map(
        per_device,
        mesh=mesh,
        in_specs=placed,
        out_specs=(P("ctx", "head"), P("ctx", "head")),
        check_vma=False,
    )
```

```python
from functools import partial

import jax
import jax.numpy as jnp
from jax import lax
from jax.experimental import pallas as pl
from jax.experimental.pallas import tpu as pltpu
from jax.sharding import PartitionSpec as P

F32 = jnp.float32
BF16 = jnp.bfloat16
W = 128
GROUP = 4
SIDES = 4
HALF = W // 2
NN = (((1,), (0,)), ((), ()))
NT = (((1,), (1,)), ((), ()))
TN = (((0,), (0,)), ((), ()))


def dot(a, b, dims=NN):
    return lax.dot_general(a, b, dims, preferred_element_type=F32)


def exact(a, b, dims=NN):
    return lax.dot_general(a, b, dims, precision=lax.Precision.HIGHEST, preferred_element_type=F32)


def halves(a):
    high = a.astype(BF16)
    return high, (a - high.astype(F32)).astype(BF16)


def mm3(a, b, dims=NN):
    ah, al = halves(a)
    bh, bl = halves(b)
    (ca,), (cb,) = dims[0]
    return dot(jnp.concatenate([ah, al], axis=ca), jnp.concatenate([bh, bh], axis=cb), dims) + dot(ah, bl, dims)


def iotas(shape):
    return lax.broadcasted_iota(jnp.int32, shape, 0), lax.broadcasted_iota(jnp.int32, shape, 1)


def column(array, index):
    lanes = lax.broadcasted_iota(jnp.int32, array.shape, 1)
    return jnp.sum(jnp.where(lanes == index, array, 0.0), axis=1, keepdims=True)


def inverse_all(mixes):
    ti, si = iotas((W, W))
    eye = jnp.where(ti == si, 1.0, 0.0)
    below = jnp.logical_and((ti >> 1) == (si >> 1), ti > si)
    done = [eye - jnp.where(below, a, 0.0) for a in mixes]
    for shift in range(1, 7):
        below = jnp.logical_and((ti >> (shift + 1)) == (si >> (shift + 1)), (ti >> shift) > (si >> shift))
        parts = [jnp.where(below, a, 0.0) for a in mixes]
        inner = [mm3(p, d) for p, d in zip(parts, done)]
        done = [d - mm3(d, i) for d, i in zip(done, inner)]
    return done


def head_columns(head0):
    return pl.ds(pl.multiple_of(head0 * W, GROUP * W), GROUP * W)


def give_kernel(
    place_ref, side_ref, len_hbm, x_hbm, go_hbm, wb_hbm, dec_hbm, wk_hbm, wq_hbm, wo_hbm, wv_hbm, *refs
):
    outs, refs = refs[:2], refs[2:]
    x_ref, go_ref, beta_ref, run_ref, rows_ref, keep_ref, first_ref, wkq_ref, wv_ref, wkq2_ref = refs[:10]
    len_ref, wb_ref, dec_ref, wo_ref, sems = refs[10:]
    keep0 = (place_ref[0] & 1) * GROUP
    head0 = GROUP - keep0
    base = place_ref[0] * W
    at = head_columns(head0)
    at2 = head_columns(keep0)
    pairs = (
        (wk_hbm.at[:, at], wkq_ref.at[0]), (x_hbm, x_ref), (len_hbm, len_ref), (dec_hbm, dec_ref), (wb_hbm, wb_ref),
        (wq_hbm.at[:, at], wkq_ref.at[1]), (wv_hbm.at[:, at], wv_ref), (go_hbm, go_ref), (wo_hbm.at[at, :], wo_ref),
        (wk_hbm.at[:, at2], wkq2_ref.at[0]), (wq_hbm.at[:, at2], wkq2_ref.at[1]),
    )
    gets = [pltpu.make_async_copy(src, dst, sems.at[j]) for j, (src, dst) in enumerate(pairs)]
    for get in (gets[2], gets[3], gets[4], gets[1], gets[0], gets[5], gets[6], gets[7], gets[8], gets[9], gets[10]):
        get.start()
    gets[2].wait()
    ti, si = iotas((W, W))
    begin = jnp.int32(0)
    seg_t = jnp.zeros((W, 1), jnp.int32)
    seg_s = jnp.zeros((1, W), jnp.int32)
    seg_in = jnp.int32(0)
    for j in range(len_ref.shape[0]):
        seg_t = seg_t + (ti[:, :1] + base >= begin).astype(jnp.int32)
        seg_s = seg_s + (si[:1, :] + base >= begin).astype(jnp.int32)
        seg_in = seg_in + (base - 1 >= begin).astype(jnp.int32)
        begin = begin + len_ref[j]
    keep_ref[...] = jnp.where(jnp.logical_and(seg_t == seg_s, ti >= si), 1.0, 0.0)
    lane = iotas(first_ref.shape)[1]
    marked = jnp.where(lane == 0, seg_in, seg_t[W - 1:W, :])
    first_ref[...] = jnp.where(seg_t == marked, 1.0, 0.0)
    gets[3].wait()
    tril = jnp.where(ti >= si, 1.0, 0.0)
    run_ref[...] = exact(tril, dec_ref[...], NT)
    rows_ref[...] = exact(dec_ref[...], tril, NT)
    gets[4].wait()
    gets[1].wait()
    beta_ref[...] = 1.0 / (1.0 + jnp.exp(-dot(x_ref[...], wb_ref[...], NT)))
    block_body(
        head0, x_ref, go_ref, beta_ref, run_ref, rows_ref, keep_ref, first_ref, wkq_ref, wv_ref, wo_ref,
        (gets[0], gets[5], gets[6], gets[7], gets[8]), outs,
    )
    gets[9].wait()
    gets[10].wait()


def keep_kernel(
    place_ref, x_ref, go_ref, beta_ref, run_ref, rows_ref, keep_ref, first_ref, wkq_ref, wo_hbm, wv_hbm, *refs
):
    outs = refs[:2]
    wv_ref, wo_ref, sems = refs[2:]
    head0 = (place_ref[0] & 1) * GROUP
    at = head_columns(head0)
    get_v = pltpu.make_async_copy(wv_hbm.at[:, at], wv_ref, sems.at[0])
    get_o = pltpu.make_async_copy(wo_hbm.at[at, :], wo_ref, sems.at[1])
    get_v.start()
    get_o.start()
    block_body(
        head0, x_ref, go_ref, beta_ref, run_ref, rows_ref, keep_ref, first_ref, wkq_ref, wv_ref, wo_ref,
        (None, None, get_v, None, get_o), outs,
    )


def block_body(
    head0, x_ref, go_ref, beta_ref, run_ref, rows_ref, keep_ref, first_ref, wkq_ref, wv_ref, wo_ref, gets, outs
):
    send_ref, kept_ref = outs

    def ready(*which):
        for j in which:
            if gets[j] is not None:
                gets[j].wait()

    ti, si = iotas((W, W))
    strict = ti > si
    keep = keep_ref[...] > 0.0
    first = first_ref[...][:, :1] > 0.0
    final = first_ref[...][:, 1:2] > 0.0
    beta_all, run_all, run_rows = beta_ref[...], run_ref[...], rows_ref[...]
    heads = range(GROUP)
    cut = lambda a, i: a[:, i * W:(i + 1) * W]
    ready(0)
    x = x_ref[...]
    raw_k = dot(x, wkq_ref[0])
    ready(1)
    raw_q = dot(x, wkq_ref[1])
    total = lambda a: jnp.sum(a, axis=1, keepdims=True)
    heads_at = lax.broadcasted_iota(jnp.int32, run_rows.shape, 0)
    betas = [column(beta_all, head0 + i) for i in heads]
    runs = [column(run_all, head0 + i) for i in heads]
    rows = [jnp.sum(jnp.where(heads_at == head0 + i, run_rows, 0.0), axis=0, keepdims=True) for i in heads]
    spreads = [runs[i] - rows[i] for i in heads]
    weights = [jnp.where(keep, jnp.exp(jnp.where(keep, spread, 0.0)), 0.0) for spread in spreads]
    carries = [jnp.where(first, jnp.exp(run), 0.0) for run in runs]
    closings = [jnp.where(final, jnp.exp(jnp.where(final, run[W - 1:W, :] - run, 0.0)), 0.0) for run in runs]
    rks = [cut(raw_k, i) for i in heads]
    inv_ks = [lax.rsqrt(total(rk * rk) + 1e-06) for rk in rks]
    ks = [rks[i] * inv_ks[i] for i in heads]
    key_keys = [mm3(k, k, NT) for k in ks]
    rqs = [cut(raw_q, i) for i in heads]
    inv_qs = [lax.rsqrt(total(rq * rq) + 1e-06) for rq in rqs]
    qs = [rqs[i] * inv_qs[i] * (W ** -0.5) for i in heads]
    query_keys = [mm3(qs[i], ks[i], NT) for i in heads]
    wkks = [jnp.where(strict, weights[i], 0.0) * key_keys[i] for i in heads]
    mixes = [wkks[i] * betas[i] for i in heads]
    pmats = [weights[i] * query_keys[i] for i in heads]
    for i in heads:
        last = jnp.where(si == 3, inv_ks[i], inv_qs[i])
        kept_ref[i, 10] = jnp.where(si == 0, betas[i], jnp.where(si == 1, carries[i], jnp.where(si == 2, closings[i], last)))
        kept_ref[i, 0] = ks[i]
        kept_ref[i, 1] = qs[i]
        kept_ref[i, 4] = pmats[i]
        kept_ref[i, 6] = wkks[i]
        kept_ref[i, 7] = weights[i]
    solved = inverse_all(mixes)
    ready(2)
    raw_v = dot(x, wv_ref[...])
    ready(3, 4)
    grad_o = dot(go_ref[...], wo_ref[...], NT)
    vs = [cut(raw_v, i) for i in heads]
    dos = [cut(grad_o, i) for i in heads]
    rights = [jnp.concatenate([betas[i] * vs[i], (betas[i] * carries[i]) * ks[i]], axis=1) for i in heads]
    boths = [mm3(solved[i], rights[i]) for i in heads]
    kws = [both[:, W:] for both in boths]
    inner = [mm3(pmats[i], kws[i]) for i in heads]
    flipped = [jnp.concatenate([both[:, W:], both[:, :W]], axis=1) for both in boths]
    ends = [mm3(flipped[i], closings[i] * ks[i], TN) for i in heads]
    effs = [carries[i] * qs[i] - inner[i] for i in heads]
    grads = [mm3(dos[i], effs[i], TN) for i in heads]
    for i in heads:
        kept_ref[i, 5] = solved[i]
        kept_ref[i, 2] = vs[i]
        kept_ref[i, 3] = dos[i]
        kept_ref[i, 8] = boths[i][:, :W]
        kept_ref[i, 9] = kws[i]
        send_ref[i, 0] = jnp.where(ti == si, carries[i][W - 1:W, :], 0.0) - ends[i][:W]
        send_ref[i, 1] = ends[i][W:]
        send_ref[i, 2] = grads[i]


def join_kernel(place_ref, own_ref, other_ref, *out_refs):
    second = (place_ref[0] & 1) == 1
    x = place_ref[0] >> 1
    for d in range(GROUP):
        i = (x + d) & (GROUP - 1)
        out_ref = out_refs[d]
        ta = jnp.where(second, other_ref[i, 0], own_ref[i, 0])
        tb = jnp.where(second, own_ref[i, 0], other_ref[i, 0])
        oa = jnp.where(second, other_ref[i, 1], own_ref[i, 1])
        ob = jnp.where(second, own_ref[i, 1], other_ref[i, 1])
        ga = jnp.where(second, other_ref[i, 2], own_ref[i, 2])
        gb = jnp.where(second, own_ref[i, 2], other_ref[i, 2])
        front = mm3(jnp.concatenate([ta, oa], axis=0), tb)
        out_ref[0] = front[:W]
        out_ref[1] = front[W:] + ob
        out_ref[2] = mm3(gb, ta, NT) + ga


def row_kernel(place_ref, *refs):
    x = place_ref[0] >> 1
    parts, (r_ref, state_ref, grad_ref) = refs[:GROUP], refs[GROUP:]
    for d, part in enumerate(parts):
        r_ref[(x - d) & (GROUP - 1)] = part[...]
    state = r_ref[0, 1]
    grad = r_ref[GROUP - 1, 2]
    for j in range(1, GROUP):
        state = mm3(state, r_ref[j, 0]) + r_ref[j, 1]
        b = GROUP - 1 - j
        grad = mm3(grad, r_ref[b, 0], NT) + r_ref[b, 2]
    state_ref[...] = state
    grad_ref[...] = grad


def spread_kernel(size, place_ref, r_ref, s_ref, g_ref, *refs):
    x = place_ref[0] >> 1
    outs, all_ref = refs[:GROUP], refs[GROUP]
    state = jnp.where(place_ref[0] < 2 * GROUP, 0.0, s_ref[...])
    grad = jnp.where(place_ref[0] >= size - 2 * GROUP, 0.0, g_ref[...])
    all_ref[0, 0] = state
    all_ref[GROUP - 1, 1] = grad
    for j in range(1, GROUP):
        state = mm3(state, r_ref[j - 1, 0]) + r_ref[j - 1, 1]
        all_ref[j, 0] = state
        b = GROUP - j
        grad = mm3(grad, r_ref[b, 0], NT) + r_ref[b, 2]
        all_ref[b - 1, 1] = grad
    for d, out in enumerate(outs):
        out[...] = all_ref[(x + d) & (GROUP - 1)]


def part_kernel(place_ref, own_ref, other_ref, *refs):
    chips, (mine_ref, give_ref) = refs[:GROUP], refs[GROUP:]
    second = (place_ref[0] & 1) == 1
    x = place_ref[0] >> 1
    for d, chip_ref in enumerate(chips):
        i = (x - d) & (GROUP - 1)
        ta = jnp.where(second, other_ref[i, 0], own_ref[i, 0])
        tb = jnp.where(second, own_ref[i, 0], other_ref[i, 0])
        oa = jnp.where(second, other_ref[i, 1], own_ref[i, 1])
        gb = jnp.where(second, own_ref[i, 2], other_ref[i, 2])
        s_in, g_end = chip_ref[0], chip_ref[1]
        s_mid = mm3(s_in, ta) + oa
        g_mid = mm3(g_end, tb, NT) + gb
        mine_ref[i, 0] = jnp.where(second, s_mid, s_in)
        mine_ref[i, 1] = jnp.where(second, g_end, g_mid)
        give_ref[i, 0] = jnp.where(second, s_in, s_mid)
        give_ref[i, 1] = jnp.where(second, g_mid, g_end)


def back_project(side, grads, db, wkq_ref, wv_ref, wb_ref, wide):
    at = pl.ds(pl.multiple_of(side * wide, wide), wide)
    n = grads.shape[1] // 3
    piece = dot(grads[:, :n], wkq_ref[1, at, :], NT) + dot(grads[:, n:2 * n], wkq_ref[0, at, :], NT)
    return piece + dot(grads[:, 2 * n:], wv_ref[at, :], NT) + dot(db, wb_ref[:, at])


def chunk_kernel(distances, side_ref, wb_ref, *refs):
    parts = (refs[:4], refs[4:8])
    for d, out_ref in zip(distances, refs[8:]):
        side = (side_ref[0] + d) & (SIDES - 1)
        pieces = [
            back_project(side, grads_ref[...], db_ref[...], wkq_ref, wv_ref, wb_ref, out_ref.shape[1])
            for grads_ref, db_ref, wkq_ref, wv_ref in parts
        ]
        out_ref[...] = pieces[0] + pieces[1]


def relay_kernel(next_ref, last_ref, up_ref, down_ref, next_out, last_out):
    next_out[:HALF] = next_ref[:HALF] + up_ref[...]
    next_out[HALF:] = next_ref[HALF:]
    last_out[:HALF] = last_ref[:HALF]
    last_out[HALF:] = last_ref[HALF:] + down_ref[...]


def early_kernel(kept_ref, out_ref):
    heads = range(GROUP)
    k, do, uv = ([kept_ref[i, j] for i in heads] for j in (0, 3, 8))
    ends = [kept_ref[i, 10][:, 2:3] * k[i] for i in heads]
    inner = [mm3(kept_ref[i, 4], do[i], TN) for i in heads]
    both = [mm3(kept_ref[i, 5], jnp.concatenate([inner[i], ends[i]], axis=1), TN) for i in heads]
    for i in heads:
        out_ref[i, 0] = both[i][:, :W]
        out_ref[i, 1] = both[i][:, W:]
        out_ref[i, 2] = mm3(do[i], uv[i], NT)


def second_kernel(chained, *refs):
    place_ref, side_ref, back_ref, kept_ref, early_ref, wb_ref, wkq_ref, wv_ref = refs[:8]
    refs = refs[8:]
    if chained:
        before_ref, gd_before_ref, up_ref, down_ref, gd_ref, grads_ref, db_ref = refs
        wide = up_ref.shape[-1]
    else:
        total_ref, gd_ref, grads_ref, db_ref = refs
        wide = total_ref.shape[-1]
    keep0 = (place_ref[0] & 1) * GROUP
    head0 = GROUP - keep0 if chained else keep0
    side = side_ref[0]
    ti, si = iotas((W, W))
    strict = ti > si
    upper = jnp.where(si >= ti, 1.0, 0.0)
    t8, h8 = iotas((W, 8))
    none = jnp.zeros((W, 8), F32)
    heads = range(GROUP)
    s0, g1 = ([back_ref[i, j] for i in heads] for j in range(2))
    k, q, v, do, pmat, wkk, weight, uv, kw, col = ([kept_ref[i, j] for i in heads] for j in (0, 1, 2, 3, 4, 6, 7, 8, 9, 10))
    beta, carried, closing, inv_k, inv_q = ([c[:, j:j + 1] for c in col] for j in range(5))
    dr = [early_ref[i, 0] + mm3(early_ref[i, 1], g1[i], NT) for i in heads]
    u = [uv[i] - mm3(kw[i], s0[i], NT) for i in heads]
    ds = [mm3(jnp.concatenate([do[i], dr[i]], axis=0), s0[i]) for i in heads]
    da = [-mm3(dr[i], u[i], NT) for i in heads]
    ug = [closing[i] * mm3(u[i], g1[i]) for i in heads]
    dp = [early_ref[i, 2] - mm3(ds[i][:W], kw[i], NT) for i in heads]
    dkk = [jnp.where(strict, weight[i], 0.0) * da[i] * beta[i] for i in heads]
    dqk = [weight[i] * dp[i] for i in heads]
    pairs = [halves(dp[i] * pmat[i] + da[i] * wkk[i] * beta[i]) for i in heads]
    ub = upper.astype(BF16)
    front = [mm3(jnp.concatenate([dqk[i], dkk[i]], axis=0), k[i]) for i in heads]
    under = [mm3(jnp.concatenate([dkk[i], dqk[i]], axis=0), jnp.concatenate([k[i], q[i]], axis=0), TN) for i in heads]
    across = [dot(ub, high) + dot(ub, low) for high, low in pairs]
    dq_state = [carried[i] * ds[i][:W] for i in heads]
    dr_s = [carried[i] * ds[i][W:] for i in heads]
    total = lambda a: jnp.sum(a, axis=1, keepdims=True)
    known = [total(dr_s[i] * k[i]) for i in heads]
    dbeta = [total(dr[i] * v[i] + da[i] * wkk[i]) - known[i] for i in heads]
    evec = [total(jnp.where(strict, across[i], 0.0)) for i in heads]
    fvec = [total(ug[i] * k[i]) for i in heads]
    cvec = [total(dq_state[i] * q[i]) - beta[i] * known[i] for i in heads]
    ends = [carried[i][W - 1:W, :] * jnp.sum(total(g1[i] * s0[i]), axis=0, keepdims=True) for i in heads]
    cvec = [cvec[i] + jnp.where(t8[:, :1] == W - 1, ends[i], 0.0) for i in heads]
    dq = [front[i][:W] + dq_state[i] for i in heads]
    dk = [front[i][W:] + under[i] - beta[i] * dr_s[i] + ug[i] for i in heads]
    along_k = [total(k[i] * dk[i]) for i in heads]
    along_q = [total(q[i] * dq[i]) for i in heads]
    gks = [(inv_k[i] * (dk[i] - k[i] * along_k[i])).astype(BF16) for i in heads]
    gqs = [((inv_q[i] * (W ** -0.5)) * (dq[i] - (q[i] * float(W)) * along_q[i])).astype(BF16) for i in heads]
    gvs = [(beta[i] * dr[i]).astype(BF16) for i in heads]
    cterm, fterm, eterm, dball = none, none, none, none
    for i in heads:
        here = h8 == head0 + i
        cterm = jnp.where(here, cvec[i], cterm)
        fterm = jnp.where(here, fvec[i], fterm)
        eterm = jnp.where(here, evec[i], eterm)
        dball = jnp.where(here, dbeta[i] * beta[i] * (1.0 - beta[i]), dball)
    grads = jnp.concatenate(gqs + gks + gvs, axis=1)
    db = dball.astype(BF16)
    project = lambda d: back_project((side + d) & (SIDES - 1), grads, db, wkq_ref, wv_ref, wb_ref, wide)
    grads_ref[...] = grads
    db_ref[...] = db
    if chained:
        far = before_ref[...] + project(2)
        up_ref[...] = far[:HALF]
        down_ref[...] = far[HALF:]
    else:
        total_ref[...] = project(2)
    eye = jnp.where(ti == si, 1.0, 0.0)
    terms = jnp.concatenate([cterm, fterm, eterm], axis=0)
    top = terms.astype(BF16)
    middle, bottom = halves(terms - top.astype(F32))
    sums = dot(jnp.concatenate([top, middle, bottom], axis=1), jnp.concatenate([jnp.where(ti >= si, 1.0, 0.0), jnp.where(si > ti, 1.0, 0.0), eye], axis=0).astype(BF16), TN)
    decays = sums[:8] + sums[8:16] + sums[16:]
    gd_ref[...] = gd_before_ref[...] + decays if chained else decays


SMEM = pl.BlockSpec(memory_space=pltpu.SMEM)
VMEM = pl.BlockSpec(memory_space=pltpu.VMEM)
HBM = pl.BlockSpec(memory_space=pltpu.HBM)


def shape(*dims):
    return jax.ShapeDtypeStruct(dims, F32)


def in_hbm(*arrays):
    return [pltpu.with_memory_space_constraint(a, pltpu.HBM) for a in arrays]


def block_shapes():
    return [shape(GROUP, 3, W, W), shape(GROUP, 11, W, W)]


def run_give(place, side, lengths, inputs, grad_out, beta_t, decay_t, w_key, w_query, w_out, w_value):
    rows, width = inputs.shape
    heads, span = beta_t.shape[0], GROUP * W
    wide = jax.ShapeDtypeStruct((rows, width), BF16)
    tall = jax.ShapeDtypeStruct((width, span), BF16)
    two = jax.ShapeDtypeStruct((2, width, span), BF16)
    out = pl.pallas_call(
        give_kernel,
        in_specs=[SMEM] * 2 + [HBM] * 9,
        out_specs=[VMEM] * 12,
        out_shape=block_shapes() + [wide, wide, shape(rows, heads), shape(rows, heads), shape(heads, rows), shape(W, W), shape(W, heads)] + [two, tall, two],
        scratch_shapes=[
            pltpu.SMEM(lengths.shape, jnp.int32), pltpu.VMEM(beta_t.shape, BF16), pltpu.VMEM(decay_t.shape, F32),
            pltpu.VMEM((span, width), BF16), pltpu.SemaphoreType.DMA((11,)),
        ],
        compiler_params=pltpu.CompilerParams(vmem_limit_bytes=28 << 20),
        name="block_forward_give",
    )(place, side, *in_hbm(lengths, inputs, grad_out, beta_t, decay_t, w_key, w_query, w_out, w_value))
    return out[0], out[1], out[2:9], out[9:11], out[11]


def run_keep(place, shared, w_keep, w_out, w_value):
    _, width, span = w_keep.shape
    out = pl.pallas_call(
        keep_kernel,
        in_specs=[SMEM] + [VMEM] * 8 + [HBM] * 2,
        out_specs=[VMEM] * 3,
        out_shape=block_shapes() + [jax.ShapeDtypeStruct((width, span), BF16)],
        scratch_shapes=[pltpu.VMEM((span, width), BF16), pltpu.SemaphoreType.DMA((2,))],
        compiler_params=pltpu.CompilerParams(vmem_limit_bytes=24 << 20),
        name="block_forward_keep",
    )(place, *shared, w_keep, *in_hbm(w_out, w_value))
    return out


def run_backward(place, side, back, kept, early, beta_t, w_both, w_value, before):
    heads, width = beta_t.shape
    wide = width // SIDES
    out_shape = [shape(HALF, wide)] * 2 if before else [shape(W, wide)]
    out_shape += [shape(heads, W), jax.ShapeDtypeStruct((W, 3 * GROUP * W), BF16), jax.ShapeDtypeStruct((W, heads), BF16)]
    return pl.pallas_call(
        partial(second_kernel, bool(before)),
        in_specs=[SMEM] * 2 + [VMEM] * 6 + [VMEM] * len(before),
        out_specs=[VMEM] * len(out_shape),
        out_shape=out_shape,
        compiler_params=pltpu.CompilerParams(vmem_limit_bytes=24 << 20),
        name="block_backward",
    )(place, side, back, kept, early, beta_t, w_both, w_value, *before)


def run_chunk(distances, side, beta_t, first, second):
    width = beta_t.shape[1]
    return pl.pallas_call(
        partial(chunk_kernel, distances),
        in_specs=[SMEM] + [VMEM] * 9,
        out_specs=[VMEM] * len(distances),
        out_shape=[shape(W, width // SIDES)] * len(distances),
        compiler_params=pltpu.CompilerParams(vmem_limit_bytes=16 << 20),
        name="near_chunks" if len(distances) > 1 else "own_chunk",
    )(side, beta_t, *first, *second)


def per_device(inputs, grad_out, w_query, w_key, w_value, w_beta, w_out, log_decay, lengths):
    size = lax.axis_size("ctx")
    place = lax.axis_index("ctx").astype(jnp.int32).reshape(1)
    side = lax.axis_index("head").astype(jnp.int32).reshape(1)
    beta_t, decay_t = w_beta.T, log_decay.T
    small = pltpu.CompilerParams(vmem_limit_bytes=8 << 20)

    pair = [(j, j ^ 1) for j in range(size)]
    give, give_kept, shared, give_w, keep_w = run_give(
        place, side, lengths, inputs, grad_out, beta_t, decay_t, w_key, w_query, w_out, w_value
    )
    other = lax.ppermute(give, "ctx", pair)
    own, own_kept, keep_v = run_keep(place, shared, keep_w, w_out, w_value)
    row = 2 * GROUP

    def call(kernel, name, scalars, arrays, out_shape, scratch=()):
        return pl.pallas_call(
            kernel,
            in_specs=[SMEM] * len(scalars) + [VMEM] * len(arrays),
            out_specs=[VMEM] * len(out_shape),
            out_shape=out_shape,
            scratch_shapes=list(scratch),
            compiler_params=small,
            name=name,
        )(*scalars, *arrays)

    def along_x(parts):
        got = {0: parts[0]}
        for d in (2, 1, 3):
            moves = [(j, j - j % row + (j + 2 * d) % row) for j in range(size)]
            got[d] = lax.ppermute(parts[d], "ctx", moves)
        return [got[d] for d in range(GROUP)]

    def early(kept):
        return pl.pallas_call(
            early_kernel, in_specs=[VMEM], out_specs=VMEM, out_shape=shape(GROUP, 3, W, W), name="early",
            compiler_params=pltpu.CompilerParams(vmem_limit_bytes=12 << 20),
            cost_estimate=pl.CostEstimate(flops=1 << 30, bytes_accessed=4 << 20, transcendentals=0),
        )(kept)

    whole = call(join_kernel, "chip_join", (place,), (own, other), [shape(3, W, W)] * GROUP)
    *whole, give_kept, own_kept = lax.optimization_barrier((*whole, give_kept, own_kept))
    *arrived, own_early, give_early = lax.optimization_barrier((*along_x(whole), early(own_kept), early(give_kept)))
    mine, state, grad = call(
        row_kernel, "row_ends", (place,), arrived, [shape(GROUP, 3, W, W), shape(W, W), shape(W, W)]
    )
    state = lax.ppermute(state, "ctx", [(j, (j + row) % size) for j in range(size)])
    grad = lax.ppermute(grad, "ctx", [((j + row) % size, j) for j in range(size)])
    spread = call(
        partial(spread_kernel, size), "row_states", (place,), (mine, state, grad), [shape(2, W, W)] * GROUP, [pltpu.VMEM((GROUP, 2, W, W), F32)]
    )
    own_back, give_back = call(
        part_kernel, "chip_part", (place,), (own, other, *along_x(spread)), [shape(GROUP, 2, W, W)] * 2
    )
    other_back = lax.ppermute(give_back, "ctx", pair)
    *before, keep_grads, keep_db = run_backward(place, side, own_back, own_kept, own_early, beta_t, keep_w, keep_v, ())
    up, down, grad_d, grads, db = run_backward(place, side, other_back, give_kept, give_early, beta_t, *give_w, before)
    after = [(j, (j + 1) % SIDES) for j in range(SIDES)]
    ahead = [((j + 1) % SIDES, j) for j in range(SIDES)]
    kept_part = (keep_grads, keep_db, keep_w, keep_v)
    near = run_chunk((1, 3), side, beta_t, kept_part, (grads, db, *give_w))
    halfway = (*near, lax.ppermute(up, "head", after), lax.ppermute(down, "head", ahead))
    near = call(relay_kernel, "relay", (), lax.optimization_barrier(halfway), [shape(*near[0].shape)] * 2)
    *near, grads = lax.optimization_barrier((*near, grads))
    (total,) = run_chunk((0,), side, beta_t, kept_part, (grads, db, *give_w))
    total = total + lax.ppermute(near[0], "head", after) + lax.ppermute(near[1], "head", ahead)
    return (total.astype(BF16), grad_d.T)


def solution(mesh):
    placed = (
        P("ctx", None),
        P("ctx", None),
        P(None, "head"),
        P(None, "head"),
        P(None, "head"),
        P(None, "head"),
        P("head", None),
        P("ctx", "head"),
        P(),
    )
    return jax.shard_map(
        per_device,
        mesh=mesh,
        in_specs=placed,
        out_specs=(P("ctx", "head"), P("ctx", "head")),
        check_vma=False,
    )
```

```python
from functools import partial

import jax
import jax.numpy as jnp
from jax import lax
from jax.experimental import pallas as pl
from jax.experimental.pallas import tpu as pltpu
from jax.sharding import PartitionSpec as P

F32 = jnp.float32
BF16 = jnp.bfloat16
W = 128
GROUP = 4
SIDES = 4
HALF = W // 2
NN = (((1,), (0,)), ((), ()))
NT = (((1,), (1,)), ((), ()))
TN = (((0,), (0,)), ((), ()))


def dot(a, b, dims=NN):
    return lax.dot_general(a, b, dims, preferred_element_type=F32)


def exact(a, b, dims=NN):
    return lax.dot_general(a, b, dims, precision=lax.Precision.HIGHEST, preferred_element_type=F32)


def halves(a):
    high = a.astype(BF16)
    return high, (a - high.astype(F32)).astype(BF16)


def mm3(a, b, dims=NN):
    ah, al = halves(a)
    bh, bl = halves(b)
    (ca,), (cb,) = dims[0]
    return dot(jnp.concatenate([ah, al], axis=ca), jnp.concatenate([bh, bh], axis=cb), dims) + dot(ah, bl, dims)


def iotas(shape):
    return lax.broadcasted_iota(jnp.int32, shape, 0), lax.broadcasted_iota(jnp.int32, shape, 1)


def column(array, index):
    lanes = lax.broadcasted_iota(jnp.int32, array.shape, 1)
    return jnp.sum(jnp.where(lanes == index, array, 0.0), axis=1, keepdims=True)


def inverse_all(mixes):
    ti, si = iotas((W, W))
    eye = jnp.where(ti == si, 1.0, 0.0)
    below = jnp.logical_and((ti >> 1) == (si >> 1), ti > si)
    done = [eye - jnp.where(below, a, 0.0) for a in mixes]
    for shift in range(1, 7):
        below = jnp.logical_and((ti >> (shift + 1)) == (si >> (shift + 1)), (ti >> shift) > (si >> shift))
        parts = [jnp.where(below, a, 0.0) for a in mixes]
        inner = [mm3(p, d) for p, d in zip(parts, done)]
        done = [d - mm3(d, i) for d, i in zip(done, inner)]
    return done


def head_columns(head0):
    return pl.ds(pl.multiple_of(head0 * W, GROUP * W), GROUP * W)


def give_kernel(
    place_ref, side_ref, len_hbm, x_hbm, go_hbm, wb_hbm, dec_hbm, wk_hbm, wq_hbm, wo_hbm, wv_hbm, *refs
):
    outs, refs = refs[:2], refs[2:]
    x_ref, go_ref, beta_ref, run_ref, rows_ref, keep_ref, first_ref, wkq_ref, wv_ref, wkq2_ref = refs[:10]
    len_ref, wb_ref, dec_ref, wo_ref, sems = refs[10:]
    keep0 = (place_ref[0] & 1) * GROUP
    head0 = GROUP - keep0
    base = place_ref[0] * W
    at = head_columns(head0)
    at2 = head_columns(keep0)
    pairs = (
        (wk_hbm.at[:, at], wkq_ref.at[0]), (x_hbm, x_ref), (len_hbm, len_ref), (dec_hbm, dec_ref), (wb_hbm, wb_ref),
        (wq_hbm.at[:, at], wkq_ref.at[1]), (wv_hbm.at[:, at], wv_ref), (go_hbm, go_ref), (wo_hbm.at[at, :], wo_ref),
        (wk_hbm.at[:, at2], wkq2_ref.at[0]), (wq_hbm.at[:, at2], wkq2_ref.at[1]),
    )
    gets = [pltpu.make_async_copy(src, dst, sems.at[j]) for j, (src, dst) in enumerate(pairs)]
    for get in (gets[2], gets[3], gets[4], gets[1], gets[0], gets[5], gets[6], gets[7], gets[8], gets[9], gets[10]):
        get.start()
    gets[2].wait()
    ti, si = iotas((W, W))
    begin = jnp.int32(0)
    seg_t = jnp.zeros((W, 1), jnp.int32)
    seg_s = jnp.zeros((1, W), jnp.int32)
    seg_in = jnp.int32(0)
    for j in range(len_ref.shape[0]):
        seg_t = seg_t + (ti[:, :1] + base >= begin).astype(jnp.int32)
        seg_s = seg_s + (si[:1, :] + base >= begin).astype(jnp.int32)
        seg_in = seg_in + (base - 1 >= begin).astype(jnp.int32)
        begin = begin + len_ref[j]
    keep_ref[...] = jnp.where(jnp.logical_and(seg_t == seg_s, ti >= si), 1.0, 0.0)
    lane = iotas(first_ref.shape)[1]
    marked = jnp.where(lane == 0, seg_in, seg_t[W - 1:W, :])
    first_ref[...] = jnp.where(seg_t == marked, 1.0, 0.0)
    gets[3].wait()
    tril = jnp.where(ti >= si, 1.0, 0.0)
    run_ref[...] = exact(tril, dec_ref[...], NT)
    rows_ref[...] = exact(dec_ref[...], tril, NT)
    gets[4].wait()
    gets[1].wait()
    beta_ref[...] = 1.0 / (1.0 + jnp.exp(-dot(x_ref[...], wb_ref[...], NT)))
    block_body(
        head0, x_ref, go_ref, beta_ref, run_ref, rows_ref, keep_ref, first_ref, wkq_ref, wv_ref, wo_ref,
        (gets[0], gets[5], gets[6], gets[7], gets[8]), outs,
    )
    gets[9].wait()
    gets[10].wait()


def keep_kernel(
    place_ref, x_ref, go_ref, beta_ref, run_ref, rows_ref, keep_ref, first_ref, wkq_ref, wo_hbm, wv_hbm, *refs
):
    outs = refs[:2]
    wv_ref, wo_ref, sems = refs[2:]
    head0 = (place_ref[0] & 1) * GROUP
    at = head_columns(head0)
    get_v = pltpu.make_async_copy(wv_hbm.at[:, at], wv_ref, sems.at[0])
    get_o = pltpu.make_async_copy(wo_hbm.at[at, :], wo_ref, sems.at[1])
    get_v.start()
    get_o.start()
    block_body(
        head0, x_ref, go_ref, beta_ref, run_ref, rows_ref, keep_ref, first_ref, wkq_ref, wv_ref, wo_ref,
        (None, None, get_v, None, get_o), outs,
    )


def block_body(
    head0, x_ref, go_ref, beta_ref, run_ref, rows_ref, keep_ref, first_ref, wkq_ref, wv_ref, wo_ref, gets, outs
):
    send_ref, kept_ref = outs

    def ready(*which):
        for j in which:
            if gets[j] is not None:
                gets[j].wait()

    ti, si = iotas((W, W))
    strict = ti > si
    keep = keep_ref[...] > 0.0
    first = first_ref[...][:, :1] > 0.0
    final = first_ref[...][:, 1:2] > 0.0
    beta_all, run_all, run_rows = beta_ref[...], run_ref[...], rows_ref[...]
    heads = range(GROUP)
    cut = lambda a, i: a[:, i * W:(i + 1) * W]
    ready(0)
    x = x_ref[...]
    raw_k = dot(x, wkq_ref[0])
    ready(1)
    raw_q = dot(x, wkq_ref[1])
    total = lambda a: jnp.sum(a, axis=1, keepdims=True)
    heads_at = lax.broadcasted_iota(jnp.int32, run_rows.shape, 0)
    betas = [column(beta_all, head0 + i) for i in heads]
    runs = [column(run_all, head0 + i) for i in heads]
    rows = [jnp.sum(jnp.where(heads_at == head0 + i, run_rows, 0.0), axis=0, keepdims=True) for i in heads]
    spreads = [runs[i] - rows[i] for i in heads]
    weights = [jnp.where(keep, jnp.exp(jnp.where(keep, spread, 0.0)), 0.0) for spread in spreads]
    carries = [jnp.where(first, jnp.exp(run), 0.0) for run in runs]
    closings = [jnp.where(final, jnp.exp(jnp.where(final, run[W - 1:W, :] - run, 0.0)), 0.0) for run in runs]
    rks = [cut(raw_k, i) for i in heads]
    inv_ks = [lax.rsqrt(total(rk * rk) + 1e-06) for rk in rks]
    ks = [rks[i] * inv_ks[i] for i in heads]
    key_keys = [mm3(k, k, NT) for k in ks]
    rqs = [cut(raw_q, i) for i in heads]
    inv_qs = [lax.rsqrt(total(rq * rq) + 1e-06) for rq in rqs]
    qs = [rqs[i] * inv_qs[i] * (W ** -0.5) for i in heads]
    query_keys = [mm3(qs[i], ks[i], NT) for i in heads]
    wkks = [jnp.where(strict, weights[i], 0.0) * key_keys[i] for i in heads]
    mixes = [wkks[i] * betas[i] for i in heads]
    pmats = [weights[i] * query_keys[i] for i in heads]
    for i in heads:
        last = jnp.where(si == 3, inv_ks[i], inv_qs[i])
        kept_ref[i, 10] = jnp.where(si == 0, betas[i], jnp.where(si == 1, carries[i], jnp.where(si == 2, closings[i], last)))
        kept_ref[i, 0] = ks[i]
        kept_ref[i, 1] = qs[i]
        kept_ref[i, 4] = pmats[i]
        kept_ref[i, 6] = wkks[i]
        kept_ref[i, 7] = weights[i]
    solved = inverse_all(mixes)
    ready(2)
    raw_v = dot(x, wv_ref[...])
    ready(3, 4)
    grad_o = dot(go_ref[...], wo_ref[...], NT)
    vs = [cut(raw_v, i) for i in heads]
    dos = [cut(grad_o, i) for i in heads]
    rights = [jnp.concatenate([betas[i] * vs[i], (betas[i] * carries[i]) * ks[i]], axis=1) for i in heads]
    boths = [mm3(solved[i], rights[i]) for i in heads]
    kws = [both[:, W:] for both in boths]
    inner = [mm3(pmats[i], kws[i]) for i in heads]
    flipped = [jnp.concatenate([both[:, W:], both[:, :W]], axis=1) for both in boths]
    ends = [mm3(flipped[i], closings[i] * ks[i], TN) for i in heads]
    effs = [carries[i] * qs[i] - inner[i] for i in heads]
    grads = [mm3(dos[i], effs[i], TN) for i in heads]
    for i in heads:
        kept_ref[i, 5] = solved[i]
        kept_ref[i, 2] = vs[i]
        kept_ref[i, 3] = dos[i]
        kept_ref[i, 8] = boths[i][:, :W]
        kept_ref[i, 9] = kws[i]
        send_ref[i, 0] = jnp.where(ti == si, carries[i][W - 1:W, :], 0.0) - ends[i][:W]
        send_ref[i, 1] = ends[i][W:]
        send_ref[i, 2] = grads[i]


def join_kernel(place_ref, own_ref, other_ref, *out_refs):
    second = (place_ref[0] & 1) == 1
    x = place_ref[0] >> 1
    for d in range(GROUP):
        i = (x + d) & (GROUP - 1)
        out_ref = out_refs[d]
        ta = jnp.where(second, other_ref[i, 0], own_ref[i, 0])
        tb = jnp.where(second, own_ref[i, 0], other_ref[i, 0])
        oa = jnp.where(second, other_ref[i, 1], own_ref[i, 1])
        ob = jnp.where(second, own_ref[i, 1], other_ref[i, 1])
        ga = jnp.where(second, other_ref[i, 2], own_ref[i, 2])
        gb = jnp.where(second, own_ref[i, 2], other_ref[i, 2])
        front = mm3(jnp.concatenate([ta, oa], axis=0), tb)
        out_ref[0] = front[:W]
        out_ref[1] = front[W:] + ob
        out_ref[2] = mm3(gb, ta, NT) + ga


def row_kernel(place_ref, *refs):
    x = place_ref[0] >> 1
    parts, (r_ref, state_ref, grad_ref) = refs[:GROUP], refs[GROUP:]
    for d, part in enumerate(parts):
        r_ref[(x - d) & (GROUP - 1)] = part[...]
    state = r_ref[0, 1]
    grad = r_ref[GROUP - 1, 2]
    for j in range(1, GROUP):
        state = mm3(state, r_ref[j, 0]) + r_ref[j, 1]
        b = GROUP - 1 - j
        grad = mm3(grad, r_ref[b, 0], NT) + r_ref[b, 2]
    state_ref[...] = state
    grad_ref[...] = grad


def spread_kernel(size, place_ref, r_ref, s_ref, g_ref, *refs):
    x = place_ref[0] >> 1
    outs, all_ref = refs[:GROUP], refs[GROUP]
    state = jnp.where(place_ref[0] < 2 * GROUP, 0.0, s_ref[...])
    grad = jnp.where(place_ref[0] >= size - 2 * GROUP, 0.0, g_ref[...])
    all_ref[0, 0] = state
    all_ref[GROUP - 1, 1] = grad
    for j in range(1, GROUP):
        state = mm3(state, r_ref[j - 1, 0]) + r_ref[j - 1, 1]
        all_ref[j, 0] = state
        b = GROUP - j
        grad = mm3(grad, r_ref[b, 0], NT) + r_ref[b, 2]
        all_ref[b - 1, 1] = grad
    for d, out in enumerate(outs):
        out[...] = all_ref[(x + d) & (GROUP - 1)]


def part_kernel(place_ref, own_ref, other_ref, *refs):
    chips, (mine_ref, give_ref) = refs[:GROUP], refs[GROUP:]
    second = (place_ref[0] & 1) == 1
    x = place_ref[0] >> 1
    for d, chip_ref in enumerate(chips):
        i = (x - d) & (GROUP - 1)
        ta = jnp.where(second, other_ref[i, 0], own_ref[i, 0])
        tb = jnp.where(second, own_ref[i, 0], other_ref[i, 0])
        oa = jnp.where(second, other_ref[i, 1], own_ref[i, 1])
        gb = jnp.where(second, own_ref[i, 2], other_ref[i, 2])
        s_in, g_end = chip_ref[0], chip_ref[1]
        s_mid = mm3(s_in, ta) + oa
        g_mid = mm3(g_end, tb, NT) + gb
        mine_ref[i, 0] = jnp.where(second, s_mid, s_in)
        mine_ref[i, 1] = jnp.where(second, g_end, g_mid)
        give_ref[i, 0] = jnp.where(second, s_in, s_mid)
        give_ref[i, 1] = jnp.where(second, g_mid, g_end)


def back_project(side, grads, db, wkq_ref, wv_ref, wb_ref, wide):
    at = pl.ds(pl.multiple_of(side * wide, wide), wide)
    n = grads.shape[1] // 3
    piece = dot(grads[:, :n], wkq_ref[1, at, :], NT) + dot(grads[:, n:2 * n], wkq_ref[0, at, :], NT)
    return piece + dot(grads[:, 2 * n:], wv_ref[at, :], NT) + dot(db, wb_ref[:, at])


def chunk_kernel(distances, side_ref, wb_ref, *refs):
    parts = (refs[:4], refs[4:8])
    for d, out_ref in zip(distances, refs[8:]):
        side = (side_ref[0] + d) & (SIDES - 1)
        pieces = [
            back_project(side, grads_ref[...], db_ref[...], wkq_ref, wv_ref, wb_ref, out_ref.shape[1])
            for grads_ref, db_ref, wkq_ref, wv_ref in parts
        ]
        out_ref[...] = pieces[0] + pieces[1]


def relay_kernel(next_ref, last_ref, up_ref, down_ref, next_out, last_out):
    next_out[:HALF] = next_ref[:HALF] + up_ref[...]
    next_out[HALF:] = next_ref[HALF:]
    last_out[:HALF] = last_ref[:HALF]
    last_out[HALF:] = last_ref[HALF:] + down_ref[...]


def early_kernel(kept_ref, out_ref):
    heads = range(GROUP)
    k, do, uv = ([kept_ref[i, j] for i in heads] for j in (0, 3, 8))
    ends = [kept_ref[i, 10][:, 2:3] * k[i] for i in heads]
    inner = [mm3(kept_ref[i, 4], do[i], TN) for i in heads]
    both = [mm3(kept_ref[i, 5], jnp.concatenate([inner[i], ends[i]], axis=1), TN) for i in heads]
    for i in heads:
        out_ref[i, 0] = both[i][:, :W]
        out_ref[i, 1] = both[i][:, W:]
        out_ref[i, 2] = mm3(do[i], uv[i], NT)


def second_kernel(chained, *refs):
    place_ref, side_ref, back_ref, kept_ref, early_ref, wb_ref, wkq_ref, wv_ref = refs[:8]
    refs = refs[8:]
    if chained:
        before_ref, up_ref, down_ref, grads_ref, db_ref, pairs_ref, terms_ref = refs
        wide = up_ref.shape[-1]
    else:
        total_ref, grads_ref, db_ref, pairs_ref, terms_ref = refs
        wide = total_ref.shape[-1]
    keep0 = (place_ref[0] & 1) * GROUP
    head0 = GROUP - keep0 if chained else keep0
    side = side_ref[0]
    ti, si = iotas((W, W))
    strict = ti > si
    t8, h8 = iotas((W, 8))
    none = jnp.zeros((W, 8), F32)
    heads = range(GROUP)
    s0, g1 = ([back_ref[i, j] for i in heads] for j in range(2))
    k, q, v, do, pmat, wkk, weight, uv, kw, col = ([kept_ref[i, j] for i in heads] for j in (0, 1, 2, 3, 4, 6, 7, 8, 9, 10))
    beta, carried, closing, inv_k, inv_q = ([c[:, j:j + 1] for c in col] for j in range(5))
    dr = [early_ref[i, 0] + mm3(early_ref[i, 1], g1[i], NT) for i in heads]
    u = [uv[i] - mm3(kw[i], s0[i], NT) for i in heads]
    ds = [mm3(jnp.concatenate([do[i], dr[i]], axis=0), s0[i]) for i in heads]
    da = [-mm3(dr[i], u[i], NT) for i in heads]
    ug = [closing[i] * mm3(u[i], g1[i]) for i in heads]
    dp = [early_ref[i, 2] - mm3(ds[i][:W], kw[i], NT) for i in heads]
    dkk = [jnp.where(strict, weight[i], 0.0) * da[i] * beta[i] for i in heads]
    dqk = [weight[i] * dp[i] for i in heads]
    front = [mm3(jnp.concatenate([dqk[i], dkk[i]], axis=0), k[i]) for i in heads]
    under = [mm3(jnp.concatenate([dkk[i], dqk[i]], axis=0), jnp.concatenate([k[i], q[i]], axis=0), TN) for i in heads]
    dq_state = [carried[i] * ds[i][:W] for i in heads]
    dr_s = [carried[i] * ds[i][W:] for i in heads]
    total = lambda a: jnp.sum(a, axis=1, keepdims=True)
    known = [total(dr_s[i] * k[i]) for i in heads]
    dbeta = [total(dr[i] * v[i] + da[i] * wkk[i]) - known[i] for i in heads]
    fvec = [total(ug[i] * k[i]) for i in heads]
    cvec = [total(dq_state[i] * q[i]) - beta[i] * known[i] for i in heads]
    ends = [carried[i][W - 1:W, :] * jnp.sum(total(g1[i] * s0[i]), axis=0, keepdims=True) for i in heads]
    cvec = [cvec[i] + jnp.where(t8[:, :1] == W - 1, ends[i], 0.0) for i in heads]
    dq = [front[i][:W] + dq_state[i] for i in heads]
    dk = [front[i][W:] + under[i] - beta[i] * dr_s[i] + ug[i] for i in heads]
    along_k = [total(k[i] * dk[i]) for i in heads]
    along_q = [total(q[i] * dq[i]) for i in heads]
    gks = [(inv_k[i] * (dk[i] - k[i] * along_k[i])).astype(BF16) for i in heads]
    gqs = [((inv_q[i] * (W ** -0.5)) * (dq[i] - (q[i] * float(W)) * along_q[i])).astype(BF16) for i in heads]
    gvs = [(beta[i] * dr[i]).astype(BF16) for i in heads]
    cterm, fterm, dball = none, none, none
    for i in heads:
        here = h8 == head0 + i
        cterm = jnp.where(here, cvec[i], cterm)
        fterm = jnp.where(here, fvec[i], fterm)
        pairs_ref[i] = dp[i] * pmat[i] + da[i] * wkk[i] * beta[i]
        dball = jnp.where(here, dbeta[i] * beta[i] * (1.0 - beta[i]), dball)
    grads = jnp.concatenate(gqs + gks + gvs, axis=1)
    db = dball.astype(BF16)
    project = lambda d: back_project((side + d) & (SIDES - 1), grads, db, wkq_ref, wv_ref, wb_ref, wide)
    grads_ref[...] = grads
    db_ref[...] = db
    if chained:
        far = before_ref[...] + project(2)
        up_ref[...] = far[:HALF]
        down_ref[...] = far[HALF:]
    else:
        total_ref[...] = project(2)
    terms_ref[:W] = cterm
    terms_ref[W:] = fterm


def decay_kernel(place_ref, keep_pairs_ref, keep_terms_ref, give_pairs_ref, give_terms_ref, out_ref):
    keep0 = (place_ref[0] & 1) * GROUP
    ti, si = iotas((W, W))
    upper = jnp.where(si >= ti, 1.0, 0.0).astype(BF16)
    h8 = iotas((W, 8))[1]
    eterm = jnp.zeros((W, 8), F32)
    for head0, ref in ((keep0, keep_pairs_ref), (GROUP - keep0, give_pairs_ref)):
        pairs = [halves(ref[i]) for i in range(GROUP)]
        across = [dot(upper, high) + dot(upper, low) for high, low in pairs]
        for i in range(GROUP):
            evec = jnp.sum(jnp.where(ti > si, across[i], 0.0), axis=1, keepdims=True)
            eterm = jnp.where(h8 == head0 + i, evec, eterm)
    terms = jnp.concatenate([keep_terms_ref[...] + give_terms_ref[...], eterm], axis=0)
    top = terms.astype(BF16)
    middle, bottom = halves(terms - top.astype(F32))
    reach = [jnp.where(ti >= si, 1.0, 0.0), jnp.where(si > ti, 1.0, 0.0), jnp.where(ti == si, 1.0, 0.0)]
    sums = dot(jnp.concatenate([top, middle, bottom], axis=1), jnp.concatenate(reach, axis=0).astype(BF16), TN)
    out_ref[...] = sums[:8] + sums[8:16] + sums[16:]


SMEM = pl.BlockSpec(memory_space=pltpu.SMEM)
VMEM = pl.BlockSpec(memory_space=pltpu.VMEM)
HBM = pl.BlockSpec(memory_space=pltpu.HBM)


def shape(*dims):
    return jax.ShapeDtypeStruct(dims, F32)


def in_hbm(*arrays):
    return [pltpu.with_memory_space_constraint(a, pltpu.HBM) for a in arrays]


def block_shapes():
    return [shape(GROUP, 3, W, W), shape(GROUP, 11, W, W)]


def run_give(place, side, lengths, inputs, grad_out, beta_t, decay_t, w_key, w_query, w_out, w_value):
    rows, width = inputs.shape
    heads, span = beta_t.shape[0], GROUP * W
    wide = jax.ShapeDtypeStruct((rows, width), BF16)
    tall = jax.ShapeDtypeStruct((width, span), BF16)
    two = jax.ShapeDtypeStruct((2, width, span), BF16)
    out = pl.pallas_call(
        give_kernel,
        in_specs=[SMEM] * 2 + [HBM] * 9,
        out_specs=[VMEM] * 12,
        out_shape=block_shapes() + [wide, wide, shape(rows, heads), shape(rows, heads), shape(heads, rows), shape(W, W), shape(W, heads)] + [two, tall, two],
        scratch_shapes=[
            pltpu.SMEM(lengths.shape, jnp.int32), pltpu.VMEM(beta_t.shape, BF16), pltpu.VMEM(decay_t.shape, F32),
            pltpu.VMEM((span, width), BF16), pltpu.SemaphoreType.DMA((11,)),
        ],
        compiler_params=pltpu.CompilerParams(vmem_limit_bytes=28 << 20),
        name="block_forward_give",
    )(place, side, *in_hbm(lengths, inputs, grad_out, beta_t, decay_t, w_key, w_query, w_out, w_value))
    return out[0], out[1], out[2:9], out[9:11], out[11]


def run_keep(place, shared, w_keep, w_out, w_value):
    _, width, span = w_keep.shape
    out = pl.pallas_call(
        keep_kernel,
        in_specs=[SMEM] + [VMEM] * 8 + [HBM] * 2,
        out_specs=[VMEM] * 3,
        out_shape=block_shapes() + [jax.ShapeDtypeStruct((width, span), BF16)],
        scratch_shapes=[pltpu.VMEM((span, width), BF16), pltpu.SemaphoreType.DMA((2,))],
        compiler_params=pltpu.CompilerParams(vmem_limit_bytes=24 << 20),
        name="block_forward_keep",
    )(place, *shared, w_keep, *in_hbm(w_out, w_value))
    return out


def run_backward(place, side, back, kept, early, beta_t, w_both, w_value, before):
    heads, width = beta_t.shape
    wide = width // SIDES
    out_shape = [shape(HALF, wide)] * 2 if before else [shape(W, wide)]
    out_shape += [jax.ShapeDtypeStruct((W, 3 * GROUP * W), BF16), jax.ShapeDtypeStruct((W, heads), BF16)]
    out_shape += [shape(GROUP, W, W), shape(2 * W, heads)]
    return pl.pallas_call(
        partial(second_kernel, bool(before)),
        in_specs=[SMEM] * 2 + [VMEM] * 6 + [VMEM] * len(before),
        out_specs=[VMEM] * len(out_shape),
        out_shape=out_shape,
        compiler_params=pltpu.CompilerParams(vmem_limit_bytes=24 << 20),
        name="block_backward",
    )(place, side, back, kept, early, beta_t, w_both, w_value, *before)


def run_chunk(distances, side, beta_t, first, second):
    width = beta_t.shape[1]
    return pl.pallas_call(
        partial(chunk_kernel, distances),
        in_specs=[SMEM] + [VMEM] * 9,
        out_specs=[VMEM] * len(distances),
        out_shape=[shape(W, width // SIDES)] * len(distances),
        compiler_params=pltpu.CompilerParams(vmem_limit_bytes=16 << 20),
        name="near_chunks" if len(distances) > 1 else "own_chunk",
    )(side, beta_t, *first, *second)


def per_device(inputs, grad_out, w_query, w_key, w_value, w_beta, w_out, log_decay, lengths):
    size = lax.axis_size("ctx")
    place = lax.axis_index("ctx").astype(jnp.int32).reshape(1)
    side = lax.axis_index("head").astype(jnp.int32).reshape(1)
    beta_t, decay_t = w_beta.T, log_decay.T
    small = pltpu.CompilerParams(vmem_limit_bytes=8 << 20)

    pair = [(j, j ^ 1) for j in range(size)]
    give, give_kept, shared, give_w, keep_w = run_give(
        place, side, lengths, inputs, grad_out, beta_t, decay_t, w_key, w_query, w_out, w_value
    )
    other = lax.ppermute(give, "ctx", pair)
    own, own_kept, keep_v = run_keep(place, shared, keep_w, w_out, w_value)
    row = 2 * GROUP

    def call(kernel, name, scalars, arrays, out_shape, scratch=()):
        return pl.pallas_call(
            kernel,
            in_specs=[SMEM] * len(scalars) + [VMEM] * len(arrays),
            out_specs=[VMEM] * len(out_shape),
            out_shape=out_shape,
            scratch_shapes=list(scratch),
            compiler_params=small,
            name=name,
        )(*scalars, *arrays)

    def along_x(parts):
        got = {0: parts[0]}
        for d in (2, 1, 3):
            moves = [(j, j - j % row + (j + 2 * d) % row) for j in range(size)]
            got[d] = lax.ppermute(parts[d], "ctx", moves)
        return [got[d] for d in range(GROUP)]

    def early(kept):
        return pl.pallas_call(
            early_kernel, in_specs=[VMEM], out_specs=VMEM, out_shape=shape(GROUP, 3, W, W), name="early",
            compiler_params=pltpu.CompilerParams(vmem_limit_bytes=12 << 20),
            cost_estimate=pl.CostEstimate(flops=1 << 30, bytes_accessed=4 << 20, transcendentals=0),
        )(kept)

    whole = call(join_kernel, "chip_join", (place,), (own, other), [shape(3, W, W)] * GROUP)
    *whole, give_kept, own_kept = lax.optimization_barrier((*whole, give_kept, own_kept))
    *arrived, own_early, give_early = lax.optimization_barrier((*along_x(whole), early(own_kept), early(give_kept)))
    mine, state, grad = call(
        row_kernel, "row_ends", (place,), arrived, [shape(GROUP, 3, W, W), shape(W, W), shape(W, W)]
    )
    state = lax.ppermute(state, "ctx", [(j, (j + row) % size) for j in range(size)])
    grad = lax.ppermute(grad, "ctx", [((j + row) % size, j) for j in range(size)])
    spread = call(
        partial(spread_kernel, size), "row_states", (place,), (mine, state, grad), [shape(2, W, W)] * GROUP, [pltpu.VMEM((GROUP, 2, W, W), F32)]
    )
    own_back, give_back = call(
        part_kernel, "chip_part", (place,), (own, other, *along_x(spread)), [shape(GROUP, 2, W, W)] * 2
    )
    other_back = lax.ppermute(give_back, "ctx", pair)
    before, keep_grads, keep_db, *keep_sums = run_backward(place, side, own_back, own_kept, own_early, beta_t, keep_w, keep_v, ())
    up, down, grads, db, *give_sums = run_backward(
        place, side, other_back, give_kept, give_early, beta_t, *give_w, (before,)
    )
    after = [(j, (j + 1) % SIDES) for j in range(SIDES)]
    ahead = [((j + 1) % SIDES, j) for j in range(SIDES)]
    kept_part = (keep_grads, keep_db, keep_w, keep_v)
    near = run_chunk((1, 3), side, beta_t, kept_part, (grads, db, *give_w))
    halfway = (*near, lax.ppermute(up, "head", after), lax.ppermute(down, "head", ahead))
    near = call(relay_kernel, "relay", (), lax.optimization_barrier(halfway), [shape(*near[0].shape)] * 2)
    *near, grads, keep_pairs = lax.optimization_barrier((*near, grads, keep_sums[0]))
    sums = (keep_pairs, keep_sums[1], *give_sums)
    (grad_d,) = call(decay_kernel, "decay_sums", (place,), sums, [shape(2 * GROUP, W)])
    (total,) = run_chunk((0,), side, beta_t, kept_part, (grads, db, *give_w))
    total = total + lax.ppermute(near[0], "head", after) + lax.ppermute(near[1], "head", ahead)
    return (total.astype(BF16), grad_d.T)


def solution(mesh):
    placed = (
        P("ctx", None),
        P("ctx", None),
        P(None, "head"),
        P(None, "head"),
        P(None, "head"),
        P(None, "head"),
        P("head", None),
        P("ctx", "head"),
        P(),
    )
    return jax.shard_map(
        per_device,
        mesh=mesh,
        in_specs=placed,
        out_specs=(P("ctx", "head"), P("ctx", "head")),
        check_vma=False,
    )
```

```python
from functools import partial

import jax
import jax.numpy as jnp
from jax import lax
from jax.experimental import pallas as pl
from jax.experimental.pallas import tpu as pltpu
from jax.sharding import PartitionSpec as P

F32 = jnp.float32
BF16 = jnp.bfloat16
W = 128
GROUP = 4
SIDES = 4
HALF = W // 2
NN = (((1,), (0,)), ((), ()))
NT = (((1,), (1,)), ((), ()))
TN = (((0,), (0,)), ((), ()))


def dot(a, b, dims=NN):
    return lax.dot_general(a, b, dims, preferred_element_type=F32)


def exact(a, b, dims=NN):
    return lax.dot_general(a, b, dims, precision=lax.Precision.HIGHEST, preferred_element_type=F32)


def halves(a):
    high = a.astype(BF16)
    return high, (a - high.astype(F32)).astype(BF16)


def mm3(a, b, dims=NN):
    ah, al = halves(a)
    bh, bl = halves(b)
    (ca,), (cb,) = dims[0]
    return dot(jnp.concatenate([ah, al], axis=ca), jnp.concatenate([bh, bh], axis=cb), dims) + dot(ah, bl, dims)


def iotas(shape):
    return lax.broadcasted_iota(jnp.int32, shape, 0), lax.broadcasted_iota(jnp.int32, shape, 1)


def column(array, index):
    lanes = lax.broadcasted_iota(jnp.int32, array.shape, 1)
    return jnp.sum(jnp.where(lanes == index, array, 0.0), axis=1, keepdims=True)


def inverse_all(mixes):
    ti, si = iotas((W, W))
    eye = jnp.where(ti == si, 1.0, 0.0)
    below = jnp.logical_and((ti >> 1) == (si >> 1), ti > si)
    done = [eye - jnp.where(below, a, 0.0) for a in mixes]
    for shift in range(1, 7):
        below = jnp.logical_and((ti >> (shift + 1)) == (si >> (shift + 1)), (ti >> shift) > (si >> shift))
        parts = [jnp.where(below, a, 0.0) for a in mixes]
        inner = [mm3(p, d) for p, d in zip(parts, done)]
        done = [d - mm3(d, i) for d, i in zip(done, inner)]
    return done


def head_columns(head0):
    return pl.ds(pl.multiple_of(head0 * W, GROUP * W), GROUP * W)


def give_kernel(
    place_ref, side_ref, len_hbm, x_hbm, go_hbm, wb_hbm, dec_hbm, wk_hbm, wq_hbm, wo_hbm, wv_hbm, *refs
):
    outs, refs = refs[:2], refs[2:]
    x_ref, go_ref, beta_ref, run_ref, rows_ref, keep_ref, first_ref, wkq_ref, wv_ref, wkq2_ref = refs[:10]
    len_ref, wb_ref, dec_ref, wo_ref, sems = refs[10:]
    keep0 = (place_ref[0] & 1) * GROUP
    head0 = GROUP - keep0
    base = place_ref[0] * W
    at = head_columns(head0)
    at2 = head_columns(keep0)
    pairs = (
        (wk_hbm.at[:, at], wkq_ref.at[0]), (x_hbm, x_ref), (len_hbm, len_ref), (dec_hbm, dec_ref), (wb_hbm, wb_ref),
        (wq_hbm.at[:, at], wkq_ref.at[1]), (wv_hbm.at[:, at], wv_ref), (go_hbm, go_ref), (wo_hbm.at[at, :], wo_ref),
        (wk_hbm.at[:, at2], wkq2_ref.at[0]), (wq_hbm.at[:, at2], wkq2_ref.at[1]),
    )
    gets = [pltpu.make_async_copy(src, dst, sems.at[j]) for j, (src, dst) in enumerate(pairs)]
    for get in (gets[2], gets[3], gets[4], gets[1], gets[0], gets[5], gets[6], gets[7], gets[8], gets[9], gets[10]):
        get.start()
    gets[2].wait()
    ti, si = iotas((W, W))
    begin = jnp.int32(0)
    seg_t = jnp.zeros((W, 1), jnp.int32)
    seg_s = jnp.zeros((1, W), jnp.int32)
    seg_in = jnp.int32(0)
    for j in range(len_ref.shape[0]):
        seg_t = seg_t + (ti[:, :1] + base >= begin).astype(jnp.int32)
        seg_s = seg_s + (si[:1, :] + base >= begin).astype(jnp.int32)
        seg_in = seg_in + (base - 1 >= begin).astype(jnp.int32)
        begin = begin + len_ref[j]
    keep_ref[...] = jnp.where(jnp.logical_and(seg_t == seg_s, ti >= si), 1.0, 0.0)
    lane = iotas(first_ref.shape)[1]
    marked = jnp.where(lane == 0, seg_in, seg_t[W - 1:W, :])
    first_ref[...] = jnp.where(seg_t == marked, 1.0, 0.0)
    gets[3].wait()
    tril = jnp.where(ti >= si, 1.0, 0.0)
    run_ref[...] = exact(tril, dec_ref[...], NT)
    rows_ref[...] = exact(dec_ref[...], tril, NT)
    gets[4].wait()
    gets[1].wait()
    beta_ref[...] = 1.0 / (1.0 + jnp.exp(-dot(x_ref[...], wb_ref[...], NT)))
    block_body(
        head0, x_ref, go_ref, beta_ref, run_ref, rows_ref, keep_ref, first_ref, wkq_ref, wv_ref, wo_ref,
        (gets[0], gets[5], gets[6], gets[7], gets[8]), outs,
    )
    gets[9].wait()
    gets[10].wait()


def keep_kernel(
    place_ref, x_ref, go_ref, beta_ref, run_ref, rows_ref, keep_ref, first_ref, wkq_ref, wo_hbm, wv_hbm, *refs
):
    outs = refs[:2]
    wv_ref, wo_ref, sems = refs[2:]
    head0 = (place_ref[0] & 1) * GROUP
    at = head_columns(head0)
    get_v = pltpu.make_async_copy(wv_hbm.at[:, at], wv_ref, sems.at[0])
    get_o = pltpu.make_async_copy(wo_hbm.at[at, :], wo_ref, sems.at[1])
    get_v.start()
    get_o.start()
    block_body(
        head0, x_ref, go_ref, beta_ref, run_ref, rows_ref, keep_ref, first_ref, wkq_ref, wv_ref, wo_ref,
        (None, None, get_v, None, get_o), outs,
    )


def block_body(
    head0, x_ref, go_ref, beta_ref, run_ref, rows_ref, keep_ref, first_ref, wkq_ref, wv_ref, wo_ref, gets, outs
):
    send_ref, kept_ref = outs

    def ready(*which):
        for j in which:
            if gets[j] is not None:
                gets[j].wait()

    ti, si = iotas((W, W))
    strict = ti > si
    keep = keep_ref[...] > 0.0
    first = first_ref[...][:, :1] > 0.0
    final = first_ref[...][:, 1:2] > 0.0
    beta_all, run_all, run_rows = beta_ref[...], run_ref[...], rows_ref[...]
    heads = range(GROUP)
    cut = lambda a, i: a[:, i * W:(i + 1) * W]
    ready(0)
    x = x_ref[...]
    raw_k = dot(x, wkq_ref[0])
    ready(1)
    raw_q = dot(x, wkq_ref[1])
    total = lambda a: jnp.sum(a, axis=1, keepdims=True)
    heads_at = lax.broadcasted_iota(jnp.int32, run_rows.shape, 0)
    betas = [column(beta_all, head0 + i) for i in heads]
    runs = [column(run_all, head0 + i) for i in heads]
    rows = [jnp.sum(jnp.where(heads_at == head0 + i, run_rows, 0.0), axis=0, keepdims=True) for i in heads]
    spreads = [runs[i] - rows[i] for i in heads]
    weights = [jnp.where(keep, jnp.exp(jnp.where(keep, spread, 0.0)), 0.0) for spread in spreads]
    carries = [jnp.where(first, jnp.exp(run), 0.0) for run in runs]
    closings = [jnp.where(final, jnp.exp(jnp.where(final, run[W - 1:W, :] - run, 0.0)), 0.0) for run in runs]
    rks = [cut(raw_k, i) for i in heads]
    inv_ks = [lax.rsqrt(total(rk * rk) + 1e-06) for rk in rks]
    ks = [rks[i] * inv_ks[i] for i in heads]
    key_keys = [mm3(k, k, NT) for k in ks]
    rqs = [cut(raw_q, i) for i in heads]
    inv_qs = [lax.rsqrt(total(rq * rq) + 1e-06) for rq in rqs]
    qs = [rqs[i] * inv_qs[i] * (W ** -0.5) for i in heads]
    query_keys = [mm3(qs[i], ks[i], NT) for i in heads]
    wkks = [jnp.where(strict, weights[i], 0.0) * key_keys[i] for i in heads]
    mixes = [wkks[i] * betas[i] for i in heads]
    pmats = [weights[i] * query_keys[i] for i in heads]
    for i in heads:
        last = jnp.where(si == 3, inv_ks[i], inv_qs[i])
        kept_ref[i, 10] = jnp.where(si == 0, betas[i], jnp.where(si == 1, carries[i], jnp.where(si == 2, closings[i], last)))
        kept_ref[i, 0] = ks[i]
        kept_ref[i, 1] = qs[i]
        kept_ref[i, 4] = pmats[i]
        kept_ref[i, 6] = wkks[i]
        kept_ref[i, 7] = weights[i]
    solved = inverse_all(mixes)
    ready(2)
    raw_v = dot(x, wv_ref[...])
    ready(3, 4)
    grad_o = dot(go_ref[...], wo_ref[...], NT)
    vs = [cut(raw_v, i) for i in heads]
    dos = [cut(grad_o, i) for i in heads]
    rights = [jnp.concatenate([betas[i] * vs[i], (betas[i] * carries[i]) * ks[i]], axis=1) for i in heads]
    boths = [mm3(solved[i], rights[i]) for i in heads]
    kws = [both[:, W:] for both in boths]
    inner = [mm3(pmats[i], kws[i]) for i in heads]
    flipped = [jnp.concatenate([both[:, W:], both[:, :W]], axis=1) for both in boths]
    ends = [mm3(flipped[i], closings[i] * ks[i], TN) for i in heads]
    effs = [carries[i] * qs[i] - inner[i] for i in heads]
    grads = [mm3(dos[i], effs[i], TN) for i in heads]
    for i in heads:
        kept_ref[i, 5] = solved[i]
        kept_ref[i, 2] = vs[i]
        kept_ref[i, 3] = dos[i]
        kept_ref[i, 8] = boths[i][:, :W]
        kept_ref[i, 9] = kws[i]
        send_ref[i, 0] = jnp.where(ti == si, carries[i][W - 1:W, :], 0.0) - ends[i][:W]
        send_ref[i, 1] = ends[i][W:]
        send_ref[i, 2] = grads[i]


def join_kernel(place_ref, own_ref, other_ref, *out_refs):
    second = (place_ref[0] & 1) == 1
    x = place_ref[0] >> 1
    for d in range(GROUP):
        i = (x + d) & (GROUP - 1)
        out_ref = out_refs[d]
        ta = jnp.where(second, other_ref[i, 0], own_ref[i, 0])
        tb = jnp.where(second, own_ref[i, 0], other_ref[i, 0])
        oa = jnp.where(second, other_ref[i, 1], own_ref[i, 1])
        ob = jnp.where(second, own_ref[i, 1], other_ref[i, 1])
        ga = jnp.where(second, other_ref[i, 2], own_ref[i, 2])
        gb = jnp.where(second, own_ref[i, 2], other_ref[i, 2])
        front = mm3(jnp.concatenate([ta, oa], axis=0), tb)
        out_ref[0] = front[:W]
        out_ref[1] = front[W:] + ob
        out_ref[2] = mm3(gb, ta, NT) + ga


def row_kernel(place_ref, *refs):
    x = place_ref[0] >> 1
    parts, (r_ref, state_ref, grad_ref) = refs[:GROUP], refs[GROUP:]
    for d, part in enumerate(parts):
        r_ref[(x - d) & (GROUP - 1)] = part[...]
    state = r_ref[0, 1]
    grad = r_ref[GROUP - 1, 2]
    for j in range(1, GROUP):
        state = mm3(state, r_ref[j, 0]) + r_ref[j, 1]
        b = GROUP - 1 - j
        grad = mm3(grad, r_ref[b, 0], NT) + r_ref[b, 2]
    state_ref[...] = state
    grad_ref[...] = grad


def spread_kernel(size, place_ref, r_ref, s_ref, g_ref, *refs):
    x = place_ref[0] >> 1
    outs, all_ref = refs[:GROUP], refs[GROUP]
    state = jnp.where(place_ref[0] < 2 * GROUP, 0.0, s_ref[...])
    grad = jnp.where(place_ref[0] >= size - 2 * GROUP, 0.0, g_ref[...])
    all_ref[0, 0] = state
    all_ref[GROUP - 1, 1] = grad
    for j in range(1, GROUP):
        state = mm3(state, r_ref[j - 1, 0]) + r_ref[j - 1, 1]
        all_ref[j, 0] = state
        b = GROUP - j
        grad = mm3(grad, r_ref[b, 0], NT) + r_ref[b, 2]
        all_ref[b - 1, 1] = grad
    for d, out in enumerate(outs):
        out[...] = all_ref[(x + d) & (GROUP - 1)]


def part_kernel(place_ref, own_ref, other_ref, *refs):
    chips, (mine_ref, give_ref) = refs[:GROUP], refs[GROUP:]
    second = (place_ref[0] & 1) == 1
    x = place_ref[0] >> 1
    for d, chip_ref in enumerate(chips):
        i = (x - d) & (GROUP - 1)
        ta = jnp.where(second, other_ref[i, 0], own_ref[i, 0])
        tb = jnp.where(second, own_ref[i, 0], other_ref[i, 0])
        oa = jnp.where(second, other_ref[i, 1], own_ref[i, 1])
        gb = jnp.where(second, own_ref[i, 2], other_ref[i, 2])
        s_in, g_end = chip_ref[0], chip_ref[1]
        s_mid = mm3(s_in, ta) + oa
        g_mid = mm3(g_end, tb, NT) + gb
        mine_ref[i, 0] = jnp.where(second, s_mid, s_in)
        mine_ref[i, 1] = jnp.where(second, g_end, g_mid)
        give_ref[i, 0] = jnp.where(second, s_in, s_mid)
        give_ref[i, 1] = jnp.where(second, g_mid, g_end)


def back_project(side, grads, db, wkq_ref, wv_ref, wb_ref, wide):
    at = pl.ds(pl.multiple_of(side * wide, wide), wide)
    n = grads.shape[1] // 3
    piece = dot(grads[:, :n], wkq_ref[1, at, :], NT) + dot(grads[:, n:2 * n], wkq_ref[0, at, :], NT)
    return piece + dot(grads[:, 2 * n:], wv_ref[at, :], NT) + dot(db, wb_ref[:, at])


def chunk_kernel(distances, side_ref, wb_ref, *refs):
    parts = (refs[:4], refs[4:8])
    for d, out_ref in zip(distances, refs[8:]):
        side = (side_ref[0] + d) & (SIDES - 1)
        pieces = [
            back_project(side, grads_ref[...], db_ref[...], wkq_ref, wv_ref, wb_ref, out_ref.shape[1])
            for grads_ref, db_ref, wkq_ref, wv_ref in parts
        ]
        out_ref[...] = pieces[0] + pieces[1]


def relay_kernel(next_ref, last_ref, up_ref, down_ref, next_out, last_out):
    next_out[:HALF] = next_ref[:HALF] + up_ref[...]
    next_out[HALF:] = next_ref[HALF:]
    last_out[:HALF] = last_ref[:HALF]
    last_out[HALF:] = last_ref[HALF:] + down_ref[...]


def early_kernel(kept_ref, out_ref):
    heads = range(GROUP)
    k, do, uv = ([kept_ref[i, j] for i in heads] for j in (0, 3, 8))
    ends = [kept_ref[i, 10][:, 2:3] * k[i] for i in heads]
    inner = [mm3(kept_ref[i, 4], do[i], TN) for i in heads]
    both = [mm3(kept_ref[i, 5], jnp.concatenate([inner[i], ends[i]], axis=1), TN) for i in heads]
    for i in heads:
        out_ref[i, 0] = both[i][:, :W]
        out_ref[i, 1] = both[i][:, W:]
        out_ref[i, 2] = mm3(do[i], uv[i], NT)


def second_kernel(chained, *refs):
    place_ref, side_ref, back_ref, kept_ref, early_ref, wb_ref, wkq_ref, wv_ref = refs[:8]
    refs = refs[8:]
    if chained:
        before_ref, up_ref, down_ref, grads_ref, db_ref, pairs_ref, terms_ref = refs
        wide = up_ref.shape[-1]
    else:
        total_ref, grads_ref, db_ref, pairs_ref, terms_ref = refs
        wide = total_ref.shape[-1]
    keep0 = (place_ref[0] & 1) * GROUP
    head0 = GROUP - keep0 if chained else keep0
    side = side_ref[0]
    ti, si = iotas((W, W))
    strict = ti > si
    t8, h8 = iotas((W, 8))
    none = jnp.zeros((W, 8), F32)
    heads = range(GROUP)
    s0, g1 = ([back_ref[i, j] for i in heads] for j in range(2))
    k, q, v, do, pmat, wkk, weight, uv, kw, col = ([kept_ref[i, j] for i in heads] for j in (0, 1, 2, 3, 4, 6, 7, 8, 9, 10))
    beta, carried, closing, inv_k, inv_q = ([c[:, j:j + 1] for c in col] for j in range(5))
    dr = [early_ref[i, 0] + mm3(early_ref[i, 1], g1[i], NT) for i in heads]
    u = [uv[i] - mm3(kw[i], s0[i], NT) for i in heads]
    ds = [mm3(jnp.concatenate([do[i], dr[i]], axis=0), s0[i]) for i in heads]
    da = [-mm3(dr[i], u[i], NT) for i in heads]
    ug = [closing[i] * mm3(u[i], g1[i]) for i in heads]
    dp = [early_ref[i, 2] - mm3(ds[i][:W], kw[i], NT) for i in heads]
    dkk = [jnp.where(strict, weight[i], 0.0) * da[i] * beta[i] for i in heads]
    dqk = [weight[i] * dp[i] for i in heads]
    front = [mm3(jnp.concatenate([dqk[i], dkk[i]], axis=0), k[i]) for i in heads]
    under = [mm3(jnp.concatenate([dkk[i], dqk[i]], axis=0), jnp.concatenate([k[i], q[i]], axis=0), TN) for i in heads]
    dq_state = [carried[i] * ds[i][:W] for i in heads]
    dr_s = [carried[i] * ds[i][W:] for i in heads]
    total = lambda a: jnp.sum(a, axis=1, keepdims=True)
    known = [total(dr_s[i] * k[i]) for i in heads]
    dbeta = [total(dr[i] * v[i] + da[i] * wkk[i]) - known[i] for i in heads]
    fvec = [total(ug[i] * k[i]) for i in heads]
    cvec = [total(dq_state[i] * q[i]) - beta[i] * known[i] for i in heads]
    ends = [carried[i][W - 1:W, :] * jnp.sum(total(g1[i] * s0[i]), axis=0, keepdims=True) for i in heads]
    cvec = [cvec[i] + jnp.where(t8[:, :1] == W - 1, ends[i], 0.0) for i in heads]
    dq = [front[i][:W] + dq_state[i] for i in heads]
    dk = [front[i][W:] + under[i] - beta[i] * dr_s[i] + ug[i] for i in heads]
    along_k = [total(k[i] * dk[i]) for i in heads]
    along_q = [total(q[i] * dq[i]) for i in heads]
    gks = [(inv_k[i] * (dk[i] - k[i] * along_k[i])).astype(BF16) for i in heads]
    gqs = [((inv_q[i] * (W ** -0.5)) * (dq[i] - (q[i] * float(W)) * along_q[i])).astype(BF16) for i in heads]
    gvs = [(beta[i] * dr[i]).astype(BF16) for i in heads]
    cterm, fterm, dball = none, none, none
    for i in heads:
        here = h8 == head0 + i
        cterm = jnp.where(here, cvec[i], cterm)
        fterm = jnp.where(here, fvec[i], fterm)
        pairs_ref[i] = dp[i] * pmat[i] + da[i] * wkk[i] * beta[i]
        dball = jnp.where(here, dbeta[i] * beta[i] * (1.0 - beta[i]), dball)
    grads = jnp.concatenate(gqs + gks + gvs, axis=1)
    db = dball.astype(BF16)
    project = lambda d: back_project((side + d) & (SIDES - 1), grads, db, wkq_ref, wv_ref, wb_ref, wide)
    grads_ref[...] = grads
    db_ref[...] = db
    if chained:
        far = before_ref[...] + project(2)
        up_ref[...] = far[:HALF]
        down_ref[...] = far[HALF:]
    else:
        total_ref[...] = project(2)
    terms_ref[:W] = cterm
    terms_ref[W:] = fterm


def decay_kernel(place_ref, keep_pairs_ref, keep_terms_ref, give_pairs_ref, give_terms_ref, out_ref):
    keep0 = (place_ref[0] & 1) * GROUP
    ti, si = iotas((W, W))
    upper = jnp.where(si >= ti, 1.0, 0.0).astype(BF16)
    h8 = iotas((W, 8))[1]
    eterm = jnp.zeros((W, 8), F32)
    for head0, ref in ((keep0, keep_pairs_ref), (GROUP - keep0, give_pairs_ref)):
        pairs = [halves(ref[i]) for i in range(GROUP)]
        across = [dot(upper, high) + dot(upper, low) for high, low in pairs]
        for i in range(GROUP):
            evec = jnp.sum(jnp.where(ti > si, across[i], 0.0), axis=1, keepdims=True)
            eterm = jnp.where(h8 == head0 + i, evec, eterm)
    terms = jnp.concatenate([keep_terms_ref[...] + give_terms_ref[...], eterm], axis=0)
    top = terms.astype(BF16)
    middle, bottom = halves(terms - top.astype(F32))
    reach = [jnp.where(ti >= si, 1.0, 0.0), jnp.where(si > ti, 1.0, 0.0), jnp.where(ti == si, 1.0, 0.0)]
    sums = dot(jnp.concatenate([top, middle, bottom], axis=1), jnp.concatenate(reach, axis=0).astype(BF16), TN)
    out_ref[...] = sums[:8] + sums[8:16] + sums[16:]


SMEM = pl.BlockSpec(memory_space=pltpu.SMEM)
VMEM = pl.BlockSpec(memory_space=pltpu.VMEM)
HBM = pl.BlockSpec(memory_space=pltpu.HBM)


def shape(*dims):
    return jax.ShapeDtypeStruct(dims, F32)


def in_hbm(*arrays):
    return [pltpu.with_memory_space_constraint(a, pltpu.HBM) for a in arrays]


def block_shapes():
    return [shape(GROUP, 3, W, W), shape(GROUP, 11, W, W)]


def run_give(place, side, lengths, inputs, grad_out, beta_t, decay_t, w_key, w_query, w_out, w_value):
    rows, width = inputs.shape
    heads, span = beta_t.shape[0], GROUP * W
    wide = jax.ShapeDtypeStruct((rows, width), BF16)
    tall = jax.ShapeDtypeStruct((width, span), BF16)
    two = jax.ShapeDtypeStruct((2, width, span), BF16)
    out = pl.pallas_call(
        give_kernel,
        in_specs=[SMEM] * 2 + [HBM] * 9,
        out_specs=[VMEM] * 12,
        out_shape=block_shapes() + [wide, wide, shape(rows, heads), shape(rows, heads), shape(heads, rows), shape(W, W), shape(W, heads)] + [two, tall, two],
        scratch_shapes=[
            pltpu.SMEM(lengths.shape, jnp.int32), pltpu.VMEM(beta_t.shape, BF16), pltpu.VMEM(decay_t.shape, F32),
            pltpu.VMEM((span, width), BF16), pltpu.SemaphoreType.DMA((11,)),
        ],
        compiler_params=pltpu.CompilerParams(vmem_limit_bytes=28 << 20),
        name="block_forward_give",
    )(place, side, *in_hbm(lengths, inputs, grad_out, beta_t, decay_t, w_key, w_query, w_out, w_value))
    return out[0], out[1], out[2:9], out[9:11], out[11]


def run_keep(place, shared, w_keep, w_out, w_value):
    _, width, span = w_keep.shape
    out = pl.pallas_call(
        keep_kernel,
        in_specs=[SMEM] + [VMEM] * 8 + [HBM] * 2,
        out_specs=[VMEM] * 3,
        out_shape=block_shapes() + [jax.ShapeDtypeStruct((width, span), BF16)],
        scratch_shapes=[pltpu.VMEM((span, width), BF16), pltpu.SemaphoreType.DMA((2,))],
        compiler_params=pltpu.CompilerParams(vmem_limit_bytes=24 << 20),
        name="block_forward_keep",
    )(place, *shared, w_keep, *in_hbm(w_out, w_value))
    return out


def run_backward(place, side, back, kept, early, beta_t, w_both, w_value, before):
    heads, width = beta_t.shape
    wide = width // SIDES
    out_shape = [shape(HALF, wide)] * 2 if before else [shape(W, wide)]
    out_shape += [jax.ShapeDtypeStruct((W, 3 * GROUP * W), BF16), jax.ShapeDtypeStruct((W, heads), BF16)]
    out_shape += [shape(GROUP, W, W), shape(2 * W, heads)]
    return pl.pallas_call(
        partial(second_kernel, bool(before)),
        in_specs=[SMEM] * 2 + [VMEM] * 6 + [VMEM] * len(before),
        out_specs=[VMEM] * len(out_shape),
        out_shape=out_shape,
        compiler_params=pltpu.CompilerParams(vmem_limit_bytes=24 << 20),
        name="block_backward",
    )(place, side, back, kept, early, beta_t, w_both, w_value, *before)


def run_chunk(distances, side, beta_t, first, second):
    width = beta_t.shape[1]
    return pl.pallas_call(
        partial(chunk_kernel, distances),
        in_specs=[SMEM] + [VMEM] * 9,
        out_specs=[VMEM] * len(distances),
        out_shape=[shape(W, width // SIDES)] * len(distances),
        compiler_params=pltpu.CompilerParams(vmem_limit_bytes=16 << 20),
        name="near_chunks" if len(distances) > 1 else "own_chunk",
    )(side, beta_t, *first, *second)


def per_device(inputs, grad_out, w_query, w_key, w_value, w_beta, w_out, log_decay, lengths):
    size = lax.axis_size("ctx")
    place = lax.axis_index("ctx").astype(jnp.int32).reshape(1)
    side = lax.axis_index("head").astype(jnp.int32).reshape(1)
    beta_t, decay_t = w_beta.T, log_decay.T
    small = pltpu.CompilerParams(vmem_limit_bytes=8 << 20)

    pair = [(j, j ^ 1) for j in range(size)]
    give, give_kept, shared, give_w, keep_w = run_give(
        place, side, lengths, inputs, grad_out, beta_t, decay_t, w_key, w_query, w_out, w_value
    )
    other = lax.ppermute(give, "ctx", pair)
    own, own_kept, keep_v = run_keep(place, shared, keep_w, w_out, w_value)
    row = 2 * GROUP

    def call(kernel, name, scalars, arrays, out_shape, scratch=()):
        return pl.pallas_call(
            kernel,
            in_specs=[SMEM] * len(scalars) + [VMEM] * len(arrays),
            out_specs=[VMEM] * len(out_shape),
            out_shape=out_shape,
            scratch_shapes=list(scratch),
            compiler_params=small,
            name=name,
        )(*scalars, *arrays)

    def along_x(parts):
        got = {0: parts[0]}
        for d in (1, 3, 2):
            moves = [(j, j - j % row + (j + 2 * d) % row) for j in range(size)]
            got[d] = lax.ppermute(parts[d], "ctx", moves)
        return [got[d] for d in range(GROUP)]

    def early(kept):
        return pl.pallas_call(
            early_kernel, in_specs=[VMEM], out_specs=VMEM, out_shape=shape(GROUP, 3, W, W), name="early",
            compiler_params=pltpu.CompilerParams(vmem_limit_bytes=12 << 20),
            cost_estimate=pl.CostEstimate(flops=1 << 30, bytes_accessed=4 << 20, transcendentals=0),
        )(kept)

    whole = call(join_kernel, "chip_join", (place,), (own, other), [shape(3, W, W)] * GROUP)
    *whole, give_kept, own_kept = lax.optimization_barrier((*whole, give_kept, own_kept))
    *arrived, own_early, give_early = lax.optimization_barrier((*along_x(whole), early(own_kept), early(give_kept)))
    mine, state, grad = call(
        row_kernel, "row_ends", (place,), arrived, [shape(GROUP, 3, W, W), shape(W, W), shape(W, W)]
    )
    state = lax.ppermute(state, "ctx", [(j, (j + row) % size) for j in range(size)])
    grad = lax.ppermute(grad, "ctx", [((j + row) % size, j) for j in range(size)])
    spread = call(
        partial(spread_kernel, size), "row_states", (place,), (mine, state, grad), [shape(2, W, W)] * GROUP, [pltpu.VMEM((GROUP, 2, W, W), F32)]
    )
    own_back, give_back = call(
        part_kernel, "chip_part", (place,), (own, other, *along_x(spread)), [shape(GROUP, 2, W, W)] * 2
    )
    other_back = lax.ppermute(give_back, "ctx", pair)
    before, keep_grads, keep_db, *keep_sums = run_backward(place, side, own_back, own_kept, own_early, beta_t, keep_w, keep_v, ())
    up, down, grads, db, *give_sums = run_backward(
        place, side, other_back, give_kept, give_early, beta_t, *give_w, (before,)
    )
    after = [(j, (j + 1) % SIDES) for j in range(SIDES)]
    ahead = [((j + 1) % SIDES, j) for j in range(SIDES)]
    kept_part = (keep_grads, keep_db, keep_w, keep_v)
    near = run_chunk((1, 3), side, beta_t, kept_part, (grads, db, *give_w))
    halfway = (*near, lax.ppermute(up, "head", after), lax.ppermute(down, "head", ahead))
    near = call(relay_kernel, "relay", (), lax.optimization_barrier(halfway), [shape(*near[0].shape)] * 2)
    *near, grads, keep_pairs = lax.optimization_barrier((*near, grads, keep_sums[0]))
    sums = (keep_pairs, keep_sums[1], *give_sums)
    (grad_d,) = call(decay_kernel, "decay_sums", (place,), sums, [shape(2 * GROUP, W)])
    (total,) = run_chunk((0,), side, beta_t, kept_part, (grads, db, *give_w))
    total = total + lax.ppermute(near[0], "head", after) + lax.ppermute(near[1], "head", ahead)
    return (total.astype(BF16), grad_d.T)


def solution(mesh):
    placed = (
        P("ctx", None),
        P("ctx", None),
        P(None, "head"),
        P(None, "head"),
        P(None, "head"),
        P(None, "head"),
        P("head", None),
        P("ctx", "head"),
        P(),
    )
    return jax.shard_map(
        per_device,
        mesh=mesh,
        in_specs=placed,
        out_specs=(P("ctx", "head"), P("ctx", "head")),
        check_vma=False,
    )
```
